128 devices in a mesh: gx: 8 (over x, core), gy: 16 (over y, z).
Axes of the slice: x: 4, y: 4, z: 4, core: 2. Of those that a mesh axis runs over, the one named last changes fastest.
Arguments:
- estimate: float32 [16, 1024, 2048], P(None, 'gx', 'gy'), may hold values from 0.5 to 2
- measured: bfloat16 [2, 16, 1024, 2048], P(None, None, 'gx', 'gy'), may hold values from 0.25 to 4
- kernels: float32 [2, 4, 2, 17], replicated, may hold values from 0.2 to 2
- depth_band: int32 [16], replicated, may hold values from 0 to 3
- group_shift: int32 [2, 64], replicated, may hold values from 0 to 127, as said below
- group_length: int32 [2, 64], replicated, may hold values from 1 to 3, 128 in all within a row
Outputs:
- updated: float32 [16, 1024, 2048], P(None, 'gx', 'gy')
The draws below stay inside these ranges and needn't reach their ends.
Inputs may be any that keep to these rules, and one draw needn't show every extreme that they name: `group_shift`: in each row the 64 values are distinct, and 0 and 127 are among them. `group_length`: each row sums to 128, and its largest entry is 3.
All inputs are finite; a program needn't handle non-finite values.
Results may differ from the reference program's by a relative error of at most 0.00035.
Values may be sent and summed in bfloat16 or wider, within the bound.
No kernel may reach another device: no remote copies, remote signals or barrier semaphores. Data moves between devices by JAX's collectives and lax.ppermute only.
A program may use at most 64 MiB of HBM per device.

```python
import math
import jax
import jax.numpy as jnp
import numpy as np
from jax import lax

TY = 128
TX = 128
DZ = 16
VIEWS = 2
BANDS = 4
HW = 8
CAP = 3
KW = 17
NBLK = 128
BR = 1
GROUPS = 64
NY = 1024
NX = 2048
N_GX = 8
N_GY = 16
DEVICES = 128


def draw_group_shift(key, part):
    rows_out = []
    for view_id in range(VIEWS):
        view_key = jax.random.fold_in(key, 11 + view_id)
        first_key, second_key = jax.random.split(view_key)
        middle = jax.random.permutation(first_key, DEVICES - 2)[:GROUPS - 2] + 1
        chosen = jnp.concatenate([jnp.array([0, DEVICES - 1], dtype=jnp.int32), middle.astype(jnp.int32)])
        ordering = jax.random.permutation(second_key, GROUPS)
        rows_out.append(chosen[ordering])
    return jnp.stack(rows_out).astype(jnp.int32)


def place_ends(entries, stream_key, least, top_value):
    longest = entries.shape.index(max(entries.shape))
    spots = []
    for shift in (0, 1):
        where = [jax.random.randint(jax.random.fold_in(stream_key, axis), (), 0, length) for axis, length in enumerate(entries.shape)]
        where[longest] = (where[longest] + shift) % entries.shape[longest]
        spots.append(tuple(where))
    return entries.at[spots[0]].set(least).at[spots[1]].set(top_value)


def block_scale(rng, dims, cuts, smallest, high):
    level, own = 1.0, jax.random.fold_in(rng, 6)
    for dim, blocks in cuts:
        steps = jnp.exp(jax.random.uniform(jax.random.fold_in(own, dim), (blocks,), jnp.float32, smallest / len(cuts), high / len(cuts)))
        level = level * jnp.repeat(steps, dims[dim] // blocks).reshape([-1 if axis == dim else 1 for axis in range(len(dims))])
    return level


def profile(count, total, most, skew):
    loads = [(1 << 20) // math.isqrt(rank ** skew) + 1 for rank in range(2, count + 1)]
    spare, given = total - most - (count - 1), [1] * (count - 1)
    while spare > 0:
        movable = [i for i in range(count - 1) if given[i] < most]
        whole, remaining = sum([loads[i] for i in movable]), spare
        for i in movable:
            addition = min(most - given[i], max(1, remaining * loads[i] // whole), spare)
            given[i] = given[i] + addition
            spare = spare - addition
    return np.array([most] + given)


def ragged(key, count, total, limit, lean):
    if count == 2:
        one = jax.random.randint(key, (), max(1, total - limit), min(limit, total - 1) + 1)
        return jnp.stack([one, total - one])
    lengths = jnp.asarray(profile(count, total, limit, lean), jnp.int32)
    pairs = (count - 1) // 2
    source_of, sink = lengths[1:1 + 2 * pairs:2], lengths[2:2 + 2 * pairs:2]
    slack = jnp.minimum(source_of - 1, limit - sink)
    shifted = jax.random.randint(jax.random.fold_in(key, 1), (pairs,), 0, 1 << 20) % (slack + 1)
    lengths = lengths.at[1:1 + 2 * pairs:2].set(source_of - shifted).at[2:2 + 2 * pairs:2].set(sink + shifted)
    return lengths[jax.random.permutation(jax.random.fold_in(key, 2), count)]


def setup_inputs(seed: int = 0) -> dict:
    key_list = jax.random.split(jax.random.key(seed), 7)
    return {
        "estimate": jnp.clip(0.5 + 1.5 * jax.random.uniform(key_list[0], (DZ, NY, NX), jnp.float32) ** block_scale(key_list[0], (DZ, NY, NX), ((1, 8), (2, 16)), -0.2, 0.2), 0.5, 2.0),
        "measured": jnp.clip(0.25 + 3.75 * jax.random.uniform(key_list[1], (VIEWS, DZ, NY, NX), jnp.float32) ** block_scale(key_list[1], (VIEWS, DZ, NY, NX), ((2, 8), (3, 16)), -0.2, 0.2), 0.25, 4.0).astype(jnp.bfloat16),
        "kernels": jnp.clip(jnp.exp(jax.random.uniform(key_list[2], (VIEWS, BANDS, 2, KW), jnp.float32, math.log(0.2), math.log(2.0))), 0.2, 2.0),
        "depth_band": place_ends(jax.random.randint(key_list[3], (DZ,), 0, BANDS), jax.random.fold_in(key_list[3], 1), 0, BANDS - 1).astype(jnp.int32),
        "group_shift": draw_group_shift(jax.random.fold_in(key_list[6], 71), 0),
        "group_length": jax.vmap(lambda own: ragged(own, GROUPS, NBLK, CAP, 1))(jax.random.split(key_list[5], VIEWS)).reshape((VIEWS, GROUPS)).astype(jnp.int32),
    }


HIGHEST = lax.Precision.HIGHEST


def depth_taps(norm_kernels, depth_band, view_id, axis_id):
    onehot = (depth_band[:, None] == jnp.arange(BANDS, dtype=jnp.int32)[None, :]).astype(jnp.float32)
    return jnp.dot(onehot, norm_kernels[view_id, :, axis_id, :], preferred_element_type=jnp.float32, precision=HIGHEST)


def shift_blur(volume_in, rows_taps, cols_taps, adjoint):
    rows_count = volume_in.shape[1]
    cols_count = volume_in.shape[2]
    padded = jnp.pad(volume_in, ((0, 0), (HW, HW), (HW, HW)))
    along_rows = jnp.zeros((volume_in.shape[0], rows_count, cols_count + 2 * HW), jnp.float32)
    for tap_index in range(2 * HW + 1):
        begin_at = 2 * HW - tap_index if adjoint else tap_index
        along_rows = along_rows + rows_taps[:, tap_index, None, None] * padded[:, begin_at:begin_at + rows_count, :]
    result = jnp.zeros(volume_in.shape, jnp.float32)
    for tap_index in range(2 * HW + 1):
        begin_at = 2 * HW - tap_index if adjoint else tap_index
        result = result + cols_taps[:, tap_index, None, None] * along_rows[:, :, begin_at:begin_at + cols_count]
    return result


def to_blocks(volume_in):
    shaped = volume_in.reshape(DZ, N_GX, NBLK, BR, N_GY, TX)
    shaped = jnp.transpose(shaped, (1, 4, 2, 0, 3, 5))
    return shaped.reshape(N_GX * N_GY, NBLK, DZ, BR * TX)


def from_blocks(blocks):
    shaped = blocks.reshape(N_GX, N_GY, NBLK, DZ, BR, TX)
    shaped = jnp.transpose(shaped, (3, 0, 2, 4, 1, 5))
    return shaped.reshape(DZ, N_GX * TY, N_GY * TX)


def reference(estimate, measured, kernels, depth_band, group_shift, group_length):
    norm_kernels = kernels / jnp.sum(kernels, axis=3, keepdims=True)
    devices = N_GX * N_GY
    ends_at = jnp.cumsum(group_length, axis=1).astype(jnp.int32)
    starts_at = (ends_at - group_length).astype(jnp.int32)
    block_ids = jnp.arange(NBLK, dtype=jnp.int32)
    member = (block_ids[None, :, None] >= starts_at[:, None, :]) & (block_ids[None, :, None] < ends_at[:, None, :])
    shift_of = jnp.sum(jnp.where(member, group_shift[:, None, :], 0), axis=2).astype(jnp.int32)
    total = jnp.zeros(estimate.shape, jnp.float32)
    for view_id in range(VIEWS):
        rows_taps = depth_taps(norm_kernels, depth_band, view_id, 0)
        cols_taps = depth_taps(norm_kernels, depth_band, view_id, 1)
        forward = shift_blur(estimate, rows_taps, cols_taps, False).astype(jnp.bfloat16)
        blocks = to_blocks(measured[view_id])
        if view_id % 2 == 1:
            blocks = jnp.flip(blocks, axis=3)
        source = ((jnp.arange(devices, dtype=jnp.int32)[:, None] - shift_of[view_id][None, :]) % devices).astype(jnp.int32)
        joined_data = from_blocks(blocks[source, block_ids[None, :]])
        ratio_field = (joined_data.astype(jnp.float32) / forward.astype(jnp.float32)).astype(jnp.bfloat16)
        total = total + shift_blur(ratio_field.astype(jnp.float32), rows_taps, cols_taps, True)
    return estimate * (total / VIEWS)
```

```python
import functools

import jax
import jax.numpy as jnp
from jax import lax
from jax.experimental import pallas as pl
from jax.experimental.pallas import tpu as pltpu
from jax.sharding import PartitionSpec as P

HW = 8
CAP = 3
LANES = 256
F32 = jnp.float32
BF16 = jnp.bfloat16

VMEM = pl.BlockSpec(memory_space=pltpu.VMEM)
SMEM = pl.BlockSpec(memory_space=pltpu.SMEM)


def call(kernel, ins, out_shape, scratch=()):
    return pl.pallas_call(
        kernel,
        in_specs=ins,
        out_specs=jax.tree.map(lambda _: VMEM, out_shape),
        out_shape=out_shape,
        scratch_shapes=list(scratch),
        compiler_params=pltpu.CompilerParams(vmem_limit_bytes=48 * 2**20),
    )


def split(x):
    high = x.astype(BF16)
    return high, (x - high.astype(F32)).astype(BF16)


def dot(a, b, dims=((1,), (0,))):
    return lax.dot_general(a, b, (dims, ((), ())), preferred_element_type=F32)


def dot3(a, b, dims=((1,), (0,))):
    return dot(a[0], b[0], dims) + (dot(a[1], b[0], dims) + dot(a[0], b[1], dims))


NT = ((1,), (1,))


def pack_kernel(devices, me_ref, shift_ref, length_ref, measured_ref, out_ref, rows_ref):
    views, depth, tile_rows, tile_cols = measured_ref.shape
    groups = shift_ref.shape[1]
    rows_ref[:, tile_rows:] = jnp.zeros((views, rows_ref.shape[1] - tile_rows) + rows_ref.shape[2:], BF16)
    lane = lax.broadcasted_iota(jnp.int32, (tile_cols, tile_cols), 1)
    sub = lax.broadcasted_iota(jnp.int32, (tile_cols, tile_cols), 0)
    turn = (lane + sub == tile_cols - 1).astype(BF16)
    me = me_ref[0]
    for view in range(views):
        for r0 in range(0, tile_rows, 16):
            x = measured_ref[view, :, r0 : r0 + 16, :]
            if view % 2 == 1:
                x = dot(x.reshape(depth * 16, tile_cols), turn).reshape(depth, 16, tile_cols)
            x = jnp.transpose(x.astype(F32), (1, 0, 2))
            rows_ref[view, r0 : r0 + 16] = x.astype(BF16)

        def group(g, start, view=view):
            base = lax.rem(me + shift_ref[view, g], devices) * (views * CAP) + view * CAP
            for k in range(CAP):
                out_ref[base + k] = rows_ref[view, start + k]
            return start + length_ref[view, g]

        lax.fori_loop(0, groups, group, 0, unroll=4)


def unpack_kernel(devices, me_ref, shift_ref, length_ref, arrived_ref, recip_ref, out_ref, rows_ref):
    views, depth, tile_rows, tile_cols = out_ref.shape
    groups = shift_ref.shape[1]
    me = me_ref[0]
    for view in range(views):

        def group(g, start, view=view):
            source = lax.rem(me - shift_ref[view, g] + devices, devices)
            base = source * (views * CAP) + view * CAP
            for k in range(CAP):
                rows_ref[view, start + k] = arrived_ref[base + k].astype(F32)
            return start + length_ref[view, g]

        lax.fori_loop(0, groups, group, 0, unroll=4)
        for r0 in range(0, tile_rows, 16):
            x = jnp.transpose(rows_ref[view, r0 : r0 + 16], (1, 0, 2))
            out_ref[view, :, r0 : r0 + 16, :] = (x * recip_ref[view, :, r0 : r0 + 16, :]).astype(BF16)


def band(taps, size):
    wide = jnp.broadcast_to(taps, (size, LANES))
    inner = pltpu.roll(wide, LANES - HW, 1, stride=1, stride_axis=0)
    before = pltpu.roll(wide, size + HW, 1, stride=1, stride_axis=0)
    lane = lax.broadcasted_iota(jnp.int32, (size, LANES), 1)
    out = jnp.where(lane < size + HW, inner, jnp.where(lane < size + 2 * HW, before, 0.0))
    return out[:, : size + 2 * HW]


def forward_kernel(band_ref, taps_ref, padded_ref, recip_ref, adjoint_ref, fwd_ref):
    views, depth, tile_rows, tile_cols = recip_ref.shape
    bands = taps_ref.shape[2]
    for view in range(views):
        for b in range(bands):
            for axis in range(2):
                for way, ref in ((0, fwd_ref), (1, adjoint_ref)):
                    high, low = split(band(taps_ref[way, view, b, axis : axis + 1, :], tile_rows))
                    ref[view, b, axis, 0] = high
                    ref[view, b, axis, 1] = low

    def plane(z, carry):
        b = band_ref[z]
        cells = split(padded_ref[z])
        for view in range(views):
            rows = (fwd_ref[view, b, 0, 0], fwd_ref[view, b, 0, 1])
            cols = (fwd_ref[view, b, 1, 0], fwd_ref[view, b, 1, 1])
            blurred = dot3(split(dot3(rows, cells)), cols, NT)
            recip_ref[view, z] = 1.0 / blurred.astype(BF16).astype(F32)
        return carry

    lax.fori_loop(0, depth, plane, 0)


def adjoint_kernel(band_ref, adjoint_ref, ratio_ref, estimate_ref, out_ref):
    views = ratio_ref.shape[0]
    depth = ratio_ref.shape[1]

    def plane(z, carry):
        b = band_ref[z]
        total = None
        for view in range(views):
            cells = ratio_ref[view, z]
            rows = (adjoint_ref[view, b, 0, 0], adjoint_ref[view, b, 0, 1])
            blurred = dot(cells, adjoint_ref[view, b, 1, 0], NT) + dot(cells, adjoint_ref[view, b, 1, 1], NT)
            part = dot3(rows, split(blurred))
            total = part if total is None else total + part
        out_ref[z] = estimate_ref[z] * (total * (1.0 / views))
        return carry

    lax.fori_loop(0, depth, plane, 0)


def padded(cells, sides):
    for axis, dim in sides:
        count = lax.axis_size(axis)
        ends = count - 1
        head = lax.slice_in_dim(cells, 0, HW, axis=dim)
        tail = lax.slice_in_dim(cells, cells.shape[dim] - HW, cells.shape[dim], axis=dim)
        before = lax.ppermute(tail, axis, [(i, i + 1) for i in range(ends)])
        after = lax.ppermute(head, axis, [(i + 1, i) for i in range(ends)])
        cells = jnp.concatenate([cells, after, before], axis=dim)
    return cells


def body(estimate, measured, kernels, depth_band, group_shift, group_length):
    devices = lax.axis_size("gx") * lax.axis_size("gy")
    me = (lax.axis_index("gx") * lax.axis_size("gy") + lax.axis_index("gy")).reshape(1).astype(jnp.int32)
    views, depth, tile_rows, tile_cols = measured.shape
    spare = tile_rows + 8
    outgoing = call(
        functools.partial(pack_kernel, devices),
        [SMEM, SMEM, SMEM, VMEM],
        jax.ShapeDtypeStruct((devices * views * CAP, depth, tile_cols), BF16),
        [pltpu.VMEM((views, spare, depth, tile_cols), BF16)],
    )(me, group_shift, group_length, measured)
    arrived = lax.all_to_all(outgoing, ("gx", "gy"), split_axis=0, concat_axis=0, tiled=True)

    norm = kernels / jnp.sum(kernels, axis=3, keepdims=True)
    tap_rows = jnp.stack([norm, norm[..., ::-1]])
    tap_rows = jnp.pad(tap_rows, ((0, 0),) * 4 + ((0, LANES - kernels.shape[3]),))
    cells = padded(estimate, (("gx", 1), ("gy", 2)))
    matrices = (views, kernels.shape[1], 2, 2, tile_rows, tile_rows + 2 * HW)
    recip, adjoint = call(
        forward_kernel,
        [SMEM, VMEM, VMEM],
        (jax.ShapeDtypeStruct(measured.shape, F32), jax.ShapeDtypeStruct(matrices, BF16)),
        [pltpu.VMEM(matrices, BF16)],
    )(depth_band, tap_rows, cells)

    ratio = call(
        functools.partial(unpack_kernel, devices),
        [SMEM, SMEM, SMEM, VMEM, VMEM],
        jax.ShapeDtypeStruct(measured.shape, BF16),
        [pltpu.VMEM((views, spare, depth, tile_cols), F32)],
    )(me, group_shift, group_length, arrived, recip)
    ratio = padded(ratio, (("gx", 2), ("gy", 3)))
    return call(
        adjoint_kernel,
        [SMEM, VMEM, VMEM, VMEM],
        jax.ShapeDtypeStruct(estimate.shape, F32),
    )(depth_band, adjoint, ratio, estimate)


def solution(mesh):
    return jax.shard_map(
        body,
        mesh=mesh,
        in_specs=(P(None, "gx", "gy"), P(None, None, "gx", "gy"), P(), P(), P(), P()),
        out_specs=P(None, "gx", "gy"),
        check_vma=False,
    )
```

```python
import functools

import jax
import jax.numpy as jnp
from jax import lax
from jax.experimental import pallas as pl
from jax.experimental.pallas import tpu as pltpu
from jax.sharding import PartitionSpec as P

HW = 8
CAP = 3
LANES = 256
F32 = jnp.float32
BF16 = jnp.bfloat16

VMEM = pl.BlockSpec(memory_space=pltpu.VMEM)
SMEM = pl.BlockSpec(memory_space=pltpu.SMEM)
NN = ((1,), (0,))
NT = ((1,), (1,))


def call(kernel, ins, out_shape, scratch=()):
    return pl.pallas_call(
        kernel,
        in_specs=ins,
        out_specs=jax.tree.map(lambda _: VMEM, out_shape),
        out_shape=out_shape,
        scratch_shapes=list(scratch),
        compiler_params=pltpu.CompilerParams(vmem_limit_bytes=16 * 2**20),
    )


def dot(a, b, dims=NN):
    return lax.dot_general(a, b, (dims, ((), ())), preferred_element_type=F32)


def split(x):
    high = x.astype(BF16)
    return high, (x - high.astype(F32)).astype(BF16)


def stacked(x, axis):
    return jnp.concatenate(split(x), axis=axis)


def halves(x):
    n = x.shape[0] // 2
    return x[:n] + x[n:]


def quarters(x):
    n, m = x.shape[0] // 2, x.shape[1] // 2
    return x[:n, :m] + (x[n:, :m] + x[:n, m:])


def joined(after, before):
    return jnp.concatenate([after.astype(F32), before.astype(F32)], axis=0).astype(BF16)


def edge_picker(cols):
    lane = lax.broadcasted_iota(jnp.int32, (2 * HW, cols), 1)
    sub = lax.broadcasted_iota(jnp.int32, (2 * HW, cols), 0)
    return (lane == jnp.where(sub < HW, sub, sub + cols - 2 * HW)).astype(BF16)


def pack_kernel(devices, me_ref, shift_ref, length_ref, measured_ref, estimate_ref, out_ref, cols_ref, rows_ref):
    views, depth, tile_rows, tile_cols = measured_ref.shape
    groups = shift_ref.shape[1]
    rows_ref[:, tile_rows:] = jnp.zeros((views, rows_ref.shape[1] - tile_rows) + rows_ref.shape[2:], BF16)
    lane = lax.broadcasted_iota(jnp.int32, (tile_cols, tile_cols), 1)
    sub = lax.broadcasted_iota(jnp.int32, (tile_cols, tile_cols), 0)
    turn = (lane + sub == tile_cols - 1).astype(BF16)
    me = me_ref[0]
    for view in range(views):
        for r0 in range(0, tile_rows, 16):
            x = measured_ref[view, :, r0 : r0 + 16, :]
            if view % 2 == 1:
                x = dot(x.reshape(depth * 16, tile_cols), turn).reshape(depth, 16, tile_cols)
            x = jnp.transpose(x.astype(F32), (1, 0, 2))
            rows_ref[view, r0 : r0 + 16] = x.astype(BF16)

        def group(g, start, view=view):
            base = lax.rem(me + shift_ref[view, g], devices) * (views * CAP) + view * CAP
            for k in range(CAP):
                out_ref[base + k] = rows_ref[view, start + k]
            return start + length_ref[view, g]

        lax.fori_loop(0, groups, group, 0, unroll=4)
    pick = edge_picker(tile_cols)
    for z in range(depth):
        cols_ref[z] = dot(pick, estimate_ref[z].astype(BF16), NT).astype(BF16)


def slab_kernel(cols_ref, after_ref, before_ref, head_ref, tail_ref):
    tile_rows = cols_ref.shape[-1]
    pick = edge_picker(after_ref.shape[-1])

    def plane(i, carry):
        corner = dot(pick, joined(after_ref[i], before_ref[i]), NT).astype(BF16)
        head_ref[i, :, :tile_rows] = cols_ref[i, :HW]
        tail_ref[i, :, :tile_rows] = cols_ref[i, HW:]
        head_ref[i, :, tile_rows:] = corner[:HW]
        tail_ref[i, :, tile_rows:] = corner[HW:]
        return carry

    lax.fori_loop(0, cols_ref.shape[0], plane, 0, unroll=8)


def edges_kernel(devices, me_ref, shift_ref, length_ref, arrived_ref, recip_ref, top_ref, bottom_ref, rows_ref):
    views, depth, tile_rows, tile_cols = recip_ref.shape
    groups = shift_ref.shape[1]
    me = me_ref[0]
    low = tile_rows - CAP * HW
    for view in range(views):
        ending = tile_rows - low
        for g in range(groups - HW, groups):
            ending = ending - length_ref[view, g]
        for side, (first, start) in enumerate(((0, 0), (groups - HW, ending))):
            for g in range(first, first + HW):
                source = lax.rem(me - shift_ref[view, g] + devices, devices)
                base = source * (views * CAP) + view * CAP
                for k in range(CAP):
                    rows_ref[view, side, start + k] = arrived_ref[base + k].astype(F32)
                start = start + length_ref[view, g]
        x = jnp.transpose(rows_ref[view, 0, :HW], (1, 0, 2))
        top_ref[view] = (x * recip_ref[view, :, :HW, :]).astype(BF16)
        x = jnp.transpose(rows_ref[view, 1, (CAP - 1) * HW : CAP * HW], (1, 0, 2))
        bottom_ref[view] = (x * recip_ref[view, :, tile_rows - HW :, :]).astype(BF16)


def unpack_kernel(devices, me_ref, shift_ref, length_ref, arrived_ref, recip_ref, out_ref, cols_ref, rows_ref):
    views, depth, tile_rows, tile_cols = out_ref.shape
    groups = shift_ref.shape[1]
    me = me_ref[0]
    pick = edge_picker(tile_cols)
    for view in range(views):

        def group(g, start, view=view):
            source = lax.rem(me - shift_ref[view, g] + devices, devices)
            base = source * (views * CAP) + view * CAP
            for k in range(CAP):
                rows_ref[view, start + k] = arrived_ref[base + k].astype(F32)
            return start + length_ref[view, g]

        lax.fori_loop(0, groups, group, 0, unroll=4)
        for r0 in range(0, tile_rows, 16):
            x = jnp.transpose(rows_ref[view, r0 : r0 + 16], (1, 0, 2))
            out_ref[view, :, r0 : r0 + 16, :] = (x * recip_ref[view, :, r0 : r0 + 16, :]).astype(BF16)
        for z in range(depth):
            cols_ref[view, z] = dot(pick, out_ref[view, z], NT).astype(BF16)


def band(taps, size):
    wide = jnp.broadcast_to(taps, (size, LANES))
    inner = pltpu.roll(wide, LANES - HW, 1, stride=1, stride_axis=0)
    before = pltpu.roll(wide, size + HW, 1, stride=1, stride_axis=0)
    lane = lax.broadcasted_iota(jnp.int32, (size, LANES), 1)
    return jnp.where(lane < size + HW, inner, jnp.where(lane < size + 2 * HW, before, 0.0))


def blur_far(rows, far, across):
    return quarters(dot(stacked(halves(dot(rows, far, NT)), 0), across))


def forward_kernel(
    band_ref, taps_ref, cells_ref, after_ref, before_ref, right_ref, left_ref,
    recip_ref, rows_ref, cols_ref, far_ref, fwd_rows, fwd_cols, fwd_far,
):
    views, depth, tile_rows, tile_cols = recip_ref.shape
    bands = taps_ref.shape[2]
    for way, refs in ((0, (fwd_rows, fwd_cols, fwd_far)), (1, (rows_ref, cols_ref, far_ref))):
        for view in range(views):
            for b in range(bands):
                along = band(taps_ref[way, view, b, 0:1, :], tile_rows)
                refs[0][view, b] = stacked(along[:, : tile_rows + 2 * HW], 0)
                across = band(taps_ref[way, view, b, 1:2, :], tile_cols)
                refs[1][view, b] = stacked(across[:, :tile_cols].T, 1)
                refs[2][view, b] = stacked(across[:, tile_cols:].T[: 2 * HW], 1)

    def plane(z, carry):
        b = band_ref[z]
        cells = stacked(cells_ref[z], 1)
        ends = joined(after_ref[z], before_ref[z])
        far = joined(right_ref[z], left_ref[z])
        for view in range(views):
            rows = fwd_rows[view, b]
            blurred = quarters(dot(rows[:, :tile_rows], cells)) + halves(dot(rows[:, tile_rows:], ends))
            blurred = quarters(dot(stacked(blurred, 0), fwd_cols[view, b])) + blur_far(rows, far, fwd_far[view, b])
            recip_ref[view, z] = 1.0 / blurred.astype(BF16).astype(F32)
        return carry

    lax.fori_loop(0, depth, plane, 0)


def near_kernel(band_ref, rows_ref, cols_ref, ratio_ref, after_ref, before_ref, out_ref):
    views, depth = ratio_ref.shape[:2]

    def plane(z, carry):
        b = band_ref[z]
        total = None
        for view in range(views):
            cells = jnp.concatenate([ratio_ref[view, z], joined(after_ref[view, z], before_ref[view, z])], axis=0)
            blurred = dot(cells, cols_ref[view, b])
            half = blurred.shape[1] // 2
            blurred = blurred[:, :half] + blurred[:, half:]
            part = quarters(dot(rows_ref[view, b], stacked(blurred, 1)))
            total = part if total is None else total + part
        out_ref[z] = total
        return carry

    lax.fori_loop(0, depth, plane, 0, unroll=2)


def far_kernel(band_ref, rows_ref, far_ref, near_ref, right_ref, left_ref, estimate_ref, out_ref):
    views, depth = right_ref.shape[:2]

    def plane(z, carry):
        b = band_ref[z]
        total = near_ref[z]
        for view in range(views):
            total = total + blur_far(rows_ref[view, b], joined(right_ref[view, z], left_ref[view, z]), far_ref[view, b])
        out_ref[z] = estimate_ref[z] * (total * (1.0 / views))
        return carry

    lax.fori_loop(0, depth, plane, 0, unroll=2)


def swap(head, tail, axis):
    ends = lax.axis_size(axis) - 1
    after = lax.ppermute(head, axis, [(i + 1, i) for i in range(ends)])
    before = lax.ppermute(tail, axis, [(i, i + 1) for i in range(ends)])
    return after, before


def slabs(cols, after, before):
    lead = cols.shape[:-2]
    shape = (cols.size // (cols.shape[-1] * cols.shape[-2]), HW, cols.shape[-1] + 2 * HW)
    merge = lambda x: x.reshape((shape[0],) + x.shape[-2:])
    out = jax.ShapeDtypeStruct(shape, BF16)
    head, tail = call(slab_kernel, [VMEM] * 3, (out, out))(merge(cols), merge(after), merge(before))
    return head.reshape(lead + shape[1:]), tail.reshape(lead + shape[1:])


def body(estimate, measured, kernels, depth_band, group_shift, group_length):
    devices = lax.axis_size("gx") * lax.axis_size("gy")
    me = (lax.axis_index("gx") * lax.axis_size("gy") + lax.axis_index("gy")).reshape(1).astype(jnp.int32)
    views, depth, tile_rows, tile_cols = measured.shape
    bands = kernels.shape[1]
    spare = tile_rows + 8
    whole = jax.ShapeDtypeStruct(measured.shape, BF16)
    edge_cols = jax.ShapeDtypeStruct((views, depth, 2 * HW, tile_rows), BF16)
    edge_rows = jax.ShapeDtypeStruct((views, depth, HW, tile_cols), BF16)

    after, before = swap(
        estimate[:, :HW].astype(BF16), estimate[:, tile_rows - HW :].astype(BF16), "gx"
    )
    outgoing, cols = call(
        functools.partial(pack_kernel, devices),
        [SMEM, SMEM, SMEM, VMEM, VMEM],
        (
            jax.ShapeDtypeStruct((devices * views * CAP, depth, tile_cols), BF16),
            jax.ShapeDtypeStruct(edge_cols.shape[1:], BF16),
        ),
        [pltpu.VMEM((views, spare, depth, tile_cols), BF16)],
    )(me, group_shift, group_length, measured, estimate)
    right, left = swap(*slabs(cols, after, before), "gy")
    outgoing, right, left = lax.optimization_barrier((outgoing, right, left))
    arrived = lax.all_to_all(outgoing, ("gx", "gy"), split_axis=0, concat_axis=0, tiled=True)

    norm = kernels / jnp.sum(kernels, axis=3, keepdims=True)
    tap_rows = jnp.stack([norm, norm[..., ::-1]])
    tap_rows = jnp.pad(tap_rows, ((0, 0),) * 4 + ((0, LANES - kernels.shape[3]),))
    matrices = [
        (views, bands, 2 * tile_rows, tile_rows + 2 * HW),
        (views, bands, tile_cols, 2 * tile_cols),
        (views, bands, 2 * HW, 2 * tile_cols),
    ]
    recip, rows_mat, cols_mat, far_mat = call(
        forward_kernel,
        [SMEM] + [VMEM] * 6,
        (jax.ShapeDtypeStruct(measured.shape, F32), *(jax.ShapeDtypeStruct(m, BF16) for m in matrices)),
        [pltpu.VMEM(m, BF16) for m in matrices],
    )(depth_band, tap_rows, estimate, after, before, right, left)

    top, bottom = call(
        functools.partial(edges_kernel, devices),
        [SMEM, SMEM, SMEM, VMEM, VMEM],
        (edge_rows, edge_rows),
        [pltpu.VMEM((views, 2, CAP * HW + 8, depth, tile_cols), F32)],
    )(me, group_shift, group_length, arrived, recip)
    after, before = swap(top, bottom, "gx")
    ratio, cols = call(
        functools.partial(unpack_kernel, devices),
        [SMEM, SMEM, SMEM, VMEM, VMEM],
        (whole, edge_cols),
        [pltpu.VMEM((views, spare, depth, tile_cols), F32)],
    )(me, group_shift, group_length, arrived, recip)
    right, left = swap(*slabs(cols, after, before), "gy")
    near = call(
        near_kernel,
        [SMEM] + [VMEM] * 5,
        jax.ShapeDtypeStruct(estimate.shape, F32),
    )(depth_band, rows_mat, cols_mat, ratio, after, before)
    return call(
        far_kernel,
        [SMEM] + [VMEM] * 6,
        jax.ShapeDtypeStruct(estimate.shape, F32),
    )(depth_band, rows_mat, far_mat, near, right, left, estimate)


def solution(mesh):
    return jax.shard_map(
        body,
        mesh=mesh,
        in_specs=(P(None, "gx", "gy"), P(None, None, "gx", "gy"), P(), P(), P(), P()),
        out_specs=P(None, "gx", "gy"),
        check_vma=False,
    )
```

```python
import functools

import jax
import jax.numpy as jnp
from jax import lax
from jax.experimental import pallas as pl
from jax.experimental.pallas import tpu as pltpu
from jax.sharding import PartitionSpec as P

HW = 8
CAP = 3
LANES = 256
F32 = jnp.float32
BF16 = jnp.bfloat16

VMEM = pl.BlockSpec(memory_space=pltpu.VMEM)
SMEM = pl.BlockSpec(memory_space=pltpu.SMEM)
HBM = pl.BlockSpec(memory_space=pltpu.HBM)
NN = ((1,), (0,))
NT = ((1,), (1,))


def call(kernel, ins, out_shape, scratch=()):
    return pl.pallas_call(
        kernel,
        in_specs=ins,
        out_specs=jax.tree.map(lambda _: VMEM, out_shape),
        out_shape=out_shape,
        scratch_shapes=list(scratch),
        compiler_params=pltpu.CompilerParams(vmem_limit_bytes=16 * 2**20),
    )


def dot(a, b, dims=NN):
    return lax.dot_general(a, b, (dims, ((), ())), preferred_element_type=F32)


def split(x):
    high = x.astype(BF16)
    return high, (x - high.astype(F32)).astype(BF16)


def stacked(x, axis):
    return jnp.concatenate(split(x), axis=axis)


def halves(x):
    n = x.shape[0] // 2
    return x[:n] + x[n:]


def quarters(x):
    n, m = x.shape[0] // 2, x.shape[1] // 2
    return x[:n, :m] + (x[n:, :m] + x[:n, m:])


def halo(odd_ref, first, second):
    first, second = first.astype(F32), second.astype(F32)
    odd = odd_ref[0] == 1
    after = jnp.where(odd, second, first)
    before = jnp.where(odd, first, second)
    return jnp.concatenate([after, before], axis=0).astype(BF16)


def edge_picker(cols):
    lane = lax.broadcasted_iota(jnp.int32, (2 * HW, cols), 1)
    sub = lax.broadcasted_iota(jnp.int32, (2 * HW, cols), 0)
    return (lane == jnp.where(sub < HW, sub, sub + cols - 2 * HW)).astype(BF16)


def pack_kernel(
    devices, me_ref, shift_hbm, length_hbm, measured_hbm, _, out_ref, rows_ref, measured_ref, shift_ref, length_ref, sems
):
    views, depth, tile_rows, tile_cols = measured_ref.shape
    groups = shift_ref.shape[1]
    loads = [pltpu.make_async_copy(measured_hbm.at[v], measured_ref.at[v], sems.at[v]) for v in range(views)]
    tables = [
        pltpu.make_async_copy(shift_hbm, shift_ref, sems.at[views]),
        pltpu.make_async_copy(length_hbm, length_ref, sems.at[views + 1]),
    ]
    for copy in loads + tables:
        copy.start()
    rows_ref[:, tile_rows:] = jnp.zeros((views, rows_ref.shape[1] - tile_rows) + rows_ref.shape[2:], BF16)
    lane = lax.broadcasted_iota(jnp.int32, (tile_cols, tile_cols), 1)
    sub = lax.broadcasted_iota(jnp.int32, (tile_cols, tile_cols), 0)
    turn = (lane + sub == tile_cols - 1).astype(BF16)
    me = me_ref[0]
    for view in range(views):
        loads[view].wait()
        for r0 in range(0, tile_rows, 16):
            x = measured_ref[view, :, r0 : r0 + 16, :]
            if view % 2 == 1:
                x = dot(x.reshape(depth * 16, tile_cols), turn).reshape(depth, 16, tile_cols)
            x = jnp.transpose(x.astype(F32), (1, 0, 2))
            rows_ref[view, r0 : r0 + 16] = x.astype(BF16)
        if view == 0:
            for copy in tables:
                copy.wait()

        def group(g, start, view=view):
            base = lax.rem(me + shift_ref[view, g], devices) * (views * CAP) + view * CAP
            for k in range(CAP):
                out_ref[base + k] = rows_ref[view, start + k]
            return start + length_ref[view, g]

        lax.fori_loop(0, groups, group, 0, unroll=4)


def cols_kernel(cells_ref, out_ref):
    pick = edge_picker(cells_ref.shape[-1])
    for z in range(cells_ref.shape[0]):
        out_ref[z] = dot(pick, cells_ref[z].astype(BF16), NT).astype(BF16)


def slab_kernel(odd_x_ref, odd_y_ref, cols_ref, even_ref, odd_ref, first_ref, second_ref):
    tile_rows = cols_ref.shape[-1]
    pick = edge_picker(even_ref.shape[-1])
    odd = odd_y_ref[0] == 1

    def plane(i, carry):
        ends = halo(odd_x_ref, even_ref[i], odd_ref[i])
        corner = dot(pick, ends, NT)
        cols = cols_ref[i].astype(F32)
        for ref, flag in ((first_ref, odd), (second_ref, jnp.logical_not(odd))):
            ref[i, :, :tile_rows] = jnp.where(flag, cols[:HW], cols[HW:]).astype(BF16)
            ref[i, :, tile_rows:] = jnp.where(flag, corner[:HW], corner[HW:]).astype(BF16)
        return carry

    lax.fori_loop(0, cols_ref.shape[0], plane, 0, unroll=8)


def edges_kernel(
    devices, tile_rows, me_ref, odd_ref, shift_ref, length_ref, arrived_ref, recip_ref, first_ref, second_ref, rows_ref
):
    views = recip_ref.shape[0]
    odd = odd_ref[0] == 1
    groups = shift_ref.shape[1]
    me = me_ref[0]
    low = tile_rows - CAP * HW
    for view in range(views):
        ending = tile_rows - low
        for g in range(groups - HW, groups):
            ending = ending - length_ref[view, g]
        for side, (first, start) in enumerate(((0, 0), (groups - HW, ending))):
            for g in range(first, first + HW):
                source = lax.rem(me - shift_ref[view, g] + devices, devices)
                base = source * (views * CAP) + view * CAP
                for k in range(CAP):
                    rows_ref[view, side, start + k] = arrived_ref[base + k].astype(F32)
                start = start + length_ref[view, g]
        head = jnp.transpose(rows_ref[view, 0, :HW], (1, 0, 2)) * recip_ref[view, :, :HW]
        tail = rows_ref[view, 1, (CAP - 1) * HW : CAP * HW]
        tail = jnp.transpose(tail, (1, 0, 2)) * recip_ref[view, :, HW:]
        first_ref[view] = jnp.where(odd, head, tail).astype(BF16)
        second_ref[view] = jnp.where(odd, tail, head).astype(BF16)


def unpack_kernel(devices, me_ref, shift_ref, length_ref, arrived_ref, recip_ref, out_ref, cols_ref, rows_ref):
    views, depth, tile_rows, tile_cols = out_ref.shape
    groups = shift_ref.shape[1]
    me = me_ref[0]
    pick = edge_picker(tile_cols)
    for view in range(views):

        def group(g, start, view=view):
            source = lax.rem(me - shift_ref[view, g] + devices, devices)
            base = source * (views * CAP) + view * CAP
            for k in range(CAP):
                rows_ref[view, start + k] = arrived_ref[base + k].astype(F32)
            return start + length_ref[view, g]

        lax.fori_loop(0, groups, group, 0, unroll=4)
        for r0 in range(0, tile_rows, 16):
            x = jnp.transpose(rows_ref[view, r0 : r0 + 16], (1, 0, 2))
            out_ref[view, :, r0 : r0 + 16, :] = (x * recip_ref[view, :, r0 : r0 + 16, :]).astype(BF16)
        for z in range(depth):
            cols_ref[view, z] = dot(pick, out_ref[view, z], NT).astype(BF16)


def band(taps, size):
    wide = jnp.broadcast_to(taps, (size, LANES))
    inner = pltpu.roll(wide, LANES - HW, 1, stride=1, stride_axis=0)
    before = pltpu.roll(wide, size + HW, 1, stride=1, stride_axis=0)
    lane = lax.broadcasted_iota(jnp.int32, (size, LANES), 1)
    return jnp.where(lane < size + HW, inner, jnp.where(lane < size + 2 * HW, before, 0.0))


def blur_far(rows, far, across):
    return quarters(dot(stacked(halves(dot(rows, far, NT)), 0), across))


def forward_kernel(
    band_ref, odd_x_ref, odd_y_ref, taps_ref, cells_ref, even_x_ref, other_x_ref, even_y_ref, other_y_ref,
    recip_ref, edge_ref, rows_ref, ends_ref, cols_ref, turned_ref, far_ref, fwd_rows, fwd_cols, fwd_far,
):
    views, depth, tile_rows, tile_cols = recip_ref.shape
    bands = taps_ref.shape[2]
    for view in range(views):
        for b in range(bands):
            along = band(taps_ref[0, view, b, 0:1, :], tile_rows)
            fwd_rows[view, b] = stacked(along[:, : tile_rows + 2 * HW], 0)
            across = band(taps_ref[0, view, b, 1:2, :], tile_cols)
            fwd_cols[view, b] = stacked(across[:, :tile_cols].T, 1)
            fwd_far[view, b] = stacked(across[:, tile_cols:].T[: 2 * HW], 1)
    for b in range(bands):
        ends = jnp.zeros((tile_rows, LANES - tile_rows), F32)
        for view in range(views):
            along = band(taps_ref[1, view, b, 0:1, :], tile_rows)
            rows_ref[b, :, view * tile_rows : (view + 1) * tile_rows] = stacked(along[:, :tile_rows], 0)
            beyond = along[:, tile_rows:]
            ends = ends + (pltpu.roll(beyond, 2 * HW * view, 1) if view else beyond)
            turned_ref[view, b, :tile_rows] = stacked(along[:, :tile_rows].T, 1)
            turned_ref[view, b, tile_rows:] = stacked(beyond.T[: 2 * HW], 1)
            across = band(taps_ref[1, view, b, 1:2, :], tile_cols)
            cols_ref[view, b] = stacked(across[:, :tile_cols].T, 1)
            high, low = split(across[:, tile_cols:].T[: 2 * HW])
            far_ref[b, view] = jnp.concatenate([high, high, low], axis=0)
        ends = jnp.concatenate([ends[:HW], ends[tile_rows - HW :]], axis=0)
        ends_ref[b] = stacked(ends[:, : 2 * HW * views], 0)

    def plane(z, carry):
        b = band_ref[z]
        cells = stacked(cells_ref[z], 1)
        ends = halo(odd_x_ref, even_x_ref[z], other_x_ref[z])
        far = halo(odd_y_ref, even_y_ref[z], other_y_ref[z])
        for view in range(views):
            rows = fwd_rows[view, b]
            blurred = quarters(dot(rows[:, :tile_rows], cells)) + halves(dot(rows[:, tile_rows:], ends))
            blurred = quarters(dot(stacked(blurred, 0), fwd_cols[view, b])) + blur_far(rows, far, fwd_far[view, b])
            recip = 1.0 / blurred.astype(BF16).astype(F32)
            recip_ref[view, z] = recip
            edge_ref[view, z, :HW] = recip[:HW]
            edge_ref[view, z, HW:] = recip[tile_rows - HW :]
        return carry

    lax.fori_loop(0, depth, plane, 0, unroll=2)


def near_kernel(band_ref, odd_ref, rows_ref, ends_ref, cols_ref, ratio_ref, even_ref, other_ref, out_ref):
    views, depth, tile_rows, tile_cols = ratio_ref.shape

    def plane(z, carry):
        b = band_ref[z]
        inner, outer = [], []
        for view in range(views):
            ends = halo(odd_ref, even_ref[view, z], other_ref[view, z])
            blurred = dot(jnp.concatenate([ratio_ref[view, z], ends], axis=0), cols_ref[view, b])
            blurred = stacked(blurred[:, :tile_cols] + blurred[:, tile_cols:], 1)
            inner.append(blurred[:tile_rows])
            outer.append(blurred[tile_rows:])
        out_ref[z] = quarters(dot(rows_ref[b], jnp.concatenate(inner, axis=0)))
        ends = quarters(dot(ends_ref[b], jnp.concatenate(outer, axis=0)))
        out_ref[z, :HW] += ends[:HW]
        out_ref[z, tile_rows - HW :] += ends[HW:]
        return carry

    lax.fori_loop(0, depth, plane, 0, unroll=4)


def far_kernel(band_ref, odd_ref, turned_ref, far_ref, near_ref, even_ref, other_ref, estimate_ref, out_ref, slab_ref, along_ref):
    views, bands = turned_ref.shape[:2]
    depth, tile_rows, tile_cols = near_ref.shape
    for view in range(views):
        for z in range(depth):
            slab_ref[z * 2 * HW : (z + 1) * 2 * HW] = halo(odd_ref, even_ref[view, z], other_ref[view, z])
        for b in range(bands):
            along = dot(slab_ref[...], turned_ref[view, b])
            along_ref[view, b] = along[:, :tile_rows] + along[:, tile_rows:]

    def plane(z, carry):
        b = band_ref[z]
        parts = []
        for view in range(views):
            high, low = split(along_ref[view, b, pl.ds(pl.multiple_of(z * 2 * HW, 2 * HW), 2 * HW), :])
            parts += [high, low, high]
        across = far_ref[b].reshape(views * 6 * HW, tile_cols)
        total = near_ref[z] + dot(jnp.concatenate(parts, axis=0), across, ((0,), (0,)))
        out_ref[z] = estimate_ref[z] * (total * (1.0 / views))
        return carry

    lax.fori_loop(0, depth, plane, 0, unroll=4)


def swap(first, second, axis):
    count = lax.axis_size(axis)
    pairs = lambda begin: [p for i in range(begin, count - 1, 2) for p in ((i, i + 1), (i + 1, i))]
    return lax.ppermute(first, axis, pairs(0)), lax.ppermute(second, axis, pairs(1))


def slabs(odd_x, odd_y, cols, first, second):
    lead = cols.shape[:-2]
    shape = (cols.size // (cols.shape[-1] * cols.shape[-2]), HW, cols.shape[-1] + 2 * HW)
    merge = lambda x: x.reshape((shape[0],) + x.shape[-2:])
    out = jax.ShapeDtypeStruct(shape, BF16)
    pair = call(slab_kernel, [SMEM] * 2 + [VMEM] * 3, (out, out))(odd_x, odd_y, merge(cols), merge(first), merge(second))
    return [x.reshape(lead + shape[1:]) for x in pair]


def body(estimate, measured, kernels, depth_band, group_shift, group_length):
    devices = lax.axis_size("gx") * lax.axis_size("gy")
    gx, gy = lax.axis_index("gx").astype(jnp.int32), lax.axis_index("gy").astype(jnp.int32)
    me = (gx * lax.axis_size("gy") + gy).reshape(1)
    odd_x, odd_y = (gx % 2).reshape(1), (gy % 2).reshape(1)
    views, depth, tile_rows, tile_cols = measured.shape
    bands = kernels.shape[1]
    spare = tile_rows + 8
    like = jax.ShapeDtypeStruct
    whole = like(measured.shape, BF16)
    edge_cols = like((views, depth, 2 * HW, tile_rows), BF16)
    edge_rows = like((views, depth, HW, tile_cols), BF16)

    head, tail = estimate[:, :HW], estimate[:, tile_rows - HW :]
    even = gx % 2 == 0
    ex, ox = swap(jnp.where(even, tail, head), jnp.where(even, head, tail), "gx")
    cols = call(cols_kernel, [VMEM], like(edge_cols.shape[1:], BF16))(estimate)
    edges = slabs(odd_x, odd_y, cols, ex, ox)
    ey, oy = swap(*edges, "gy")
    outgoing = call(
        functools.partial(pack_kernel, devices),
        [SMEM, HBM, HBM, HBM, VMEM],
        like((devices * views * CAP, depth, tile_cols), BF16),
        [
            pltpu.VMEM((views, spare, depth, tile_cols), BF16),
            pltpu.VMEM(measured.shape, BF16),
            pltpu.SMEM(group_shift.shape, jnp.int32),
            pltpu.SMEM(group_length.shape, jnp.int32),
            pltpu.SemaphoreType.DMA((views + 2,)),
        ],
    )(me, group_shift, group_length, measured, edges[0])
    outgoing, ey, oy = lax.optimization_barrier((outgoing, ey, oy))
    arrived = lax.all_to_all(outgoing, ("gx", "gy"), split_axis=0, concat_axis=0, tiled=True)

    norm = kernels / jnp.sum(kernels, axis=3, keepdims=True)
    tap_rows = jnp.stack([norm, norm[..., ::-1]])
    tap_rows = jnp.pad(tap_rows, ((0, 0),) * 4 + ((0, LANES - kernels.shape[3]),))
    recip, edge_recip, rows_mat, ends_mat, cols_mat, turned_mat, far_mat = call(
        forward_kernel,
        [SMEM] * 3 + [VMEM] * 6,
        (
            like(measured.shape, F32),
            like((views, depth, 2 * HW, tile_cols), F32),
            like((bands, 2 * tile_rows, views * tile_rows), BF16),
            like((bands, 4 * HW, views * 2 * HW), BF16),
            like((views, bands, tile_cols, 2 * tile_cols), BF16),
            like((views, bands, tile_rows + 2 * HW, 2 * tile_rows), BF16),
            like((bands, views, 6 * HW, tile_cols), BF16),
        ),
        [
            pltpu.VMEM((views, bands, 2 * tile_rows, tile_rows + 2 * HW), BF16),
            pltpu.VMEM((views, bands, tile_cols, 2 * tile_cols), BF16),
            pltpu.VMEM((views, bands, 2 * HW, 2 * tile_cols), BF16),
        ],
    )(depth_band, odd_x, odd_y, tap_rows, estimate, ex, ox, ey, oy)

    ex, ox = swap(
        *call(
            functools.partial(edges_kernel, devices, tile_rows),
            [SMEM] * 4 + [VMEM] * 2,
            (edge_rows, edge_rows),
            [pltpu.VMEM((views, 2, CAP * HW + 8, depth, tile_cols), F32)],
        )(me, odd_x, group_shift, group_length, arrived, edge_recip),
        "gx",
    )
    ratio, cols = call(
        functools.partial(unpack_kernel, devices),
        [SMEM, SMEM, SMEM, VMEM, VMEM],
        (whole, edge_cols),
        [pltpu.VMEM((views, spare, depth, tile_cols), F32)],
    )(me, group_shift, group_length, arrived, recip)
    ey, oy = swap(*slabs(odd_x, odd_y, cols, ex, ox), "gy")
    near = call(
        near_kernel,
        [SMEM] * 2 + [VMEM] * 6,
        like(estimate.shape, F32),
    )(depth_band, odd_x, rows_mat, ends_mat, cols_mat, ratio, ex, ox)
    return call(
        far_kernel,
        [SMEM] * 2 + [VMEM] * 6,
        like(estimate.shape, F32),
        [
            pltpu.VMEM((depth * 2 * HW, tile_rows + 2 * HW), BF16),
            pltpu.VMEM((views, bands, depth * 2 * HW, tile_rows), F32),
        ],
    )(depth_band, odd_y, turned_mat, far_mat, near, ey, oy, estimate)


def solution(mesh):
    return jax.shard_map(
        body,
        mesh=mesh,
        in_specs=(P(None, "gx", "gy"), P(None, None, "gx", "gy"), P(), P(), P(), P()),
        out_specs=P(None, "gx", "gy"),
        check_vma=False,
    )
```

```python
import functools

import jax
import jax.numpy as jnp
from jax import lax
from jax.experimental import pallas as pl
from jax.experimental.pallas import tpu as pltpu
from jax.sharding import PartitionSpec as P

HW = 8
CAP = 3
LANES = 256
F32 = jnp.float32
BF16 = jnp.bfloat16

VMEM = pl.BlockSpec(memory_space=pltpu.VMEM)
SMEM = pl.BlockSpec(memory_space=pltpu.SMEM)
HBM = pl.BlockSpec(memory_space=pltpu.HBM)
NN = ((1,), (0,))
NT = ((1,), (1,))


def call(kernel, ins, out_shape, scratch=(), out_space=VMEM, limit=16):
    return pl.pallas_call(
        kernel,
        in_specs=ins,
        out_specs=jax.tree.map(lambda _: out_space, out_shape),
        out_shape=out_shape,
        scratch_shapes=list(scratch),
        compiler_params=pltpu.CompilerParams(vmem_limit_bytes=limit * 2**20),
    )


def dot(a, b, dims=NN):
    return lax.dot_general(a, b, (dims, ((), ())), preferred_element_type=F32)


def split(x):
    high = x.astype(BF16)
    return high, (x - high.astype(F32)).astype(BF16)


def stacked(x, axis):
    return jnp.concatenate(split(x), axis=axis)


def halves(x):
    n = x.shape[0] // 2
    return x[:n] + x[n:]


def quarters(x):
    n, m = x.shape[0] // 2, x.shape[1] // 2
    return x[:n, :m] + (x[n:, :m] + x[:n, m:])


def halo(odd_ref, first, second):
    first, second = first.astype(F32), second.astype(F32)
    odd = odd_ref[0] == 1
    after = jnp.where(odd, second, first)
    before = jnp.where(odd, first, second)
    return jnp.concatenate([after, before], axis=0).astype(BF16)


def edge_picker(cols):
    lane = lax.broadcasted_iota(jnp.int32, (2 * HW, cols), 1)
    sub = lax.broadcasted_iota(jnp.int32, (2 * HW, cols), 0)
    return (lane == jnp.where(sub < HW, sub, sub + cols - 2 * HW)).astype(BF16)


def pack_kernel(
    devices, me_ref, shift_hbm, length_hbm, measured_hbm, _, out_hbm,
    rows_ref, measured_ref, out_ref, shift_ref, length_ref, sems,
):
    views, depth, tile_rows, tile_cols = measured_ref.shape
    groups = shift_ref.shape[1]
    loads = [pltpu.make_async_copy(measured_hbm.at[v], measured_ref.at[v], sems.at[v]) for v in range(views)]
    tables = [
        pltpu.make_async_copy(shift_hbm, shift_ref, sems.at[views]),
        pltpu.make_async_copy(length_hbm, length_ref, sems.at[views + 1]),
    ]
    leave = [pltpu.make_async_copy(out_ref.at[v], out_hbm.at[:, v], sems.at[views + 2 + v]) for v in range(views)]
    for copy in loads + tables:
        copy.start()
    rows_ref[:, tile_rows:] = jnp.zeros((views, rows_ref.shape[1] - tile_rows) + rows_ref.shape[2:], BF16)
    lane = lax.broadcasted_iota(jnp.int32, (tile_cols, tile_cols), 1)
    sub = lax.broadcasted_iota(jnp.int32, (tile_cols, tile_cols), 0)
    turn = (lane + sub == tile_cols - 1).astype(BF16)
    me = me_ref[0]
    for view in range(views):
        loads[view].wait()
        for r0 in range(0, tile_rows, 16):
            x = measured_ref[view, :, r0 : r0 + 16, :]
            if view % 2 == 1:
                x = dot(x.reshape(depth * 16, tile_cols), turn).reshape(depth, 16, tile_cols)
            x = jnp.transpose(x.astype(F32), (1, 0, 2))
            rows_ref[view, r0 : r0 + 16] = x.astype(BF16)
        if view == 0:
            for copy in tables:
                copy.wait()

        def group(g, start, view=view):
            peer = lax.rem(me + shift_ref[view, g], devices)
            for k in range(CAP):
                out_ref[view, peer, k] = rows_ref[view, start + k]
            return start + length_ref[view, g]

        lax.fori_loop(0, groups, group, 0, unroll=4)
        leave[view].start()
    for copy in leave:
        copy.wait()


def cols_kernel(cells_ref, out_ref):
    pick = edge_picker(cells_ref.shape[-1])
    for z in range(cells_ref.shape[0]):
        out_ref[z] = dot(pick, cells_ref[z].astype(BF16), NT).astype(BF16)


def slab_kernel(odd_x_ref, odd_y_ref, cols_ref, even_ref, odd_ref, first_ref, second_ref):
    tile_rows = cols_ref.shape[-1]
    pick = edge_picker(even_ref.shape[-1])
    odd = odd_y_ref[0] == 1

    def plane(i, carry):
        ends = halo(odd_x_ref, even_ref[i], odd_ref[i])
        corner = dot(pick, ends, NT)
        cols = cols_ref[i].astype(F32)
        for ref, flag in ((first_ref, odd), (second_ref, jnp.logical_not(odd))):
            ref[i, :, :tile_rows] = jnp.where(flag, cols[:HW], cols[HW:]).astype(BF16)
            ref[i, :, tile_rows:] = jnp.where(flag, corner[:HW], corner[HW:]).astype(BF16)
        return carry

    lax.fori_loop(0, cols_ref.shape[0], plane, 0, unroll=True)


def edges_kernel(
    devices, tile_rows, me_ref, odd_ref, shift_ref, length_ref, arrived_ref, recip_ref, first_ref, second_ref, rows_ref
):
    views = recip_ref.shape[0]
    odd = odd_ref[0] == 1
    groups = shift_ref.shape[1]
    me = me_ref[0]
    low = tile_rows - CAP * HW
    for view in range(views):
        ending = tile_rows - low
        for g in range(groups - HW, groups):
            ending = ending - length_ref[view, g]
        for side, (first, start) in enumerate(((0, 0), (groups - HW, ending))):
            for g in range(first, first + HW):
                source = lax.rem(me - shift_ref[view, g] + devices, devices)
                base = source * (views * CAP) + view * CAP
                for k in range(CAP):
                    rows_ref[view, side, start + k] = arrived_ref[base + k].astype(F32)
                start = start + length_ref[view, g]
        head = jnp.transpose(rows_ref[view, 0, :HW], (1, 0, 2)) * recip_ref[view, :, :HW]
        tail = rows_ref[view, 1, (CAP - 1) * HW : CAP * HW]
        tail = jnp.transpose(tail, (1, 0, 2)) * recip_ref[view, :, HW:]
        first_ref[view] = jnp.where(odd, head, tail).astype(BF16)
        second_ref[view] = jnp.where(odd, tail, head).astype(BF16)


def unpack_kernel(devices, me_ref, shift_ref, length_ref, arrived_ref, recip_ref, out_ref, cols_ref, rows_ref):
    views, depth, tile_rows, tile_cols = out_ref.shape
    groups = shift_ref.shape[1]
    me = me_ref[0]
    pick = edge_picker(tile_cols)
    for view in range(views):

        def group(g, start, view=view):
            source = lax.rem(me - shift_ref[view, g] + devices, devices)
            base = source * (views * CAP) + view * CAP
            for k in range(CAP):
                rows_ref[view, start + k] = arrived_ref[base + k].astype(F32)
            return start + length_ref[view, g]

        lax.fori_loop(0, groups, group, 0, unroll=True)
        for r0 in range(0, tile_rows, 16):
            x = jnp.transpose(rows_ref[view, r0 : r0 + 16], (1, 0, 2))
            out_ref[view, :, r0 : r0 + 16, :] = (x * recip_ref[view, :, r0 : r0 + 16, :]).astype(BF16)
        for z in range(depth):
            cols_ref[view, z] = dot(pick, out_ref[view, z], NT).astype(BF16)


def band(taps, size):
    wide = jnp.broadcast_to(taps, (size, LANES))
    inner = pltpu.roll(wide, LANES - HW, 1, stride=1, stride_axis=0)
    before = pltpu.roll(wide, size + HW, 1, stride=1, stride_axis=0)
    lane = lax.broadcasted_iota(jnp.int32, (size, LANES), 1)
    return jnp.where(lane < size + HW, inner, jnp.where(lane < size + 2 * HW, before, 0.0))


def blur_far(rows, far, across):
    return quarters(dot(stacked(halves(dot(rows, far, NT)), 0), across))


def forward_kernel(
    band_ref, odd_x_ref, odd_y_ref, taps_ref, cells_ref, even_x_ref, other_x_ref, even_y_ref, other_y_ref,
    recip_ref, edge_ref, rows_ref, ends_ref, cols_ref, turned_ref, far_ref, fwd_rows, fwd_cols, fwd_far,
):
    views, depth, tile_rows, tile_cols = recip_ref.shape
    bands = taps_ref.shape[2]
    for view in range(views):
        for b in range(bands):
            along = band(taps_ref[0, view, b, 0:1, :], tile_rows)
            fwd_rows[view, b] = stacked(along[:, : tile_rows + 2 * HW], 0)
            across = band(taps_ref[0, view, b, 1:2, :], tile_cols)
            fwd_cols[view, b] = stacked(across[:, :tile_cols].T, 1)
            fwd_far[view, b] = stacked(across[:, tile_cols:].T[: 2 * HW], 1)
    for b in range(bands):
        ends = jnp.zeros((tile_rows, LANES - tile_rows), F32)
        for view in range(views):
            along = band(taps_ref[1, view, b, 0:1, :], tile_rows)
            rows_ref[b, :, view * tile_rows : (view + 1) * tile_rows] = stacked(along[:, :tile_rows], 0)
            beyond = along[:, tile_rows:]
            ends = ends + (pltpu.roll(beyond, 2 * HW * view, 1) if view else beyond)
            turned_ref[view, b, :tile_rows] = stacked(along[:, :tile_rows].T, 1)
            turned_ref[view, b, tile_rows:] = stacked(beyond.T[: 2 * HW], 1)
            across = band(taps_ref[1, view, b, 1:2, :], tile_cols)
            cols_ref[view, b] = stacked(across[:, :tile_cols].T, 1)
            high, low = split(across[:, tile_cols:].T[: 2 * HW])
            far_ref[b, view] = jnp.concatenate([high, high, low], axis=0)
        ends = jnp.concatenate([ends[:HW], ends[tile_rows - HW :]], axis=0)
        ends_ref[b] = stacked(ends[:, : 2 * HW * views], 0)

    def plane(z, carry):
        b = band_ref[z]
        cells = stacked(cells_ref[z], 1)
        ends = halo(odd_x_ref, even_x_ref[z], other_x_ref[z])
        far = halo(odd_y_ref, even_y_ref[z], other_y_ref[z])
        for view in range(views):
            rows = fwd_rows[view, b]
            blurred = quarters(dot(rows[:, :tile_rows], cells)) + halves(dot(rows[:, tile_rows:], ends))
            blurred = quarters(dot(stacked(blurred, 0), fwd_cols[view, b])) + blur_far(rows, far, fwd_far[view, b])
            recip = 1.0 / blurred.astype(BF16).astype(F32)
            recip_ref[view, z] = recip
            edge_ref[view, z, :HW] = recip[:HW]
            edge_ref[view, z, HW:] = recip[tile_rows - HW :]
        return carry

    lax.fori_loop(0, depth, plane, 0, unroll=2)


def near_kernel(
    band_ref, odd_ref, rows_ref, ends_ref, cols_ref, ratio_ref, even_ref, other_ref, out_ref, inner_ref, outer_ref
):
    views, depth, tile_rows, tile_cols = ratio_ref.shape

    def across(cells, weights):
        blurred = dot(cells, weights)
        return stacked(blurred[:, :tile_cols] + blurred[:, tile_cols:], 1)

    for z in range(depth):
        b = band_ref[z]
        for view in range(views):
            inner_ref[z, view * tile_rows : (view + 1) * tile_rows] = across(ratio_ref[view, z], cols_ref[view, b])
            ends = halo(odd_ref, even_ref[view, z], other_ref[view, z])
            outer_ref[z, view * 2 * HW : (view + 1) * 2 * HW] = across(ends, cols_ref[view, b])
    for z in range(depth):
        b = band_ref[z]
        out_ref[z] = quarters(dot(rows_ref[b], inner_ref[z]))
        ends = quarters(dot(ends_ref[b], outer_ref[z]))
        out_ref[z, :HW] += ends[:HW]
        out_ref[z, tile_rows - HW :] += ends[HW:]


def far_kernel(
    band_ref, odd_ref, turned_ref, far_ref, near_ref, even_ref, other_ref, estimate_ref, out_hbm,
    slab_ref, along_ref, out_ref, sems,
):
    views, bands = turned_ref.shape[:2]
    depth, tile_rows, tile_cols = near_ref.shape
    step = depth // sems.shape[0]
    for view in range(views):
        for z in range(depth):
            slab_ref[view, z * 2 * HW : (z + 1) * 2 * HW] = halo(odd_ref, even_ref[view, z], other_ref[view, z])
    for view in range(views):
        for b in range(bands):
            along = dot(slab_ref[view], turned_ref[view, b])
            high, low = split(along[:, :tile_rows] + along[:, tile_rows:])
            along_ref[view, b, 0] = high
            along_ref[view, b, 1] = low
    leave = []
    for z in range(depth):
        b = band_ref[z]
        parts = []
        for view in range(views):
            high, low = (along_ref[view, b, part, z * 2 * HW : (z + 1) * 2 * HW, :] for part in range(2))
            parts += [high, low, high]
        across = far_ref[b].reshape(views * 6 * HW, tile_cols)
        total = near_ref[z] + dot(jnp.concatenate(parts, axis=0), across, ((0,), (0,)))
        out_ref[z] = estimate_ref[z] * (total * (1.0 / views))
        if z % step == step - 1:
            part = pl.ds(z - step + 1, step)
            leave.append(pltpu.make_async_copy(out_ref.at[part], out_hbm.at[part], sems.at[z // step]))
            leave[-1].start()
    for copy in leave:
        copy.wait()


def swap(first, second, axis):
    count = lax.axis_size(axis)
    pairs = lambda begin: [p for i in range(begin, count - 1, 2) for p in ((i, i + 1), (i + 1, i))]
    return lax.ppermute(first, axis, pairs(0)), lax.ppermute(second, axis, pairs(1))


def slabs(odd_x, odd_y, cols, first, second):
    lead = cols.shape[:-2]
    shape = (cols.size // (cols.shape[-1] * cols.shape[-2]), HW, cols.shape[-1] + 2 * HW)
    merge = lambda x: x.reshape((shape[0],) + x.shape[-2:])
    out = jax.ShapeDtypeStruct(shape, BF16)
    pair = call(slab_kernel, [SMEM] * 2 + [VMEM] * 3, (out, out))(odd_x, odd_y, merge(cols), merge(first), merge(second))
    return [x.reshape(lead + shape[1:]) for x in pair]


def body(estimate, measured, kernels, depth_band, group_shift, group_length):
    devices = lax.axis_size("gx") * lax.axis_size("gy")
    gx, gy = lax.axis_index("gx").astype(jnp.int32), lax.axis_index("gy").astype(jnp.int32)
    me = (gx * lax.axis_size("gy") + gy).reshape(1)
    odd_x, odd_y = (gx % 2).reshape(1), (gy % 2).reshape(1)
    views, depth, tile_rows, tile_cols = measured.shape
    bands = kernels.shape[1]
    spare = tile_rows + 8
    like = jax.ShapeDtypeStruct
    whole = like(measured.shape, BF16)
    edge_cols = like((views, depth, 2 * HW, tile_rows), BF16)
    edge_rows = like((views, depth, HW, tile_cols), BF16)

    head, tail = estimate[:, :HW], estimate[:, tile_rows - HW :]
    even = gx % 2 == 0
    ex, ox = swap(jnp.where(even, tail, head), jnp.where(even, head, tail), "gx")
    cols = call(cols_kernel, [VMEM], like(edge_cols.shape[1:], BF16))(estimate)
    edges = slabs(odd_x, odd_y, cols, ex, ox)
    ey, oy = swap(*edges, "gy")
    outgoing = call(
        functools.partial(pack_kernel, devices),
        [SMEM, HBM, HBM, HBM, VMEM],
        like((devices, views, CAP, depth, tile_cols), BF16),
        [
            pltpu.VMEM((views, spare, depth, tile_cols), BF16),
            pltpu.VMEM(measured.shape, BF16),
            pltpu.VMEM((views, devices, CAP, depth, tile_cols), BF16),
            pltpu.SMEM(group_shift.shape, jnp.int32),
            pltpu.SMEM(group_length.shape, jnp.int32),
            pltpu.SemaphoreType.DMA((2 * views + 2,)),
        ],
        HBM,
        60,
    )(me, group_shift, group_length, measured, edges[0])
    outgoing = outgoing.reshape(devices * views * CAP, depth, tile_cols)
    outgoing, ey, oy = lax.optimization_barrier((outgoing, ey, oy))
    arrived = lax.all_to_all(outgoing, ("gx", "gy"), split_axis=0, concat_axis=0, tiled=True)

    norm = kernels / jnp.sum(kernels, axis=3, keepdims=True)
    tap_rows = jnp.stack([norm, norm[..., ::-1]])
    tap_rows = jnp.pad(tap_rows, ((0, 0),) * 4 + ((0, LANES - kernels.shape[3]),))
    recip, edge_recip, rows_mat, ends_mat, cols_mat, turned_mat, far_mat = call(
        forward_kernel,
        [SMEM] * 3 + [VMEM] * 6,
        (
            like(measured.shape, F32),
            like((views, depth, 2 * HW, tile_cols), F32),
            like((bands, 2 * tile_rows, views * tile_rows), BF16),
            like((bands, 4 * HW, views * 2 * HW), BF16),
            like((views, bands, tile_cols, 2 * tile_cols), BF16),
            like((views, bands, tile_rows + 2 * HW, 2 * tile_rows), BF16),
            like((bands, views, 6 * HW, tile_cols), BF16),
        ),
        [
            pltpu.VMEM((views, bands, 2 * tile_rows, tile_rows + 2 * HW), BF16),
            pltpu.VMEM((views, bands, tile_cols, 2 * tile_cols), BF16),
            pltpu.VMEM((views, bands, 2 * HW, 2 * tile_cols), BF16),
        ],
    )(depth_band, odd_x, odd_y, tap_rows, estimate, ex, ox, ey, oy)

    ex, ox = swap(
        *call(
            functools.partial(edges_kernel, devices, tile_rows),
            [SMEM] * 4 + [VMEM] * 2,
            (edge_rows, edge_rows),
            [pltpu.VMEM((views, 2, CAP * HW + 8, depth, tile_cols), F32)],
        )(me, odd_x, group_shift, group_length, arrived, edge_recip),
        "gx",
    )
    ratio, cols = call(
        functools.partial(unpack_kernel, devices),
        [SMEM, SMEM, SMEM, VMEM, VMEM],
        (whole, edge_cols),
        [pltpu.VMEM((views, spare, depth, tile_cols), F32)],
    )(me, group_shift, group_length, arrived, recip)
    ey, oy = swap(*slabs(odd_x, odd_y, cols, ex, ox), "gy")
    near = call(
        near_kernel,
        [SMEM] * 2 + [VMEM] * 6,
        like(estimate.shape, F32),
        [
            pltpu.VMEM((depth, views * tile_rows, 2 * tile_cols), BF16),
            pltpu.VMEM((depth, views * 2 * HW, 2 * tile_cols), BF16),
        ],
    )(depth_band, odd_x, rows_mat, ends_mat, cols_mat, ratio, ex, ox)
    return call(
        far_kernel,
        [SMEM] * 2 + [VMEM] * 6,
        like(estimate.shape, F32),
        [
            pltpu.VMEM((views, depth * 2 * HW, tile_rows + 2 * HW), BF16),
            pltpu.VMEM((views, bands, 2, depth * 2 * HW, tile_rows), BF16),
            pltpu.VMEM(estimate.shape, F32),
            pltpu.SemaphoreType.DMA((4,)),
        ],
        HBM,
    )(depth_band, odd_y, turned_mat, far_mat, near, ey, oy, estimate)


def solution(mesh):
    return jax.shard_map(
        body,
        mesh=mesh,
        in_specs=(P(None, "gx", "gy"), P(None, None, "gx", "gy"), P(), P(), P(), P()),
        out_specs=P(None, "gx", "gy"),
        check_vma=False,
    )
```

```python
import functools

import jax
import jax.numpy as jnp
from jax import lax
from jax.experimental import pallas as pl
from jax.experimental.pallas import tpu as pltpu
from jax.sharding import PartitionSpec as P

HW = 8
CAP = 3
LANES = 256
F32 = jnp.float32
BF16 = jnp.bfloat16

VMEM = pl.BlockSpec(memory_space=pltpu.VMEM)
SMEM = pl.BlockSpec(memory_space=pltpu.SMEM)
HBM = pl.BlockSpec(memory_space=pltpu.HBM)
NN = ((1,), (0,))
NT = ((1,), (1,))


def call(kernel, ins, out_shape, scratch=(), out_space=VMEM, limit=16):
    return pl.pallas_call(
        kernel,
        in_specs=ins,
        out_specs=jax.tree.map(lambda _: out_space, out_shape),
        out_shape=out_shape,
        scratch_shapes=list(scratch),
        compiler_params=pltpu.CompilerParams(vmem_limit_bytes=limit * 2**20),
    )


def dot(a, b, dims=NN):
    return lax.dot_general(a, b, (dims, ((), ())), preferred_element_type=F32)


def split(x):
    high = x.astype(BF16)
    return high, (x - high.astype(F32)).astype(BF16)


def stacked(x, axis):
    return jnp.concatenate(split(x), axis=axis)


def halves(x):
    n = x.shape[0] // 2
    return x[:n] + x[n:]


def quarters(x):
    n, m = x.shape[0] // 2, x.shape[1] // 2
    return x[:n, :m] + (x[n:, :m] + x[:n, m:])


def halo(odd_ref, first, second):
    first, second = first.astype(F32), second.astype(F32)
    odd = odd_ref[0] == 1
    after = jnp.where(odd, second, first)
    before = jnp.where(odd, first, second)
    return jnp.concatenate([after, before], axis=0).astype(BF16)


def edge_picker(cols):
    lane = lax.broadcasted_iota(jnp.int32, (2 * HW, cols), 1)
    sub = lax.broadcasted_iota(jnp.int32, (2 * HW, cols), 0)
    return (lane == jnp.where(sub < HW, sub, sub + cols - 2 * HW)).astype(BF16)


def pack_kernel(
    devices, me_ref, shift_hbm, length_hbm, measured_hbm, _, out_hbm,
    rows_ref, measured_ref, shift_ref, length_ref, sems,
):
    views, depth, tile_rows, tile_cols = measured_ref.shape
    groups = shift_ref.shape[1]
    loads = [pltpu.make_async_copy(measured_hbm.at[v], measured_ref.at[v], sems.at[v]) for v in range(views)]
    tables = [
        pltpu.make_async_copy(shift_hbm, shift_ref, sems.at[views]),
        pltpu.make_async_copy(length_hbm, length_ref, sems.at[views + 1]),
    ]
    for copy in tables + loads:
        copy.start()
    rows_ref[:, tile_rows:] = jnp.zeros((views, rows_ref.shape[1] - tile_rows) + rows_ref.shape[2:], BF16)
    lane = lax.broadcasted_iota(jnp.int32, (tile_cols, tile_cols), 1)
    sub = lax.broadcasted_iota(jnp.int32, (tile_cols, tile_cols), 0)
    turn = (lane + sub == tile_cols - 1).astype(BF16)
    me = me_ref[0]
    for view in range(views):
        loads[view].wait()
        for r0 in range(0, tile_rows, 16):
            x = measured_ref[view, :, r0 : r0 + 16, :]
            if view % 2 == 1:
                x = dot(x.reshape(depth * 16, tile_cols), turn).reshape(depth, 16, tile_cols)
            x = jnp.transpose(x.astype(F32), (1, 0, 2))
            rows_ref[view, r0 : r0 + 16] = x.astype(BF16)
        if view == 0:
            for copy in tables:
                copy.wait()

        def group(g, start, view=view):
            peer = lax.rem(me + shift_ref[view, g], devices)
            blocks = rows_ref.at[view, pl.ds(start, CAP)]
            pltpu.make_async_copy(blocks, out_hbm.at[peer, view], sems.at[views + 2 + view]).start()
            return start + length_ref[view, g]

        lax.fori_loop(0, groups, group, 0, unroll=True)
    for view in range(views):
        sent = out_hbm.at[pl.ds(0, groups), view]
        pltpu.make_async_copy(sent, sent, sems.at[views + 2 + view]).wait()


def cols_kernel(cells_ref, out_ref):
    pick = edge_picker(cells_ref.shape[-1])
    for z in range(cells_ref.shape[0]):
        out_ref[z] = dot(pick, cells_ref[z].astype(BF16), NT).astype(BF16)


def slab_kernel(odd_x_ref, odd_y_ref, cols_ref, even_ref, odd_ref, first_ref, second_ref):
    tile_rows = cols_ref.shape[-1]
    pick = edge_picker(even_ref.shape[-1])
    odd = odd_y_ref[0] == 1

    def plane(i, carry):
        ends = halo(odd_x_ref, even_ref[i], odd_ref[i])
        corner = dot(pick, ends, NT)
        cols = cols_ref[i].astype(F32)
        for ref, flag in ((first_ref, odd), (second_ref, jnp.logical_not(odd))):
            ref[i, :, :tile_rows] = jnp.where(flag, cols[:HW], cols[HW:]).astype(BF16)
            ref[i, :, tile_rows:] = jnp.where(flag, corner[:HW], corner[HW:]).astype(BF16)
        return carry

    lax.fori_loop(0, cols_ref.shape[0], plane, 0, unroll=True)


def dense_slab_kernel(odd_x_ref, odd_y_ref, cols_ref, even_ref, other_ref, first_ref, second_ref):
    views, depth, _, tile_rows = cols_ref.shape
    count = tile_rows // (2 * HW)
    pick = edge_picker(even_ref.shape[-1])
    odd = odd_y_ref[0] == 1
    for view in range(views):
        for i in range(first_ref.shape[1]):
            if i < depth:
                edge = cols_ref[view, i].astype(F32)
            else:
                planes = range((i - depth) * count, (i - depth + 1) * count)
                ends = [halo(odd_x_ref, even_ref[view, z], other_ref[view, z]) for z in planes]
                edge = dot(pick, jnp.concatenate(ends, axis=0), NT)
            first_ref[view, i] = jnp.where(odd, edge[:HW], edge[HW:]).astype(BF16)
            second_ref[view, i] = jnp.where(odd, edge[HW:], edge[:HW]).astype(BF16)


def edges_kernel(
    devices, tile_rows, me_ref, odd_ref, shift_ref, length_ref, arrived_ref, recip_ref, first_ref, second_ref, rows_ref
):
    views = recip_ref.shape[0]
    odd = odd_ref[0] == 1
    groups = shift_ref.shape[1]
    me = me_ref[0]
    low = tile_rows - CAP * HW
    for view in range(views):
        ending = tile_rows - low
        for g in range(groups - HW, groups):
            ending = ending - length_ref[view, g]
        for side, (first, start) in enumerate(((0, 0), (groups - HW, ending))):
            for g in range(first, first + HW):
                source = lax.rem(me - shift_ref[view, g] + devices, devices)
                base = source * (views * CAP) + view * CAP
                for k in range(CAP):
                    rows_ref[view, side, start + k] = arrived_ref[base + k].astype(F32)
                start = start + length_ref[view, g]
        head = jnp.transpose(rows_ref[view, 0, :HW], (1, 0, 2)) * recip_ref[view, :, :HW]
        tail = rows_ref[view, 1, (CAP - 1) * HW : CAP * HW]
        tail = jnp.transpose(tail, (1, 0, 2)) * recip_ref[view, :, HW:]
        first_ref[view] = jnp.where(odd, head, tail).astype(BF16)
        second_ref[view] = jnp.where(odd, tail, head).astype(BF16)


def unpack_kernel(devices, me_ref, shift_ref, length_ref, arrived_ref, recip_ref, out_ref, cols_ref, rows_ref):
    views, depth, tile_rows, tile_cols = out_ref.shape
    groups = shift_ref.shape[1]
    me = me_ref[0]
    pick = edge_picker(tile_cols)
    for view in range(views):

        def group(g, start, view=view):
            source = lax.rem(me - shift_ref[view, g] + devices, devices)
            base = source * (views * CAP) + view * CAP
            for k in range(CAP):
                rows_ref[view, start + k] = arrived_ref[base + k].astype(F32)
            return start + length_ref[view, g]

        lax.fori_loop(0, groups, group, 0, unroll=True)
        for r0 in range(0, tile_rows, 16):
            x = jnp.transpose(rows_ref[view, r0 : r0 + 16], (1, 0, 2))
            out_ref[view, :, r0 : r0 + 16, :] = (x * recip_ref[view, :, r0 : r0 + 16, :]).astype(BF16)
        for z in range(depth):
            cols_ref[view, z] = dot(pick, out_ref[view, z], NT).astype(BF16)


def band(taps, size):
    wide = jnp.broadcast_to(taps, (size, LANES))
    inner = pltpu.roll(wide, LANES - HW, 1, stride=1, stride_axis=0)
    before = pltpu.roll(wide, size + HW, 1, stride=1, stride_axis=0)
    lane = lax.broadcasted_iota(jnp.int32, (size, LANES), 1)
    return jnp.where(lane < size + HW, inner, jnp.where(lane < size + 2 * HW, before, 0.0))


def blur_far(rows, far, across):
    return quarters(dot(stacked(halves(dot(rows, far, NT)), 0), across))


def forward_kernel(
    band_ref, odd_x_ref, odd_y_ref, taps_ref, cells_ref, even_x_ref, other_x_ref, even_y_ref, other_y_ref,
    recip_ref, edge_ref, rows_ref, ends_ref, cols_ref, turned_ref, far_ref, fwd_rows, fwd_cols, fwd_far,
):
    views, depth, tile_rows, tile_cols = recip_ref.shape
    bands = taps_ref.shape[2]
    for view in range(views):
        for b in range(bands):
            along = band(taps_ref[0, view, b, 0:1, :], tile_rows)
            fwd_rows[view, b] = stacked(along[:, : tile_rows + 2 * HW], 0)
            across = band(taps_ref[0, view, b, 1:2, :], tile_cols)
            fwd_cols[view, b] = stacked(across[:, :tile_cols].T, 1)
            fwd_far[view, b] = stacked(across[:, tile_cols:].T[: 2 * HW], 1)
    for b in range(bands):
        ends = jnp.zeros((tile_rows, LANES - tile_rows), F32)
        for view in range(views):
            along = band(taps_ref[1, view, b, 0:1, :], tile_rows)
            rows_ref[b, :, view * tile_rows : (view + 1) * tile_rows] = stacked(along[:, :tile_rows], 0)
            beyond = along[:, tile_rows:]
            ends = ends + (pltpu.roll(beyond, 2 * HW * view, 1) if view else beyond)
            turned_ref[view, b, :tile_rows] = stacked(along[:, :tile_rows].T, 1)
            turned = stacked(beyond.T[: 2 * HW], 1)
            for at in range(tile_rows, 2 * tile_rows, 2 * HW):
                turned_ref[view, b, at : at + 2 * HW] = turned
            across = band(taps_ref[1, view, b, 1:2, :], tile_cols)
            cols_ref[view, b] = stacked(across[:, :tile_cols].T, 1)
            high, low = split(across[:, tile_cols:].T[: 2 * HW])
            far_ref[b, view] = jnp.concatenate([high, high, low], axis=0)
        ends = jnp.concatenate([ends[:HW], ends[tile_rows - HW :]], axis=0)
        ends_ref[b] = stacked(ends[:, : 2 * HW * views], 0)

    def plane(z, carry):
        b = band_ref[z]
        cells = stacked(cells_ref[z], 1)
        ends = halo(odd_x_ref, even_x_ref[z], other_x_ref[z])
        far = halo(odd_y_ref, even_y_ref[z], other_y_ref[z])
        for view in range(views):
            rows = fwd_rows[view, b]
            blurred = quarters(dot(rows[:, :tile_rows], cells)) + halves(dot(rows[:, tile_rows:], ends))
            blurred = quarters(dot(stacked(blurred, 0), fwd_cols[view, b])) + blur_far(rows, far, fwd_far[view, b])
            recip = 1.0 / blurred.astype(BF16).astype(F32)
            recip_ref[view, z] = recip
            edge_ref[view, z, :HW] = recip[:HW]
            edge_ref[view, z, HW:] = recip[tile_rows - HW :]
        return carry

    lax.fori_loop(0, depth, plane, 0, unroll=2)


def near_kernel(
    band_ref, odd_ref, rows_ref, ends_ref, cols_ref, ratio_ref, even_ref, other_ref, out_ref, inner_ref, outer_ref
):
    views, depth, tile_rows, tile_cols = ratio_ref.shape

    def across(cells, weights):
        blurred = dot(cells, weights)
        return stacked(blurred[:, :tile_cols] + blurred[:, tile_cols:], 1)

    for z in range(depth):
        b = band_ref[z]
        for view in range(views):
            inner_ref[z, view * tile_rows : (view + 1) * tile_rows] = across(ratio_ref[view, z], cols_ref[view, b])
            ends = halo(odd_ref, even_ref[view, z], other_ref[view, z])
            outer_ref[z, view * 2 * HW : (view + 1) * 2 * HW] = across(ends, cols_ref[view, b])
    for z in range(depth):
        b = band_ref[z]
        out_ref[z] = quarters(dot(rows_ref[b], inner_ref[z]))
        ends = quarters(dot(ends_ref[b], outer_ref[z]))
        out_ref[z, :HW] += ends[:HW]
        out_ref[z, tile_rows - HW :] += ends[HW:]


def far_kernel(
    band_ref, odd_ref, turned_ref, far_ref, near_ref, even_ref, other_ref, estimate_ref, out_hbm,
    slab_ref, along_ref, out_ref, sems,
):
    views, bands = turned_ref.shape[:2]
    depth, tile_rows, tile_cols = near_ref.shape
    step = depth // sems.shape[0]
    count = tile_rows // (2 * HW)
    owner = lax.broadcasted_iota(jnp.int32, (2 * HW, tile_rows), 1) // (2 * HW)
    for view in range(views):
        for z in range(depth):
            at = pl.ds(z * 2 * HW, 2 * HW)
            slab_ref[view, at, :tile_rows] = halo(odd_ref, even_ref[view, z], other_ref[view, z])
            tile = depth + z // count
            corners = halo(odd_ref, even_ref[view, tile], other_ref[view, tile])
            slab_ref[view, at, tile_rows:] = jnp.where(owner == z % count, corners.astype(F32), 0.0).astype(BF16)
    for view in range(views):
        for b in range(bands):
            along = dot(slab_ref[view], turned_ref[view, b])
            high, low = split(along[:, :tile_rows] + along[:, tile_rows:])
            along_ref[view, b, 0] = high
            along_ref[view, b, 1] = low
    leave = []
    for z in range(depth):
        b = band_ref[z]
        parts = []
        for view in range(views):
            high, low = (along_ref[view, b, part, z * 2 * HW : (z + 1) * 2 * HW, :] for part in range(2))
            parts += [high, low, high]
        across = far_ref[b].reshape(views * 6 * HW, tile_cols)
        total = near_ref[z] + dot(jnp.concatenate(parts, axis=0), across, ((0,), (0,)))
        out_ref[z] = estimate_ref[z] * (total * (1.0 / views))
        if z % step == step - 1:
            part = pl.ds(z - step + 1, step)
            leave.append(pltpu.make_async_copy(out_ref.at[part], out_hbm.at[part], sems.at[z // step]))
            leave[-1].start()
    for copy in leave:
        copy.wait()


def swap(first, second, axis):
    count = lax.axis_size(axis)
    pairs = lambda begin: [p for i in range(begin, count - 1, 2) for p in ((i, i + 1), (i + 1, i))]
    return lax.ppermute(first, axis, pairs(0)), lax.ppermute(second, axis, pairs(1))


def slabs(odd_x, odd_y, cols, first, second):
    lead = cols.shape[:-2]
    shape = (cols.size // (cols.shape[-1] * cols.shape[-2]), HW, cols.shape[-1] + 2 * HW)
    merge = lambda x: x.reshape((shape[0],) + x.shape[-2:])
    out = jax.ShapeDtypeStruct(shape, BF16)
    pair = call(slab_kernel, [SMEM] * 2 + [VMEM] * 3, (out, out))(odd_x, odd_y, merge(cols), merge(first), merge(second))
    return [x.reshape(lead + shape[1:]) for x in pair]


def body(estimate, measured, kernels, depth_band, group_shift, group_length):
    devices = lax.axis_size("gx") * lax.axis_size("gy")
    gx, gy = lax.axis_index("gx").astype(jnp.int32), lax.axis_index("gy").astype(jnp.int32)
    me = (gx * lax.axis_size("gy") + gy).reshape(1)
    odd_x, odd_y = (gx % 2).reshape(1), (gy % 2).reshape(1)
    views, depth, tile_rows, tile_cols = measured.shape
    bands = kernels.shape[1]
    spare = tile_rows + 8
    like = jax.ShapeDtypeStruct
    whole = like(measured.shape, BF16)
    edge_cols = like((views, depth, 2 * HW, tile_rows), BF16)
    edge_rows = like((views, depth, HW, tile_cols), BF16)

    head, tail = estimate[:, :HW], estimate[:, tile_rows - HW :]
    even = gx % 2 == 0
    ex, ox = swap(jnp.where(even, tail, head), jnp.where(even, head, tail), "gx")
    cols = call(cols_kernel, [VMEM], like(edge_cols.shape[1:], BF16))(estimate)
    edges = slabs(odd_x, odd_y, cols, ex, ox)
    ey, oy = (pltpu.with_memory_space_constraint(x, pltpu.HBM) for x in swap(*edges, "gy"))
    outgoing = call(
        functools.partial(pack_kernel, devices),
        [SMEM, HBM, HBM, HBM, VMEM],
        like((devices, views, CAP, depth, tile_cols), BF16),
        [
            pltpu.VMEM((views, spare, depth, tile_cols), BF16),
            pltpu.VMEM(measured.shape, BF16),
            pltpu.SMEM(group_shift.shape, jnp.int32),
            pltpu.SMEM(group_length.shape, jnp.int32),
            pltpu.SemaphoreType.DMA((2 * views + 2,)),
        ],
        HBM,
        60,
    )(me, group_shift, group_length, measured, edges[0])
    outgoing = outgoing.reshape(devices * views * CAP, depth, tile_cols)
    outgoing, ey, oy = lax.optimization_barrier((outgoing, ey, oy))
    arrived = lax.all_to_all(outgoing, ("gx", "gy"), split_axis=0, concat_axis=0, tiled=True)

    norm = kernels / jnp.sum(kernels, axis=3, keepdims=True)
    tap_rows = jnp.stack([norm, norm[..., ::-1]])
    tap_rows = jnp.pad(tap_rows, ((0, 0),) * 4 + ((0, LANES - kernels.shape[3]),))
    recip, edge_recip, rows_mat, ends_mat, cols_mat, turned_mat, far_mat = call(
        forward_kernel,
        [SMEM] * 3 + [VMEM] * 6,
        (
            like(measured.shape, F32),
            like((views, depth, 2 * HW, tile_cols), F32),
            like((bands, 2 * tile_rows, views * tile_rows), BF16),
            like((bands, 4 * HW, views * 2 * HW), BF16),
            like((views, bands, tile_cols, 2 * tile_cols), BF16),
            like((views, bands, 2 * tile_rows, 2 * tile_rows), BF16),
            like((bands, views, 6 * HW, tile_cols), BF16),
        ),
        [
            pltpu.VMEM((views, bands, 2 * tile_rows, tile_rows + 2 * HW), BF16),
            pltpu.VMEM((views, bands, tile_cols, 2 * tile_cols), BF16),
            pltpu.VMEM((views, bands, 2 * HW, 2 * tile_cols), BF16),
        ],
    )(depth_band, odd_x, odd_y, tap_rows, estimate, ex, ox, ey, oy)

    ex, ox = swap(
        *call(
            functools.partial(edges_kernel, devices, tile_rows),
            [SMEM] * 4 + [VMEM] * 2,
            (edge_rows, edge_rows),
            [pltpu.VMEM((views, 2, CAP * HW + 8, depth, tile_cols), F32)],
        )(me, odd_x, group_shift, group_length, arrived, edge_recip),
        "gx",
    )
    ratio, cols = call(
        functools.partial(unpack_kernel, devices),
        [SMEM, SMEM, SMEM, VMEM, VMEM],
        (whole, edge_cols),
        [pltpu.VMEM((views, spare, depth, tile_cols), F32)],
    )(me, group_shift, group_length, arrived, recip)
    tiles = like((views, depth + depth * 2 * HW // tile_rows, HW, tile_rows), BF16)
    edges = call(dense_slab_kernel, [SMEM] * 2 + [VMEM] * 3, (tiles, tiles))(odd_x, odd_y, cols, ex, ox)
    ey, oy = swap(*edges, "gy")
    near = call(
        near_kernel,
        [SMEM] * 2 + [VMEM] * 6,
        like(estimate.shape, F32),
        [
            pltpu.VMEM((depth, views * tile_rows, 2 * tile_cols), BF16),
            pltpu.VMEM((depth, views * 2 * HW, 2 * tile_cols), BF16),
        ],
    )(depth_band, odd_x, rows_mat, ends_mat, cols_mat, ratio, ex, ox)
    return call(
        far_kernel,
        [SMEM] * 2 + [VMEM] * 6,
        like(estimate.shape, F32),
        [
            pltpu.VMEM((views, depth * 2 * HW, 2 * tile_rows), BF16),
            pltpu.VMEM((views, bands, 2, depth * 2 * HW, tile_rows), BF16),
            pltpu.VMEM(estimate.shape, F32),
            pltpu.SemaphoreType.DMA((4,)),
        ],
        HBM,
    )(depth_band, odd_y, turned_mat, far_mat, near, ey, oy, estimate)


def solution(mesh):
    return jax.shard_map(
        body,
        mesh=mesh,
        in_specs=(P(None, "gx", "gy"), P(None, None, "gx", "gy"), P(), P(), P(), P()),
        out_specs=P(None, "gx", "gy"),
        check_vma=False,
    )
```

```python
import functools

import jax
import jax.numpy as jnp
from jax import lax
from jax.experimental import pallas as pl
from jax.experimental.pallas import tpu as pltpu
from jax.sharding import PartitionSpec as P

HW = 8
CAP = 3
LANES = 256
F32 = jnp.float32
BF16 = jnp.bfloat16

VMEM = pl.BlockSpec(memory_space=pltpu.VMEM)
SMEM = pl.BlockSpec(memory_space=pltpu.SMEM)
HBM = pl.BlockSpec(memory_space=pltpu.HBM)
NN = ((1,), (0,))
NT = ((1,), (1,))


def call(kernel, ins, out_shape, scratch=(), out_space=VMEM, limit=16):
    return pl.pallas_call(
        kernel,
        in_specs=ins,
        out_specs=jax.tree.map(lambda _: out_space, out_shape),
        out_shape=out_shape,
        scratch_shapes=list(scratch),
        compiler_params=pltpu.CompilerParams(vmem_limit_bytes=limit * 2**20),
    )


def dot(a, b, dims=NN):
    return lax.dot_general(a, b, (dims, ((), ())), preferred_element_type=F32)


def split(x):
    high = x.astype(BF16)
    return high, (x - high.astype(F32)).astype(BF16)


def stacked(x, axis):
    return jnp.concatenate(split(x), axis=axis)


def halves(x):
    n = x.shape[0] // 2
    return x[:n] + x[n:]


def quarters(x):
    n, m = x.shape[0] // 2, x.shape[1] // 2
    return x[:n, :m] + (x[n:, :m] + x[:n, m:])


def halo(odd_ref, first, second):
    first, second = first.astype(F32), second.astype(F32)
    odd = odd_ref[0] == 1
    after = jnp.where(odd, second, first)
    before = jnp.where(odd, first, second)
    return jnp.concatenate([after, before], axis=0).astype(BF16)


def edge_picker(cols):
    lane = lax.broadcasted_iota(jnp.int32, (2 * HW, cols), 1)
    sub = lax.broadcasted_iota(jnp.int32, (2 * HW, cols), 0)
    return (lane == jnp.where(sub < HW, sub, sub + cols - 2 * HW)).astype(BF16)


def pack_kernel(
    devices, me_ref, shift_hbm, length_hbm, measured_hbm, out_hbm,
    rows_ref, measured_ref, shift_ref, length_ref, sems,
):
    views, depth, tile_rows, tile_cols = measured_ref.shape
    groups = shift_ref.shape[1]
    loads = [pltpu.make_async_copy(measured_hbm.at[v], measured_ref.at[v], sems.at[v]) for v in range(views)]
    tables = [
        pltpu.make_async_copy(shift_hbm, shift_ref, sems.at[views]),
        pltpu.make_async_copy(length_hbm, length_ref, sems.at[views + 1]),
    ]
    for copy in tables + loads:
        copy.start()
    rows_ref[:, tile_rows:] = jnp.zeros((views, rows_ref.shape[1] - tile_rows) + rows_ref.shape[2:], BF16)
    lane = lax.broadcasted_iota(jnp.int32, (tile_cols, tile_cols), 1)
    sub = lax.broadcasted_iota(jnp.int32, (tile_cols, tile_cols), 0)
    turn = (lane + sub == tile_cols - 1).astype(BF16)
    me = me_ref[0]
    for view in range(views):
        loads[view].wait()
        for r0 in range(0, tile_rows, 16):
            x = measured_ref[view, :, r0 : r0 + 16, :]
            if view % 2 == 1:
                x = dot(x.reshape(depth * 16, tile_cols), turn).reshape(depth, 16, tile_cols)
            x = jnp.transpose(x.astype(F32), (1, 0, 2))
            rows_ref[view, r0 : r0 + 16] = x.astype(BF16)
        if view == 0:
            for copy in tables:
                copy.wait()

        def group(g, start, view=view):
            peer = lax.rem(me + shift_ref[view, g], devices)
            blocks = rows_ref.at[view, pl.ds(start, CAP)]
            pltpu.make_async_copy(blocks, out_hbm.at[peer, view], sems.at[views + 2 + view]).start()
            return start + length_ref[view, g]

        lax.fori_loop(0, groups, group, 0, unroll=True)
    for view in range(views):
        sent = out_hbm.at[pl.ds(0, groups), view]
        pltpu.make_async_copy(sent, sent, sems.at[views + 2 + view]).wait()


def cols_kernel(cells_ref, out_ref):
    pick = edge_picker(cells_ref.shape[-1])
    for z in range(cells_ref.shape[0]):
        out_ref[z] = dot(pick, cells_ref[z].astype(BF16), NT).astype(BF16)


def dense_slab_kernel(odd_x_ref, odd_y_ref, cols_ref, even_ref, other_ref, first_ref, second_ref):
    views, depth, _, tile_rows = cols_ref.shape
    count = tile_rows // (2 * HW)
    pick = edge_picker(even_ref.shape[-1])
    odd = odd_y_ref[0] == 1
    for view in range(views):
        for i in range(first_ref.shape[1]):
            if i < depth:
                edge = cols_ref[view, i].astype(F32)
            else:
                planes = range((i - depth) * count, (i - depth + 1) * count)
                lead = () if len(even_ref.shape) == 3 else (view,)
                ends = [halo(odd_x_ref, even_ref[*lead, z], other_ref[*lead, z]) for z in planes]
                edge = dot(pick, jnp.concatenate(ends, axis=0), NT)
            first_ref[view, i] = jnp.where(odd, edge[:HW], edge[HW:]).astype(BF16)
            second_ref[view, i] = jnp.where(odd, edge[HW:], edge[:HW]).astype(BF16)


def edges_kernel(
    devices, tile_rows, me_ref, odd_x_ref, odd_y_ref, band_ref, shift_ref, length_ref,
    arrived_ref, edge_ref, turned_ref, far_ref, even_ref, other_ref,
    first_ref, second_ref, along_ref, rows_ref, slab_ref, recip_ref,
):
    views, depth = edge_ref.shape[:2]
    odd = odd_x_ref[0] == 1
    groups = shift_ref.shape[1]
    me = me_ref[0]
    low = tile_rows - CAP * HW
    for view in range(views):
        ending = tile_rows - low
        for g in range(groups - HW, groups):
            ending = ending - length_ref[view, g]
        for side, (first, start) in enumerate(((0, 0), (groups - HW, ending))):
            for g in range(first, first + HW):
                source = lax.rem(me - shift_ref[view, g] + devices, devices)
                base = source * (views * CAP) + view * CAP
                for k in range(CAP):
                    rows_ref[view, side, start + k] = arrived_ref[base + k].astype(F32)
                start = start + length_ref[view, g]
    weights = [turned_ref.at[view] for view in range(views)]
    far_products(odd_y_ref, even_ref.at[0], other_ref.at[0], weights, slab_ref, [along_ref.at[v] for v in range(views)])
    pick = edge_picker(tile_rows)
    for view in range(views):
        for z in range(depth):
            b = band_ref[z]
            along = jnp.concatenate(far_parts(along_ref, view, b, z), axis=0)
            blurred = edge_ref[view, z] + dot(dot(pick, along, NT).astype(BF16), far_ref[b, view])
            recip_ref[z] = 1.0 / blurred.astype(BF16).astype(F32)
        head = jnp.transpose(rows_ref[view, 0, :HW], (1, 0, 2)) * recip_ref[:, :HW]
        tail = rows_ref[view, 1, (CAP - 1) * HW : CAP * HW]
        tail = jnp.transpose(tail, (1, 0, 2)) * recip_ref[:, HW:]
        first_ref[view] = jnp.where(odd, head, tail).astype(BF16)
        second_ref[view] = jnp.where(odd, tail, head).astype(BF16)


def unpack_kernel(
    devices, me_ref, band_ref, shift_ref, length_ref, arrived_ref, blurred_ref, far_ref, along_ref,
    out_ref, cols_ref, rows_ref, recip_ref,
):
    views, depth, tile_rows, tile_cols = out_ref.shape
    groups = shift_ref.shape[1]
    me = me_ref[0]
    pick = edge_picker(tile_cols)
    for view in range(views):

        def group(g, start, view=view):
            source = lax.rem(me - shift_ref[view, g] + devices, devices)
            base = source * (views * CAP) + view * CAP
            for k in range(CAP):
                rows_ref[view, start + k] = arrived_ref[base + k].astype(F32)
            return start + length_ref[view, g]

        lax.fori_loop(0, groups, group, 0, unroll=True)
        for z in range(depth):
            b = band_ref[z]
            along = jnp.concatenate(far_parts(along_ref, view, b, z), axis=0)
            blurred = blurred_ref[view, z] + dot(along, far_ref[b, view], ((0,), (0,)))
            recip_ref[z] = 1.0 / blurred.astype(BF16).astype(F32)
        for r0 in range(0, tile_rows, 16):
            x = jnp.transpose(rows_ref[view, r0 : r0 + 16], (1, 0, 2))
            out_ref[view, :, r0 : r0 + 16, :] = (x * recip_ref[:, r0 : r0 + 16, :]).astype(BF16)
        for z in range(depth):
            cols_ref[view, z] = dot(pick, out_ref[view, z], NT).astype(BF16)


def band(taps, size):
    wide = jnp.broadcast_to(taps, (size, LANES))
    inner = pltpu.roll(wide, LANES - HW, 1, stride=1, stride_axis=0)
    before = pltpu.roll(wide, size + HW, 1, stride=1, stride_axis=0)
    lane = lax.broadcasted_iota(jnp.int32, (size, LANES), 1)
    return jnp.where(lane < size + HW, inner, jnp.where(lane < size + 2 * HW, before, 0.0))


def far_products(odd_ref, even_ref, other_ref, weights, slab_ref, along_ref):
    depth = slab_ref.shape[0] // (2 * HW)
    tile_rows = slab_ref.shape[1] // 2
    count = tile_rows // (2 * HW)
    owner = lax.broadcasted_iota(jnp.int32, (2 * HW, tile_rows), 1) // (2 * HW)
    for z in range(depth):
        at = pl.ds(z * 2 * HW, 2 * HW)
        slab_ref[at, :tile_rows] = halo(odd_ref, even_ref[z], other_ref[z])
        corners = halo(odd_ref, even_ref[depth + z // count], other_ref[depth + z // count])
        slab_ref[at, tile_rows:] = jnp.where(owner == z % count, corners.astype(F32), 0.0).astype(BF16)
    for turned_ref, out_ref in zip(weights, along_ref):
        for b in range(turned_ref.shape[0]):
            along = dot(slab_ref[...], turned_ref[b])
            high, low = split(along[:, :tile_rows] + along[:, tile_rows:])
            out_ref[b, 0] = high
            out_ref[b, 1] = low


def far_parts(along_ref, view, b, z):
    at = pl.ds(z * 2 * HW, 2 * HW)
    high, low = along_ref[view, b, 0, at, :], along_ref[view, b, 1, at, :]
    return [high, low, high]


def forward_kernel(
    band_ref, odd_ref, taps_ref, cells_ref, even_ref, other_ref,
    blurred_ref, edge_ref, fwd_turned_ref, fwd_far_ref, rows_ref, ends_ref, cols_ref, turned_ref, far_ref, fwd_rows, fwd_cols,
):
    views, depth, tile_rows, tile_cols = blurred_ref.shape
    bands = taps_ref.shape[2]
    for b in range(bands):
        ends = jnp.zeros((tile_rows, LANES - tile_rows), F32)
        for view in range(views):
            for way in range(2):
                along = band(taps_ref[way, view, b, 0:1, :], tile_rows)
                across = band(taps_ref[way, view, b, 1:2, :], tile_cols)
                beyond = along[:, tile_rows:]
                turned, far = ((fwd_turned_ref, fwd_far_ref), (turned_ref, far_ref))[way]
                turned[view, b, :tile_rows] = stacked(along[:, :tile_rows].T, 1)
                corner = stacked(beyond.T[: 2 * HW], 1)
                for at in range(tile_rows, 2 * tile_rows, 2 * HW):
                    turned[view, b, at : at + 2 * HW] = corner
                high, low = split(across[:, tile_cols:].T[: 2 * HW])
                far[b, view] = jnp.concatenate([high, high, low], axis=0)
                inner = stacked(across[:, :tile_cols].T, 1)
                if way == 0:
                    fwd_rows[view, b] = stacked(along[:, : tile_rows + 2 * HW], 0)
                    fwd_cols[view, b] = inner
                else:
                    rows_ref[b, :, view * tile_rows : (view + 1) * tile_rows] = stacked(along[:, :tile_rows], 0)
                    ends = ends + (pltpu.roll(beyond, 2 * HW * view, 1) if view else beyond)
                    cols_ref[view, b] = inner
        ends = jnp.concatenate([ends[:HW], ends[tile_rows - HW :]], axis=0)
        ends_ref[b] = stacked(ends[:, : 2 * HW * views], 0)

    def plane(z, carry):
        b = band_ref[z]
        cells = stacked(cells_ref[z], 1)
        ends = halo(odd_ref, even_ref[z], other_ref[z])
        for view in range(views):
            rows = fwd_rows[view, b]
            blurred = quarters(dot(rows[:, :tile_rows], cells)) + halves(dot(rows[:, tile_rows:], ends))
            blurred = quarters(dot(stacked(blurred, 0), fwd_cols[view, b]))
            blurred_ref[view, z] = blurred
            edge_ref[view, z, :HW] = blurred[:HW]
            edge_ref[view, z, HW:] = blurred[tile_rows - HW :]
        return carry

    lax.fori_loop(0, depth, plane, 0, unroll=2)


def near_kernel(
    band_ref, odd_ref, rows_ref, ends_ref, cols_ref, ratio_ref, even_ref, other_ref, out_ref, inner_ref, outer_ref
):
    views, depth, tile_rows, tile_cols = ratio_ref.shape

    def across(cells, weights):
        blurred = dot(cells, weights)
        return stacked(blurred[:, :tile_cols] + blurred[:, tile_cols:], 1)

    for z in range(depth):
        b = band_ref[z]
        for view in range(views):
            inner_ref[z, view * tile_rows : (view + 1) * tile_rows] = across(ratio_ref[view, z], cols_ref[view, b])
            ends = halo(odd_ref, even_ref[view, z], other_ref[view, z])
            outer_ref[z, view * 2 * HW : (view + 1) * 2 * HW] = across(ends, cols_ref[view, b])
    for z in range(depth):
        b = band_ref[z]
        out_ref[z] = quarters(dot(rows_ref[b], inner_ref[z]))
        ends = quarters(dot(ends_ref[b], outer_ref[z]))
        out_ref[z, :HW] += ends[:HW]
        out_ref[z, tile_rows - HW :] += ends[HW:]


def far_kernel(
    band_ref, odd_ref, turned_ref, far_ref, near_ref, even_ref, other_ref, estimate_ref, out_hbm,
    slab_ref, along_ref, out_ref, sems,
):
    views, bands = turned_ref.shape[:2]
    depth, tile_rows, tile_cols = near_ref.shape
    step = depth // sems.shape[0]
    for view in range(views):
        far_products(odd_ref, even_ref.at[view], other_ref.at[view], [turned_ref.at[view]], slab_ref.at[view], [along_ref.at[view]])
    leave = []
    for z in range(depth):
        b = band_ref[z]
        parts = []
        for view in range(views):
            parts += far_parts(along_ref, view, b, z)
        across = far_ref[b].reshape(views * 6 * HW, tile_cols)
        total = near_ref[z] + dot(jnp.concatenate(parts, axis=0), across, ((0,), (0,)))
        out_ref[z] = estimate_ref[z] * (total * (1.0 / views))
        if z % step == step - 1:
            part = pl.ds(z - step + 1, step)
            leave.append(pltpu.make_async_copy(out_ref.at[part], out_hbm.at[part], sems.at[z // step]))
            leave[-1].start()
    for copy in leave:
        copy.wait()


def swap(first, second, axis):
    count = lax.axis_size(axis)
    pairs = lambda begin: [p for i in range(begin, count - 1, 2) for p in ((i, i + 1), (i + 1, i))]
    return lax.ppermute(first, axis, pairs(0)), lax.ppermute(second, axis, pairs(1))


def body(estimate, measured, kernels, depth_band, group_shift, group_length):
    devices = lax.axis_size("gx") * lax.axis_size("gy")
    gx, gy = lax.axis_index("gx").astype(jnp.int32), lax.axis_index("gy").astype(jnp.int32)
    me = (gx * lax.axis_size("gy") + gy).reshape(1)
    odd_x, odd_y = (gx % 2).reshape(1), (gy % 2).reshape(1)
    views, depth, tile_rows, tile_cols = measured.shape
    bands = kernels.shape[1]
    spare = tile_rows + 8
    like = jax.ShapeDtypeStruct
    whole = like(measured.shape, BF16)
    edge_cols = like((views, depth, 2 * HW, tile_rows), BF16)
    edge_rows = like((views, depth, HW, tile_cols), BF16)

    head, tail = estimate[:, :HW], estimate[:, tile_rows - HW :]
    even = gx % 2 == 0
    ex, ox = swap(jnp.where(even, tail, head), jnp.where(even, head, tail), "gx")
    outgoing = call(
        functools.partial(pack_kernel, devices),
        [SMEM, HBM, HBM, HBM],
        like((devices, views, CAP, depth, tile_cols), BF16),
        [
            pltpu.VMEM((views, spare, depth, tile_cols), BF16),
            pltpu.VMEM(measured.shape, BF16),
            pltpu.SMEM(group_shift.shape, jnp.int32),
            pltpu.SMEM(group_length.shape, jnp.int32),
            pltpu.SemaphoreType.DMA((2 * views + 2,)),
        ],
        HBM,
        60,
    )(me, group_shift, group_length, measured)
    outgoing = outgoing.reshape(devices * views * CAP, depth, tile_cols)
    ex, ox = (pltpu.with_memory_space_constraint(x, pltpu.HBM) for x in (ex, ox))
    outgoing, ex, ox, cells = lax.optimization_barrier((outgoing, ex, ox, estimate))
    arrived = lax.all_to_all(outgoing, ("gx", "gy"), split_axis=0, concat_axis=0, tiled=True)

    cols = call(cols_kernel, [VMEM], like(edge_cols.shape[1:], BF16))(cells)
    tiles = depth + depth * 2 * HW // tile_rows
    dense = lambda lead, *args: call(
        dense_slab_kernel, [SMEM] * 2 + [VMEM] * 3, (like((lead, tiles, HW, tile_rows), BF16),) * 2
    )(odd_x, odd_y, *args)
    ey, oy = swap(*dense(1, cols[None], ex, ox), "gy")

    norm = kernels / jnp.sum(kernels, axis=3, keepdims=True)
    tap_rows = jnp.stack([norm, norm[..., ::-1]])
    tap_rows = jnp.pad(tap_rows, ((0, 0),) * 4 + ((0, LANES - kernels.shape[3]),))
    turned_like = like((views, bands, 2 * tile_rows, 2 * tile_rows), BF16)
    far_like = like((bands, views, 6 * HW, tile_cols), BF16)
    blurred, edge_blurred, fwd_turned, fwd_far, rows_mat, ends_mat, cols_mat, turned_mat, far_mat = call(
        forward_kernel,
        [SMEM] * 2 + [VMEM] * 4,
        (
            like(measured.shape, F32),
            like((views, depth, 2 * HW, tile_cols), F32),
            turned_like,
            far_like,
            like((bands, 2 * tile_rows, views * tile_rows), BF16),
            like((bands, 4 * HW, views * 2 * HW), BF16),
            like((views, bands, tile_cols, 2 * tile_cols), BF16),
            turned_like,
            far_like,
        ),
        [
            pltpu.VMEM((views, bands, 2 * tile_rows, tile_rows + 2 * HW), BF16),
            pltpu.VMEM((views, bands, tile_cols, 2 * tile_cols), BF16),
        ],
    )(depth_band, odd_x, tap_rows, cells, ex, ox)

    along_like = like((views, bands, 2, depth * 2 * HW, tile_rows), BF16)
    first, second, along = call(
        functools.partial(edges_kernel, devices, tile_rows),
        [SMEM] * 6 + [VMEM] * 6,
        (edge_rows, edge_rows, along_like),
        [
            pltpu.VMEM((views, 2, CAP * HW + 8, depth, tile_cols), F32),
            pltpu.VMEM((depth * 2 * HW, 2 * tile_rows), BF16),
            pltpu.VMEM((depth, 2 * HW, tile_cols), F32),
        ],
    )(me, odd_x, odd_y, depth_band, group_shift, group_length, arrived, edge_blurred, fwd_turned, fwd_far, ey, oy)
    ex, ox = swap(first, second, "gx")
    ratio, cols = call(
        functools.partial(unpack_kernel, devices),
        [SMEM] * 4 + [VMEM] * 4,
        (whole, edge_cols),
        [pltpu.VMEM((views, spare, depth, tile_cols), F32), pltpu.VMEM(estimate.shape, F32)],
    )(me, depth_band, group_shift, group_length, arrived, blurred, fwd_far, along)
    ey, oy = swap(*dense(views, cols, ex, ox), "gy")
    near = call(
        near_kernel,
        [SMEM] * 2 + [VMEM] * 6,
        like(estimate.shape, F32),
        [
            pltpu.VMEM((depth, views * tile_rows, 2 * tile_cols), BF16),
            pltpu.VMEM((depth, views * 2 * HW, 2 * tile_cols), BF16),
        ],
    )(depth_band, odd_x, rows_mat, ends_mat, cols_mat, ratio, ex, ox)
    return call(
        far_kernel,
        [SMEM] * 2 + [VMEM] * 6,
        like(estimate.shape, F32),
        [
            pltpu.VMEM((views, depth * 2 * HW, 2 * tile_rows), BF16),
            pltpu.VMEM((views, bands, 2, depth * 2 * HW, tile_rows), BF16),
            pltpu.VMEM(estimate.shape, F32),
            pltpu.SemaphoreType.DMA((4,)),
        ],
        HBM,
    )(depth_band, odd_y, turned_mat, far_mat, near, ey, oy, estimate)


def solution(mesh):
    return jax.shard_map(
        body,
        mesh=mesh,
        in_specs=(P(None, "gx", "gy"), P(None, None, "gx", "gy"), P(), P(), P(), P()),
        out_specs=P(None, "gx", "gy"),
        check_vma=False,
    )
```

```python
import functools

import jax
import jax.numpy as jnp
from jax import lax
from jax.experimental import pallas as pl
from jax.experimental.pallas import tpu as pltpu
from jax.sharding import PartitionSpec as P

HW = 8
CAP = 3
LANES = 256
F32 = jnp.float32
BF16 = jnp.bfloat16

VMEM = pl.BlockSpec(memory_space=pltpu.VMEM)
SMEM = pl.BlockSpec(memory_space=pltpu.SMEM)
HBM = pl.BlockSpec(memory_space=pltpu.HBM)
NN = ((1,), (0,))
NT = ((1,), (1,))


def call(kernel, ins, out_shape, scratch=(), out_space=VMEM, limit=16):
    return pl.pallas_call(
        kernel,
        in_specs=ins,
        out_specs=jax.tree.map(lambda _: out_space, out_shape),
        out_shape=out_shape,
        scratch_shapes=list(scratch),
        compiler_params=pltpu.CompilerParams(vmem_limit_bytes=limit * 2**20),
    )


def dot(a, b, dims=NN):
    return lax.dot_general(a, b, (dims, ((), ())), preferred_element_type=F32)


def split(x):
    high = x.astype(BF16)
    return high, (x - high.astype(F32)).astype(BF16)


def stacked(x, axis):
    return jnp.concatenate(split(x), axis=axis)


def halves(x):
    n = x.shape[0] // 2
    return x[:n] + x[n:]


def quarters(x):
    n, m = x.shape[0] // 2, x.shape[1] // 2
    return x[:n, :m] + (x[n:, :m] + x[:n, m:])


def halo(odd_ref, first, second):
    first, second = first.astype(F32), second.astype(F32)
    odd = odd_ref[0] == 1
    after = jnp.where(odd, second, first)
    before = jnp.where(odd, first, second)
    return jnp.concatenate([after, before], axis=0).astype(BF16)


def edge_picker(cols):
    lane = lax.broadcasted_iota(jnp.int32, (2 * HW, cols), 1)
    sub = lax.broadcasted_iota(jnp.int32, (2 * HW, cols), 0)
    return (lane == jnp.where(sub < HW, sub, sub + cols - 2 * HW)).astype(BF16)


def pack_kernel(
    devices, me_ref, shift_hbm, length_hbm, measured_hbm, out_hbm,
    rows_ref, measured_ref, shift_ref, length_ref, sems,
):
    views, depth, tile_rows, tile_cols = measured_ref.shape
    groups = shift_ref.shape[1]
    loads = [pltpu.make_async_copy(measured_hbm.at[v], measured_ref.at[v], sems.at[v]) for v in range(views)]
    tables = [
        pltpu.make_async_copy(shift_hbm, shift_ref, sems.at[views]),
        pltpu.make_async_copy(length_hbm, length_ref, sems.at[views + 1]),
    ]
    for copy in tables + loads:
        copy.start()
    rows_ref[:, tile_rows:] = jnp.zeros((views, rows_ref.shape[1] - tile_rows) + rows_ref.shape[2:], BF16)
    lane = lax.broadcasted_iota(jnp.int32, (tile_cols, tile_cols), 1)
    sub = lax.broadcasted_iota(jnp.int32, (tile_cols, tile_cols), 0)
    turn = (lane + sub == tile_cols - 1).astype(BF16)
    me = me_ref[0]
    for view in range(views):
        loads[view].wait()
        for r0 in range(0, tile_rows, 16):
            x = measured_ref[view, :, r0 : r0 + 16, :]
            if view % 2 == 1:
                x = dot(x.reshape(depth * 16, tile_cols), turn).reshape(depth, 16, tile_cols)
            x = jnp.transpose(x.astype(F32), (1, 0, 2))
            rows_ref[view, r0 : r0 + 16] = x.astype(BF16)
        if view == 0:
            for copy in tables:
                copy.wait()

        def group(g, start, view=view):
            peer = lax.rem(me + shift_ref[view, g], devices)
            blocks = rows_ref.at[view, pl.ds(start, CAP)]
            pltpu.make_async_copy(blocks, out_hbm.at[peer, view], sems.at[views + 2 + view]).start()
            return start + length_ref[view, g]

        lax.fori_loop(0, groups, group, 0, unroll=True)
    for view in range(views):
        sent = out_hbm.at[pl.ds(0, groups), view]
        pltpu.make_async_copy(sent, sent, sems.at[views + 2 + view]).wait()


def cols_kernel(cells_ref, out_ref):
    pick = edge_picker(cells_ref.shape[-1])
    for z in range(cells_ref.shape[0]):
        out_ref[z] = dot(pick, cells_ref[z].astype(BF16), NT).astype(BF16)


def dense_slab_kernel(odd_x_ref, odd_y_ref, cols_ref, even_ref, other_ref, first_ref, second_ref):
    views, depth, _, tile_rows = cols_ref.shape
    count = tile_rows // (2 * HW)
    pick = edge_picker(even_ref.shape[-1])
    odd = odd_y_ref[0] == 1
    for view in range(views):
        for i in range(first_ref.shape[1]):
            if i < depth:
                edge = cols_ref[view, i].astype(F32)
            else:
                planes = range((i - depth) * count, (i - depth + 1) * count)
                lead = () if len(even_ref.shape) == 3 else (view,)
                ends = [halo(odd_x_ref, even_ref[*lead, z], other_ref[*lead, z]) for z in planes]
                edge = dot(pick, jnp.concatenate(ends, axis=0), NT)
            first_ref[view, i] = jnp.where(odd, edge[:HW], edge[HW:]).astype(BF16)
            second_ref[view, i] = jnp.where(odd, edge[HW:], edge[:HW]).astype(BF16)


def edges_kernel(
    devices, tile_rows, me_ref, odd_ref, shift_ref, length_ref, arrived_ref, recip_ref, first_ref, second_ref, rows_ref
):
    views = recip_ref.shape[0]
    odd = odd_ref[0] == 1
    groups = shift_ref.shape[1]
    me = me_ref[0]
    low = tile_rows - CAP * HW
    for view in range(views):
        ending = tile_rows - low
        for g in range(groups - HW, groups):
            ending = ending - length_ref[view, g]
        for side, (first, start) in enumerate(((0, 0), (groups - HW, ending))):
            for g in range(first, first + HW):
                source = lax.rem(me - shift_ref[view, g] + devices, devices)
                base = source * (views * CAP) + view * CAP
                for k in range(CAP):
                    rows_ref[view, side, start + k] = arrived_ref[base + k].astype(F32)
                start = start + length_ref[view, g]
        head = jnp.transpose(rows_ref[view, 0, :HW], (1, 0, 2)) * recip_ref[view, :, :HW]
        tail = rows_ref[view, 1, (CAP - 1) * HW : CAP * HW]
        tail = jnp.transpose(tail, (1, 0, 2)) * recip_ref[view, :, HW:]
        first_ref[view] = jnp.where(odd, head, tail).astype(BF16)
        second_ref[view] = jnp.where(odd, tail, head).astype(BF16)


def unpack_kernel(devices, me_ref, shift_ref, length_ref, arrived_ref, recip_ref, out_ref, cols_ref, rows_ref):
    views, depth, tile_rows, tile_cols = out_ref.shape
    groups = shift_ref.shape[1]
    me = me_ref[0]
    pick = edge_picker(tile_cols)
    for view in range(views):

        def group(g, start, view=view):
            source = lax.rem(me - shift_ref[view, g] + devices, devices)
            base = source * (views * CAP) + view * CAP
            for k in range(CAP):
                rows_ref[view, start + k] = arrived_ref[base + k].astype(F32)
            return start + length_ref[view, g]

        lax.fori_loop(0, groups, group, 0, unroll=True)
        for r0 in range(0, tile_rows, 16):
            x = jnp.transpose(rows_ref[view, r0 : r0 + 16], (1, 0, 2))
            out_ref[view, :, r0 : r0 + 16, :] = (x * recip_ref[view, :, r0 : r0 + 16, :]).astype(BF16)
        for z in range(depth):
            cols_ref[view, z] = dot(pick, out_ref[view, z], NT).astype(BF16)


def band(taps, size):
    wide = jnp.broadcast_to(taps, (size, LANES))
    inner = pltpu.roll(wide, LANES - HW, 1, stride=1, stride_axis=0)
    before = pltpu.roll(wide, size + HW, 1, stride=1, stride_axis=0)
    lane = lax.broadcasted_iota(jnp.int32, (size, LANES), 1)
    return jnp.where(lane < size + HW, inner, jnp.where(lane < size + 2 * HW, before, 0.0))


def far_products(odd_ref, even_ref, other_ref, weights, slab_ref, along_ref):
    depth = slab_ref.shape[0] // (2 * HW)
    tile_rows = slab_ref.shape[1] // 2
    count = tile_rows // (2 * HW)
    owner = lax.broadcasted_iota(jnp.int32, (2 * HW, tile_rows), 1) // (2 * HW)
    for z in range(depth):
        at = pl.ds(z * 2 * HW, 2 * HW)
        slab_ref[at, :tile_rows] = halo(odd_ref, even_ref[z], other_ref[z])
        corners = halo(odd_ref, even_ref[depth + z // count], other_ref[depth + z // count])
        slab_ref[at, tile_rows:] = jnp.where(owner == z % count, corners.astype(F32), 0.0).astype(BF16)
    for turned_ref, out_ref in zip(weights, along_ref):
        for b in range(turned_ref.shape[0]):
            along = dot(slab_ref[...], turned_ref[b])
            high, low = split(along[:, :tile_rows] + along[:, tile_rows:])
            out_ref[b, 0] = high
            out_ref[b, 1] = low


def far_parts(along_ref, view, b, z):
    at = pl.ds(z * 2 * HW, 2 * HW)
    high, low = along_ref[view, b, 0, at, :], along_ref[view, b, 1, at, :]
    return [high, low, high]


def forward_kernel(
    band_ref, odd_ref, taps_ref, cells_ref, even_ref, other_ref,
    blurred_ref, fwd_turned_ref, fwd_far_ref, rows_ref, ends_ref, cols_ref, turned_ref, far_ref, fwd_rows, fwd_cols,
):
    views, depth, tile_rows, tile_cols = blurred_ref.shape
    bands = taps_ref.shape[2]
    for b in range(bands):
        ends = jnp.zeros((tile_rows, LANES - tile_rows), F32)
        for view in range(views):
            for way in range(2):
                along = band(taps_ref[way, view, b, 0:1, :], tile_rows)
                across = band(taps_ref[way, view, b, 1:2, :], tile_cols)
                beyond = along[:, tile_rows:]
                turned, far = ((fwd_turned_ref, fwd_far_ref), (turned_ref, far_ref))[way]
                turned[view, b, :tile_rows] = stacked(along[:, :tile_rows].T, 1)
                corner = stacked(beyond.T[: 2 * HW], 1)
                for at in range(tile_rows, 2 * tile_rows, 2 * HW):
                    turned[view, b, at : at + 2 * HW] = corner
                high, low = split(across[:, tile_cols:].T[: 2 * HW])
                far[b, view] = jnp.concatenate([high, high, low], axis=0)
                inner = stacked(across[:, :tile_cols].T, 1)
                if way == 0:
                    fwd_rows[view, b] = stacked(along[:, : tile_rows + 2 * HW], 0)
                    fwd_cols[view, b] = inner
                else:
                    rows_ref[b, :, view * tile_rows : (view + 1) * tile_rows] = stacked(along[:, :tile_rows], 0)
                    ends = ends + (pltpu.roll(beyond, 2 * HW * view, 1) if view else beyond)
                    cols_ref[view, b] = inner
        ends = jnp.concatenate([ends[:HW], ends[tile_rows - HW :]], axis=0)
        ends_ref[b] = stacked(ends[:, : 2 * HW * views], 0)

    def plane(z, carry):
        b = band_ref[z]
        cells = stacked(cells_ref[z], 1)
        ends = halo(odd_ref, even_ref[z], other_ref[z])
        for view in range(views):
            rows = fwd_rows[view, b]
            blurred = quarters(dot(rows[:, :tile_rows], cells)) + halves(dot(rows[:, tile_rows:], ends))
            blurred = quarters(dot(stacked(blurred, 0), fwd_cols[view, b]))
            blurred_ref[view, z] = blurred
        return carry

    lax.fori_loop(0, depth, plane, 0, unroll=2)


def recip_kernel(
    band_ref, odd_ref, turned_ref, far_ref, even_ref, other_ref, blurred_ref, out_ref, edge_ref, slab_ref, along_ref
):
    views, depth, tile_rows, tile_cols = blurred_ref.shape
    weights = [turned_ref.at[view] for view in range(views)]
    far_products(odd_ref, even_ref.at[0], other_ref.at[0], weights, slab_ref, [along_ref.at[v] for v in range(views)])
    for view in range(views):
        for z in range(depth):
            b = band_ref[z]
            along = jnp.concatenate(far_parts(along_ref, view, b, z), axis=0)
            blurred = blurred_ref[view, z] + dot(along, far_ref[b, view], ((0,), (0,)))
            recip = 1.0 / blurred.astype(BF16).astype(F32)
            out_ref[view, z] = recip
            edge_ref[view, z, :HW] = recip[:HW]
            edge_ref[view, z, HW:] = recip[tile_rows - HW :]


def near_kernel(
    band_ref, odd_ref, rows_ref, ends_ref, cols_ref, ratio_ref, even_ref, other_ref, out_ref, inner_ref, outer_ref
):
    views, depth, tile_rows, tile_cols = ratio_ref.shape

    def across(cells, weights):
        blurred = dot(cells, weights)
        return stacked(blurred[:, :tile_cols] + blurred[:, tile_cols:], 1)

    for z in range(depth):
        b = band_ref[z]
        for view in range(views):
            inner_ref[z, view * tile_rows : (view + 1) * tile_rows] = across(ratio_ref[view, z], cols_ref[view, b])
            ends = halo(odd_ref, even_ref[view, z], other_ref[view, z])
            outer_ref[z, view * 2 * HW : (view + 1) * 2 * HW] = across(ends, cols_ref[view, b])
    for z in range(depth):
        b = band_ref[z]
        out_ref[z] = quarters(dot(rows_ref[b], inner_ref[z]))
        ends = quarters(dot(ends_ref[b], outer_ref[z]))
        out_ref[z, :HW] += ends[:HW]
        out_ref[z, tile_rows - HW :] += ends[HW:]


def far_kernel(
    band_ref, odd_ref, turned_ref, far_ref, near_ref, even_ref, other_ref, estimate_ref, out_hbm,
    slab_ref, along_ref, out_ref, sems,
):
    views, bands = turned_ref.shape[:2]
    depth, tile_rows, tile_cols = near_ref.shape
    step = depth // sems.shape[0]
    for view in range(views):
        far_products(odd_ref, even_ref.at[view], other_ref.at[view], [turned_ref.at[view]], slab_ref.at[view], [along_ref.at[view]])
    leave = []
    for z in range(depth):
        b = band_ref[z]
        parts = []
        for view in range(views):
            parts += far_parts(along_ref, view, b, z)
        across = far_ref[b].reshape(views * 6 * HW, tile_cols)
        total = near_ref[z] + dot(jnp.concatenate(parts, axis=0), across, ((0,), (0,)))
        out_ref[z] = estimate_ref[z] * (total * (1.0 / views))
        if z % step == step - 1:
            part = pl.ds(z - step + 1, step)
            leave.append(pltpu.make_async_copy(out_ref.at[part], out_hbm.at[part], sems.at[z // step]))
            leave[-1].start()
    for copy in leave:
        copy.wait()


def swap(first, second, axis):
    count = lax.axis_size(axis)
    pairs = lambda begin: [p for i in range(begin, count - 1, 2) for p in ((i, i + 1), (i + 1, i))]
    return lax.ppermute(first, axis, pairs(0)), lax.ppermute(second, axis, pairs(1))


def body(estimate, measured, kernels, depth_band, group_shift, group_length):
    devices = lax.axis_size("gx") * lax.axis_size("gy")
    gx, gy = lax.axis_index("gx").astype(jnp.int32), lax.axis_index("gy").astype(jnp.int32)
    me = (gx * lax.axis_size("gy") + gy).reshape(1)
    odd_x, odd_y = (gx % 2).reshape(1), (gy % 2).reshape(1)
    views, depth, tile_rows, tile_cols = measured.shape
    bands = kernels.shape[1]
    spare = tile_rows + 8
    like = jax.ShapeDtypeStruct
    whole = like(measured.shape, BF16)
    edge_cols = like((views, depth, 2 * HW, tile_rows), BF16)
    edge_rows = like((views, depth, HW, tile_cols), BF16)

    head, tail = estimate[:, :HW], estimate[:, tile_rows - HW :]
    even = gx % 2 == 0
    ex, ox = swap(jnp.where(even, tail, head), jnp.where(even, head, tail), "gx")
    outgoing = call(
        functools.partial(pack_kernel, devices),
        [SMEM, HBM, HBM, HBM],
        like((devices, views, CAP, depth, tile_cols), BF16),
        [
            pltpu.VMEM((views, spare, depth, tile_cols), BF16),
            pltpu.VMEM(measured.shape, BF16),
            pltpu.SMEM(group_shift.shape, jnp.int32),
            pltpu.SMEM(group_length.shape, jnp.int32),
            pltpu.SemaphoreType.DMA((2 * views + 2,)),
        ],
        HBM,
        60,
    )(me, group_shift, group_length, measured)
    outgoing = outgoing.reshape(devices * views * CAP, depth, tile_cols)
    ex, ox = (pltpu.with_memory_space_constraint(x, pltpu.HBM) for x in (ex, ox))
    outgoing, ex, ox, cells = lax.optimization_barrier((outgoing, ex, ox, estimate))
    arrived = lax.all_to_all(outgoing, ("gx", "gy"), split_axis=0, concat_axis=0, tiled=True)

    cols = call(cols_kernel, [VMEM], like(edge_cols.shape[1:], BF16))(cells)
    tiles = depth + depth * 2 * HW // tile_rows
    dense = lambda lead, *args: call(
        dense_slab_kernel, [SMEM] * 2 + [VMEM] * 3, (like((lead, tiles, HW, tile_rows), BF16),) * 2
    )(odd_x, odd_y, *args)
    ey, oy = swap(*dense(1, cols[None], ex, ox), "gy")

    norm = kernels / jnp.sum(kernels, axis=3, keepdims=True)
    tap_rows = jnp.stack([norm, norm[..., ::-1]])
    tap_rows = jnp.pad(tap_rows, ((0, 0),) * 4 + ((0, LANES - kernels.shape[3]),))
    turned_like = like((views, bands, 2 * tile_rows, 2 * tile_rows), BF16)
    far_like = like((bands, views, 6 * HW, tile_cols), BF16)
    blurred, fwd_turned, fwd_far, rows_mat, ends_mat, cols_mat, turned_mat, far_mat = call(
        forward_kernel,
        [SMEM] * 2 + [VMEM] * 4,
        (
            like(measured.shape, F32),
            turned_like,
            far_like,
            like((bands, 2 * tile_rows, views * tile_rows), BF16),
            like((bands, 4 * HW, views * 2 * HW), BF16),
            like((views, bands, tile_cols, 2 * tile_cols), BF16),
            turned_like,
            far_like,
        ),
        [
            pltpu.VMEM((views, bands, 2 * tile_rows, tile_rows + 2 * HW), BF16),
            pltpu.VMEM((views, bands, tile_cols, 2 * tile_cols), BF16),
        ],
    )(depth_band, odd_x, tap_rows, cells, ex, ox)

    recip, edge_recip = call(
        recip_kernel,
        [SMEM] * 2 + [VMEM] * 5,
        (like(measured.shape, F32), like((views, depth, 2 * HW, tile_cols), F32)),
        [
            pltpu.VMEM((depth * 2 * HW, 2 * tile_rows), BF16),
            pltpu.VMEM((views, bands, 2, depth * 2 * HW, tile_rows), BF16),
        ],
    )(depth_band, odd_y, fwd_turned, fwd_far, ey, oy, blurred)

    first, second = call(
        functools.partial(edges_kernel, devices, tile_rows),
        [SMEM] * 4 + [VMEM] * 2,
        (edge_rows, edge_rows),
        [pltpu.VMEM((views, 2, CAP * HW + 8, depth, tile_cols), F32)],
    )(me, odd_x, group_shift, group_length, arrived, edge_recip)
    ex, ox = swap(first, second, "gx")
    ratio, cols = call(
        functools.partial(unpack_kernel, devices),
        [SMEM] * 3 + [VMEM] * 2,
        (whole, edge_cols),
        [pltpu.VMEM((views, spare, depth, tile_cols), F32)],
    )(me, group_shift, group_length, arrived, recip)
    ey, oy = swap(*dense(views, cols, ex, ox), "gy")
    near = call(
        near_kernel,
        [SMEM] * 2 + [VMEM] * 6,
        like(estimate.shape, F32),
        [
            pltpu.VMEM((depth, views * tile_rows, 2 * tile_cols), BF16),
            pltpu.VMEM((depth, views * 2 * HW, 2 * tile_cols), BF16),
        ],
    )(depth_band, odd_x, rows_mat, ends_mat, cols_mat, ratio, ex, ox)
    return call(
        far_kernel,
        [SMEM] * 2 + [VMEM] * 6,
        like(estimate.shape, F32),
        [
            pltpu.VMEM((views, depth * 2 * HW, 2 * tile_rows), BF16),
            pltpu.VMEM((views, bands, 2, depth * 2 * HW, tile_rows), BF16),
            pltpu.VMEM(estimate.shape, F32),
            pltpu.SemaphoreType.DMA((4,)),
        ],
        HBM,
    )(depth_band, odd_y, turned_mat, far_mat, near, ey, oy, estimate)


def solution(mesh):
    return jax.shard_map(
        body,
        mesh=mesh,
        in_specs=(P(None, "gx", "gy"), P(None, None, "gx", "gy"), P(), P(), P(), P()),
        out_specs=P(None, "gx", "gy"),
        check_vma=False,
    )
```

```python
import functools

import jax
import jax.numpy as jnp
from jax import lax
from jax.experimental import pallas as pl
from jax.experimental.pallas import tpu as pltpu
from jax.sharding import PartitionSpec as P

HW = 8
CAP = 3
LANES = 256
LAST = 2**20
F32 = jnp.float32
BF16 = jnp.bfloat16

VMEM = pl.BlockSpec(memory_space=pltpu.VMEM)
SMEM = pl.BlockSpec(memory_space=pltpu.SMEM)
HBM = pl.BlockSpec(memory_space=pltpu.HBM)
NN = ((1,), (0,))
NT = ((1,), (1,))


def call(kernel, ins, out_shape, scratch=(), out_space=VMEM, limit=16):
    return pl.pallas_call(
        kernel,
        in_specs=ins,
        out_specs=jax.tree.map(lambda _: out_space, out_shape),
        out_shape=out_shape,
        scratch_shapes=list(scratch),
        compiler_params=pltpu.CompilerParams(vmem_limit_bytes=limit * 2**20),
    )


def dot(a, b, dims=NN):
    return lax.dot_general(a, b, (dims, ((), ())), preferred_element_type=F32)


def split(x):
    high = x.astype(BF16)
    return high, (x - high.astype(F32)).astype(BF16)


def stacked(x, axis):
    return jnp.concatenate(split(x), axis=axis)


def halves(x):
    n = x.shape[0] // 2
    return x[:n] + x[n:]


def quarters(x):
    n, m = x.shape[0] // 2, x.shape[1] // 2
    return x[:n, :m] + (x[n:, :m] + x[:n, m:])


def is_odd(place_ref):
    return place_ref[0] % 2 == 1


def halo(place_ref, first, second):
    first, second = first.astype(F32), second.astype(F32)
    odd = is_odd(place_ref)
    after = jnp.where(place_ref[0] >= LAST, 0.0, jnp.where(odd, second, first))
    before = jnp.where(place_ref[0] == 0, 0.0, jnp.where(odd, first, second))
    return jnp.concatenate([after, before], axis=0).astype(BF16)


def edge_picker(cols):
    lane = lax.broadcasted_iota(jnp.int32, (2 * HW, cols), 1)
    sub = lax.broadcasted_iota(jnp.int32, (2 * HW, cols), 0)
    return (lane == jnp.where(sub < HW, sub, sub + cols - 2 * HW)).astype(BF16)


def pack_kernel(
    devices, me_ref, shift_hbm, length_hbm, measured_hbm, out_hbm,
    rows_ref, measured_ref, shift_ref, length_ref, sems,
):
    views, depth, tile_rows, tile_cols = measured_ref.shape
    groups = shift_ref.shape[1]
    loads = [pltpu.make_async_copy(measured_hbm.at[v], measured_ref.at[v], sems.at[v]) for v in range(views)]
    tables = [
        pltpu.make_async_copy(shift_hbm, shift_ref, sems.at[views]),
        pltpu.make_async_copy(length_hbm, length_ref, sems.at[views + 1]),
    ]
    for copy in tables + loads:
        copy.start()
    rows_ref[:, tile_rows:] = jnp.zeros((views, rows_ref.shape[1] - tile_rows) + rows_ref.shape[2:], BF16)
    lane = lax.broadcasted_iota(jnp.int32, (tile_cols, tile_cols), 1)
    sub = lax.broadcasted_iota(jnp.int32, (tile_cols, tile_cols), 0)
    turn = (lane + sub == tile_cols - 1).astype(BF16)
    me = me_ref[0]
    for view in range(views):
        loads[view].wait()
        for r0 in range(0, tile_rows, 16):
            x = measured_ref[view, :, r0 : r0 + 16, :]
            if view % 2 == 1:
                x = dot(x.reshape(depth * 16, tile_cols), turn).reshape(depth, 16, tile_cols)
            x = jnp.transpose(x.astype(F32), (1, 0, 2))
            rows_ref[view, r0 : r0 + 16] = x.astype(BF16)
        if view == 0:
            for copy in tables:
                copy.wait()

        def group(g, start, view=view):
            peer = lax.rem(me + shift_ref[view, g], devices)
            blocks = rows_ref.at[view, pl.ds(start, CAP)]
            pltpu.make_async_copy(blocks, out_hbm.at[peer, view], sems.at[views + 2 + view]).start()
            return start + length_ref[view, g]

        lax.fori_loop(0, groups, group, 0, unroll=True)
    for view in range(views):
        sent = out_hbm.at[pl.ds(0, groups), view]
        pltpu.make_async_copy(sent, sent, sems.at[views + 2 + view]).wait()


def cols_kernel(cells_ref, out_ref):
    pick = edge_picker(cells_ref.shape[-1])
    for z in range(cells_ref.shape[0]):
        out_ref[z] = dot(pick, cells_ref[z].astype(BF16), NT).astype(BF16)


def dense_slab_kernel(place_x_ref, place_y_ref, cols_ref, even_ref, other_ref, first_ref, second_ref):
    views, depth, _, tile_rows = cols_ref.shape
    count = tile_rows // (2 * HW)
    pick = edge_picker(even_ref.shape[-1])
    odd = is_odd(place_y_ref)
    for view in range(views):
        for i in range(first_ref.shape[1]):
            if i < depth:
                edge = cols_ref[view, i].astype(F32)
            else:
                planes = range((i - depth) * count, (i - depth + 1) * count)
                lead = () if len(even_ref.shape) == 3 else (view,)
                ends = [halo(place_x_ref, even_ref[*lead, z], other_ref[*lead, z]) for z in planes]
                edge = dot(pick, jnp.concatenate(ends, axis=0), NT)
            first_ref[view, i] = jnp.where(odd, edge[:HW], edge[HW:]).astype(BF16)
            second_ref[view, i] = jnp.where(odd, edge[HW:], edge[:HW]).astype(BF16)


def edges_kernel(
    devices, tile_rows, me_ref, place_ref, shift_ref, length_ref, arrived_ref, recip_ref, first_ref, second_ref, rows_ref
):
    views = recip_ref.shape[0]
    odd = is_odd(place_ref)
    groups = shift_ref.shape[1]
    me = me_ref[0]
    low = tile_rows - CAP * HW
    for view in range(views):
        ending = tile_rows - low
        for g in range(groups - HW, groups):
            ending = ending - length_ref[view, g]
        for side, (first, start) in enumerate(((0, 0), (groups - HW, ending))):
            for g in range(first, first + HW):
                source = lax.rem(me - shift_ref[view, g] + devices, devices)
                base = source * (views * CAP) + view * CAP
                for k in range(CAP):
                    rows_ref[view, side, start + k] = arrived_ref[base + k].astype(F32)
                start = start + length_ref[view, g]
        head = jnp.transpose(rows_ref[view, 0, :HW], (1, 0, 2)) * recip_ref[view, :, :HW]
        tail = rows_ref[view, 1, (CAP - 1) * HW : CAP * HW]
        tail = jnp.transpose(tail, (1, 0, 2)) * recip_ref[view, :, HW:]
        first_ref[view] = jnp.where(odd, head, tail).astype(BF16)
        second_ref[view] = jnp.where(odd, tail, head).astype(BF16)


def unpack_kernel(devices, me_ref, shift_ref, length_ref, arrived_ref, recip_ref, out_ref, cols_ref, rows_ref):
    views, depth, tile_rows, tile_cols = out_ref.shape
    groups = shift_ref.shape[1]
    me = me_ref[0]
    pick = edge_picker(tile_cols)
    for view in range(views):

        def group(g, start, view=view):
            source = lax.rem(me - shift_ref[view, g] + devices, devices)
            base = source * (views * CAP) + view * CAP
            for k in range(CAP):
                rows_ref[view, start + k] = arrived_ref[base + k].astype(F32)
            return start + length_ref[view, g]

        lax.fori_loop(0, groups, group, 0, unroll=True)
        for r0 in range(0, tile_rows, 16):
            x = jnp.transpose(rows_ref[view, r0 : r0 + 16], (1, 0, 2))
            out_ref[view, :, r0 : r0 + 16, :] = (x * recip_ref[view, :, r0 : r0 + 16, :]).astype(BF16)
        for z in range(depth):
            cols_ref[view, z] = dot(pick, out_ref[view, z], NT).astype(BF16)


def band(taps, size):
    wide = jnp.broadcast_to(taps, (size, LANES))
    inner = pltpu.roll(wide, LANES - HW, 1, stride=1, stride_axis=0)
    before = pltpu.roll(wide, size + HW, 1, stride=1, stride_axis=0)
    lane = lax.broadcasted_iota(jnp.int32, (size, LANES), 1)
    return jnp.where(lane < size + HW, inner, jnp.where(lane < size + 2 * HW, before, 0.0))


def far_products(place_ref, even_ref, other_ref, weights, slab_ref, along_ref):
    depth = slab_ref.shape[0] // (2 * HW)
    tile_rows = slab_ref.shape[1] // 2
    count = tile_rows // (2 * HW)
    owner = lax.broadcasted_iota(jnp.int32, (2 * HW, tile_rows), 1) // (2 * HW)
    for z in range(depth):
        at = pl.ds(z * 2 * HW, 2 * HW)
        slab_ref[at, :tile_rows] = halo(place_ref, even_ref[z], other_ref[z])
        corners = halo(place_ref, even_ref[depth + z // count], other_ref[depth + z // count])
        slab_ref[at, tile_rows:] = jnp.where(owner == z % count, corners.astype(F32), 0.0).astype(BF16)
    for turned_ref, out_ref in zip(weights, along_ref):
        for b in range(turned_ref.shape[0]):
            along = dot(slab_ref[...], turned_ref[b])
            high, low = split(along[:, :tile_rows] + along[:, tile_rows:])
            out_ref[b, 0] = high
            out_ref[b, 1] = low


def far_parts(along_ref, view, b, z):
    at = pl.ds(z * 2 * HW, 2 * HW)
    high, low = along_ref[view, b, 0, at, :], along_ref[view, b, 1, at, :]
    return [high, low, high]


def forward_kernel(
    band_ref, place_ref, taps_ref, cells_ref, even_ref, other_ref,
    blurred_ref, fwd_turned_ref, fwd_far_ref, rows_ref, ends_ref, cols_ref, turned_ref, far_ref, fwd_rows, fwd_cols,
):
    views, depth, tile_rows, tile_cols = blurred_ref.shape
    bands = taps_ref.shape[2]
    for b in range(bands):
        ends = jnp.zeros((tile_rows, LANES - tile_rows), F32)
        for view in range(views):
            for way in range(2):
                along = band(taps_ref[way, view, b, 0:1, :], tile_rows)
                across = band(taps_ref[way, view, b, 1:2, :], tile_cols)
                beyond = along[:, tile_rows:]
                turned, far = ((fwd_turned_ref, fwd_far_ref), (turned_ref, far_ref))[way]
                turned[view, b, :tile_rows] = stacked(along[:, :tile_rows].T, 1)
                corner = stacked(beyond.T[: 2 * HW], 1)
                for at in range(tile_rows, 2 * tile_rows, 2 * HW):
                    turned[view, b, at : at + 2 * HW] = corner
                high, low = split(across[:, tile_cols:].T[: 2 * HW])
                far[b, view] = jnp.concatenate([high, high, low], axis=0)
                inner = stacked(across[:, :tile_cols].T, 1)
                if way == 0:
                    fwd_rows[view, b] = stacked(along[:, : tile_rows + 2 * HW], 0)
                    fwd_cols[view, b] = inner
                else:
                    rows_ref[b, :, view * tile_rows : (view + 1) * tile_rows] = stacked(along[:, :tile_rows], 0)
                    ends = ends + (pltpu.roll(beyond, 2 * HW * view, 1) if view else beyond)
                    cols_ref[view, b] = inner
        ends = jnp.concatenate([ends[:HW], ends[tile_rows - HW :]], axis=0)
        ends_ref[b] = stacked(ends[:, : 2 * HW * views], 0)

    def plane(z, carry):
        b = band_ref[z]
        cells = stacked(cells_ref[z], 1)
        ends = halo(place_ref, even_ref[z], other_ref[z])
        for view in range(views):
            rows = fwd_rows[view, b]
            blurred = quarters(dot(rows[:, :tile_rows], cells)) + halves(dot(rows[:, tile_rows:], ends))
            blurred = quarters(dot(stacked(blurred, 0), fwd_cols[view, b]))
            blurred_ref[view, z] = blurred
        return carry

    lax.fori_loop(0, depth, plane, 0, unroll=2)


def recip_kernel(
    band_ref, place_ref, turned_ref, far_ref, even_ref, other_ref, blurred_ref, out_ref, edge_ref, slab_ref, along_ref
):
    views, depth, tile_rows, tile_cols = blurred_ref.shape
    weights = [turned_ref.at[view] for view in range(views)]
    far_products(place_ref, even_ref.at[0], other_ref.at[0], weights, slab_ref, [along_ref.at[v] for v in range(views)])
    for view in range(views):
        for z in range(depth):
            b = band_ref[z]
            along = jnp.concatenate(far_parts(along_ref, view, b, z), axis=0)
            blurred = blurred_ref[view, z] + dot(along, far_ref[b, view], ((0,), (0,)))
            recip = 1.0 / blurred.astype(BF16).astype(F32)
            out_ref[view, z] = recip
            edge_ref[view, z, :HW] = recip[:HW]
            edge_ref[view, z, HW:] = recip[tile_rows - HW :]


def near_kernel(
    band_ref, place_ref, rows_ref, ends_ref, cols_ref, ratio_ref, even_ref, other_ref, out_ref, inner_ref, outer_ref
):
    views, depth, tile_rows, tile_cols = ratio_ref.shape

    def across(cells, weights):
        blurred = dot(cells, weights)
        return stacked(blurred[:, :tile_cols] + blurred[:, tile_cols:], 1)

    for z in range(depth):
        b = band_ref[z]
        for view in range(views):
            inner_ref[z, view * tile_rows : (view + 1) * tile_rows] = across(ratio_ref[view, z], cols_ref[view, b])
            ends = halo(place_ref, even_ref[view, z], other_ref[view, z])
            outer_ref[z, view * 2 * HW : (view + 1) * 2 * HW] = across(ends, cols_ref[view, b])
    for z in range(depth):
        b = band_ref[z]
        out_ref[z] = quarters(dot(rows_ref[b], inner_ref[z]))
        ends = quarters(dot(ends_ref[b], outer_ref[z]))
        out_ref[z, :HW] += ends[:HW]
        out_ref[z, tile_rows - HW :] += ends[HW:]


def far_kernel(
    band_ref, place_ref, turned_ref, far_ref, near_ref, even_ref, other_ref, estimate_ref, out_hbm,
    slab_ref, along_ref, out_ref, sems,
):
    views, bands = turned_ref.shape[:2]
    depth, tile_rows, tile_cols = near_ref.shape
    step = depth // sems.shape[0]
    for view in range(views):
        far_products(place_ref, even_ref.at[view], other_ref.at[view], [turned_ref.at[view]], slab_ref.at[view], [along_ref.at[view]])
    leave = []
    for z in range(depth):
        b = band_ref[z]
        parts = []
        for view in range(views):
            parts += far_parts(along_ref, view, b, z)
        across = far_ref[b].reshape(views * 6 * HW, tile_cols)
        total = near_ref[z] + dot(jnp.concatenate(parts, axis=0), across, ((0,), (0,)))
        out_ref[z] = estimate_ref[z] * (total * (1.0 / views))
        if z % step == step - 1:
            part = pl.ds(z - step + 1, step)
            leave.append(pltpu.make_async_copy(out_ref.at[part], out_hbm.at[part], sems.at[z // step]))
            leave[-1].start()
    for copy in leave:
        copy.wait()


def swap(first, second, axis):
    count = lax.axis_size(axis)
    pairs = lambda begin: [p for i in range(begin, count, 2) for p in ((i, (i + 1) % count), ((i + 1) % count, i))]
    return lax.ppermute(first, axis, pairs(0)), lax.ppermute(second, axis, pairs(1))


def place(count, at):
    return jnp.where(at == count - 1, at + LAST, at).reshape(1)


def body(estimate, measured, kernels, depth_band, group_shift, group_length):
    devices = lax.axis_size("gx") * lax.axis_size("gy")
    gx, gy = lax.axis_index("gx").astype(jnp.int32), lax.axis_index("gy").astype(jnp.int32)
    me = (gx * lax.axis_size("gy") + gy).reshape(1)
    place_x, place_y = (place(lax.axis_size(axis), at) for axis, at in (("gx", gx), ("gy", gy)))
    views, depth, tile_rows, tile_cols = measured.shape
    bands = kernels.shape[1]
    spare = tile_rows + 8
    like = jax.ShapeDtypeStruct
    whole = like(measured.shape, BF16)
    edge_cols = like((views, depth, 2 * HW, tile_rows), BF16)
    edge_rows = like((views, depth, HW, tile_cols), BF16)

    head, tail = estimate[:, :HW], estimate[:, tile_rows - HW :]
    even = gx % 2 == 0
    ex, ox = swap(jnp.where(even, tail, head), jnp.where(even, head, tail), "gx")
    outgoing = call(
        functools.partial(pack_kernel, devices),
        [SMEM, HBM, HBM, HBM],
        like((devices, views, CAP, depth, tile_cols), BF16),
        [
            pltpu.VMEM((views, spare, depth, tile_cols), BF16),
            pltpu.VMEM(measured.shape, BF16),
            pltpu.SMEM(group_shift.shape, jnp.int32),
            pltpu.SMEM(group_length.shape, jnp.int32),
            pltpu.SemaphoreType.DMA((2 * views + 2,)),
        ],
        HBM,
        60,
    )(me, group_shift, group_length, measured)
    outgoing = outgoing.reshape(devices * views * CAP, depth, tile_cols)
    ex, ox = (pltpu.with_memory_space_constraint(x, pltpu.HBM) for x in (ex, ox))
    outgoing, ex, ox, cells = lax.optimization_barrier((outgoing, ex, ox, estimate))
    arrived = lax.all_to_all(outgoing, ("gx", "gy"), split_axis=0, concat_axis=0, tiled=True)

    cols = call(cols_kernel, [VMEM], like(edge_cols.shape[1:], BF16))(cells)
    tiles = depth + depth * 2 * HW // tile_rows
    dense = lambda lead, *args: call(
        dense_slab_kernel, [SMEM] * 2 + [VMEM] * 3, (like((lead, tiles, HW, tile_rows), BF16),) * 2
    )(place_x, place_y, *args)
    ey, oy = swap(*dense(1, cols[None], ex, ox), "gy")

    norm = kernels / jnp.sum(kernels, axis=3, keepdims=True)
    tap_rows = jnp.stack([norm, norm[..., ::-1]])
    tap_rows = jnp.pad(tap_rows, ((0, 0),) * 4 + ((0, LANES - kernels.shape[3]),))
    turned_like = like((views, bands, 2 * tile_rows, 2 * tile_rows), BF16)
    far_like = like((bands, views, 6 * HW, tile_cols), BF16)
    blurred, fwd_turned, fwd_far, rows_mat, ends_mat, cols_mat, turned_mat, far_mat = call(
        forward_kernel,
        [SMEM] * 2 + [VMEM] * 4,
        (
            like(measured.shape, F32),
            turned_like,
            far_like,
            like((bands, 2 * tile_rows, views * tile_rows), BF16),
            like((bands, 4 * HW, views * 2 * HW), BF16),
            like((views, bands, tile_cols, 2 * tile_cols), BF16),
            turned_like,
            far_like,
        ),
        [
            pltpu.VMEM((views, bands, 2 * tile_rows, tile_rows + 2 * HW), BF16),
            pltpu.VMEM((views, bands, tile_cols, 2 * tile_cols), BF16),
        ],
    )(depth_band, place_x, tap_rows, cells, ex, ox)

    recip, edge_recip = call(
        recip_kernel,
        [SMEM] * 2 + [VMEM] * 5,
        (like(measured.shape, F32), like((views, depth, 2 * HW, tile_cols), F32)),
        [
            pltpu.VMEM((depth * 2 * HW, 2 * tile_rows), BF16),
            pltpu.VMEM((views, bands, 2, depth * 2 * HW, tile_rows), BF16),
        ],
    )(depth_band, place_y, fwd_turned, fwd_far, ey, oy, blurred)

    first, second = call(
        functools.partial(edges_kernel, devices, tile_rows),
        [SMEM] * 4 + [VMEM] * 2,
        (edge_rows, edge_rows),
        [pltpu.VMEM((views, 2, CAP * HW + 8, depth, tile_cols), F32)],
    )(me, place_x, group_shift, group_length, arrived, edge_recip)
    ex, ox = swap(first, second, "gx")
    ratio, cols = call(
        functools.partial(unpack_kernel, devices),
        [SMEM] * 3 + [VMEM] * 2,
        (whole, edge_cols),
        [pltpu.VMEM((views, spare, depth, tile_cols), F32)],
    )(me, group_shift, group_length, arrived, recip)
    ey, oy = swap(*dense(views, cols, ex, ox), "gy")
    near = call(
        near_kernel,
        [SMEM] * 2 + [VMEM] * 6,
        like(estimate.shape, F32),
        [
            pltpu.VMEM((depth, views * tile_rows, 2 * tile_cols), BF16),
            pltpu.VMEM((depth, views * 2 * HW, 2 * tile_cols), BF16),
        ],
    )(depth_band, place_x, rows_mat, ends_mat, cols_mat, ratio, ex, ox)
    return call(
        far_kernel,
        [SMEM] * 2 + [VMEM] * 6,
        like(estimate.shape, F32),
        [
            pltpu.VMEM((views, depth * 2 * HW, 2 * tile_rows), BF16),
            pltpu.VMEM((views, bands, 2, depth * 2 * HW, tile_rows), BF16),
            pltpu.VMEM(estimate.shape, F32),
            pltpu.SemaphoreType.DMA((4,)),
        ],
        HBM,
    )(depth_band, place_y, turned_mat, far_mat, near, ey, oy, estimate)


def solution(mesh):
    return jax.shard_map(
        body,
        mesh=mesh,
        in_specs=(P(None, "gx", "gy"), P(None, None, "gx", "gy"), P(), P(), P(), P()),
        out_specs=P(None, "gx", "gy"),
        check_vma=False,
    )
```

```python
import functools

import jax
import jax.numpy as jnp
from jax import lax
from jax.experimental import pallas as pl
from jax.experimental.pallas import tpu as pltpu
from jax.sharding import PartitionSpec as P

HW = 8
CAP = 3
LANES = 256
LAST = 2**20
F32 = jnp.float32
BF16 = jnp.bfloat16

VMEM = pl.BlockSpec(memory_space=pltpu.VMEM)
SMEM = pl.BlockSpec(memory_space=pltpu.SMEM)
HBM = pl.BlockSpec(memory_space=pltpu.HBM)
NN = ((1,), (0,))
NT = ((1,), (1,))


def call(kernel, ins, out_shape, scratch=(), out_space=VMEM, limit=16):
    return pl.pallas_call(
        kernel,
        in_specs=ins,
        out_specs=jax.tree.map(lambda _: out_space, out_shape),
        out_shape=out_shape,
        scratch_shapes=list(scratch),
        compiler_params=pltpu.CompilerParams(vmem_limit_bytes=limit * 2**20),
    )


def dot(a, b, dims=NN):
    return lax.dot_general(a, b, (dims, ((), ())), preferred_element_type=F32)


def split(x):
    high = x.astype(BF16)
    return high, (x - high.astype(F32)).astype(BF16)


def stacked(x, axis):
    return jnp.concatenate(split(x), axis=axis)


def halves(x):
    n = x.shape[0] // 2
    return x[:n] + x[n:]


def quarters(x):
    n, m = x.shape[0] // 2, x.shape[1] // 2
    return x[:n, :m] + (x[n:, :m] + x[:n, m:])


def is_odd(place_ref):
    return place_ref[0] % 2 == 1


def halo(place_ref, first, second):
    first, second = first.astype(F32), second.astype(F32)
    odd = is_odd(place_ref)
    after = jnp.where(place_ref[0] >= LAST, 0.0, jnp.where(odd, second, first))
    before = jnp.where(place_ref[0] == 0, 0.0, jnp.where(odd, first, second))
    return jnp.concatenate([after, before], axis=0).astype(BF16)


def edge_picker(cols):
    lane = lax.broadcasted_iota(jnp.int32, (2 * HW, cols), 1)
    sub = lax.broadcasted_iota(jnp.int32, (2 * HW, cols), 0)
    return (lane == jnp.where(sub < HW, sub, sub + cols - 2 * HW)).astype(BF16)


def pack_kernel(
    devices, me_ref, shift_hbm, length_hbm, measured_hbm, out_hbm,
    rows_ref, measured_ref, shift_ref, length_ref, sems,
):
    views, depth, tile_rows, tile_cols = measured_ref.shape
    groups = shift_ref.shape[1]
    loads = [pltpu.make_async_copy(measured_hbm.at[v], measured_ref.at[v], sems.at[v]) for v in range(views)]
    tables = [
        pltpu.make_async_copy(shift_hbm, shift_ref, sems.at[views]),
        pltpu.make_async_copy(length_hbm, length_ref, sems.at[views + 1]),
    ]
    for copy in tables + loads:
        copy.start()
    rows_ref[:, tile_rows:] = jnp.zeros((views, rows_ref.shape[1] - tile_rows) + rows_ref.shape[2:], BF16)
    lane = lax.broadcasted_iota(jnp.int32, (tile_cols, tile_cols), 1)
    sub = lax.broadcasted_iota(jnp.int32, (tile_cols, tile_cols), 0)
    turn = (lane + sub == tile_cols - 1).astype(BF16)
    me = me_ref[0]
    for view in range(views):
        loads[view].wait()
        for r0 in range(0, tile_rows, 16):
            x = measured_ref[view, :, r0 : r0 + 16, :]
            if view % 2 == 1:
                x = dot(x.reshape(depth * 16, tile_cols), turn).reshape(depth, 16, tile_cols)
            x = jnp.transpose(x.astype(F32), (1, 0, 2))
            rows_ref[view, r0 : r0 + 16] = x.astype(BF16)
        if view == 0:
            for copy in tables:
                copy.wait()

        def group(g, start, view=view):
            peer = lax.rem(me + shift_ref[view, g], devices)
            blocks = rows_ref.at[view, pl.ds(start, CAP)]
            pltpu.make_async_copy(blocks, out_hbm.at[peer, view], sems.at[views + 2 + view]).start()
            return start + length_ref[view, g]

        lax.fori_loop(0, groups, group, 0, unroll=True)
    for view in range(views):
        sent = out_hbm.at[pl.ds(0, groups), view]
        pltpu.make_async_copy(sent, sent, sems.at[views + 2 + view]).wait()


def cols_kernel(cells_ref, out_ref):
    pick = edge_picker(cells_ref.shape[-1])
    for z in range(cells_ref.shape[0]):
        out_ref[z] = dot(pick, cells_ref[z].astype(BF16), NT).astype(BF16)


def dense_slab_kernel(place_x_ref, place_y_ref, cols_ref, even_ref, other_ref, first_ref, second_ref):
    views, depth, _, tile_rows = cols_ref.shape
    count = tile_rows // (2 * HW)
    pick = edge_picker(even_ref.shape[-1])
    odd = is_odd(place_y_ref)
    for view in range(views):
        for i in range(first_ref.shape[1]):
            if i < depth:
                edge = cols_ref[view, i].astype(F32)
            else:
                planes = range((i - depth) * count, (i - depth + 1) * count)
                lead = () if len(even_ref.shape) == 3 else (view,)
                ends = [halo(place_x_ref, even_ref[*lead, z], other_ref[*lead, z]) for z in planes]
                edge = dot(pick, jnp.concatenate(ends, axis=0), NT)
            first_ref[view, i] = jnp.where(odd, edge[:HW], edge[HW:]).astype(BF16)
            second_ref[view, i] = jnp.where(odd, edge[HW:], edge[:HW]).astype(BF16)


def edges_kernel(
    devices, tile_rows, me_ref, place_ref, shift_ref, length_ref, arrived_ref, recip_ref, first_ref, second_ref, rows_ref
):
    views = recip_ref.shape[0]
    odd = is_odd(place_ref)
    groups = shift_ref.shape[1]
    me = me_ref[0]
    low = tile_rows - CAP * HW
    for view in range(views):
        ending = tile_rows - low
        for g in range(groups - HW, groups):
            ending = ending - length_ref[view, g]
        for side, (first, start) in enumerate(((0, 0), (groups - HW, ending))):
            for g in range(first, first + HW):
                source = lax.rem(me - shift_ref[view, g] + devices, devices)
                base = source * (views * CAP) + view * CAP
                for k in range(CAP):
                    rows_ref[view, side, start + k] = arrived_ref[base + k].astype(F32)
                start = start + length_ref[view, g]
        head = jnp.transpose(rows_ref[view, 0, :HW], (1, 0, 2)) * recip_ref[view, :, :HW]
        tail = rows_ref[view, 1, (CAP - 1) * HW : CAP * HW]
        tail = jnp.transpose(tail, (1, 0, 2)) * recip_ref[view, :, HW:]
        first_ref[view] = jnp.where(odd, head, tail).astype(BF16)
        second_ref[view] = jnp.where(odd, tail, head).astype(BF16)


def unpack_kernel(devices, me_ref, shift_ref, length_ref, arrived_ref, recip_ref, out_ref, cols_ref, rows_ref):
    views, depth, tile_rows, tile_cols = out_ref.shape
    groups = shift_ref.shape[1]
    me = me_ref[0]
    pick = edge_picker(tile_cols)
    for view in range(views):

        def group(g, start, view=view):
            source = lax.rem(me - shift_ref[view, g] + devices, devices)
            base = source * (views * CAP) + view * CAP
            for k in range(CAP):
                rows_ref[view, start + k] = arrived_ref[base + k].astype(F32)
            return start + length_ref[view, g]

        lax.fori_loop(0, groups, group, 0, unroll=True)
        for r0 in range(0, tile_rows, 16):
            x = jnp.transpose(rows_ref[view, r0 : r0 + 16], (1, 0, 2))
            out_ref[view, :, r0 : r0 + 16, :] = (x * recip_ref[view, :, r0 : r0 + 16, :]).astype(BF16)
        for z in range(depth):
            cols_ref[view, z] = dot(pick, out_ref[view, z], NT).astype(BF16)


def band(taps, size):
    wide = jnp.broadcast_to(taps, (size, LANES))
    inner = pltpu.roll(wide, LANES - HW, 1, stride=1, stride_axis=0)
    before = pltpu.roll(wide, size + HW, 1, stride=1, stride_axis=0)
    lane = lax.broadcasted_iota(jnp.int32, (size, LANES), 1)
    return jnp.where(lane < size + HW, inner, jnp.where(lane < size + 2 * HW, before, 0.0))


def far_products(place_ref, even_ref, other_ref, weights, slab_ref, along_ref):
    depth = slab_ref.shape[0] // (2 * HW)
    tile_rows = slab_ref.shape[1] // 2
    count = tile_rows // (2 * HW)
    owner = lax.broadcasted_iota(jnp.int32, (2 * HW, tile_rows), 1) // (2 * HW)
    for z in range(depth):
        at = pl.ds(z * 2 * HW, 2 * HW)
        slab_ref[at, :tile_rows] = halo(place_ref, even_ref[z], other_ref[z])
        corners = halo(place_ref, even_ref[depth + z // count], other_ref[depth + z // count])
        slab_ref[at, tile_rows:] = jnp.where(owner == z % count, corners.astype(F32), 0.0).astype(BF16)
    for turned_ref, out_ref in zip(weights, along_ref):
        for b in range(turned_ref.shape[0]):
            along = dot(slab_ref[...], turned_ref[b])
            high, low = split(along[:, :tile_rows] + along[:, tile_rows:])
            out_ref[b, 0] = high
            out_ref[b, 1] = low


def far_parts(along_ref, view, b, z):
    at = pl.ds(z * 2 * HW, 2 * HW)
    high, low = along_ref[view, b, 0, at, :], along_ref[view, b, 1, at, :]
    return [high, low, high]


def forward_kernel(
    band_ref, place_ref, taps_ref, cells_ref, even_ref, other_ref,
    blurred_ref, fwd_turned_ref, fwd_far_ref, rows_ref, ends_ref, cols_ref, turned_ref, far_ref, fwd_rows, fwd_cols,
):
    views, depth, tile_rows, tile_cols = blurred_ref.shape
    bands = taps_ref.shape[2]
    for b in range(bands):
        ends = jnp.zeros((tile_rows, LANES - tile_rows), F32)
        for view in range(views):
            for way in range(2):
                along = band(taps_ref[way, view, b, 0:1, :], tile_rows)
                across = band(taps_ref[way, view, b, 1:2, :], tile_cols)
                beyond = along[:, tile_rows:]
                turned, far = ((fwd_turned_ref, fwd_far_ref), (turned_ref, far_ref))[way]
                turned[view, b, :tile_rows] = stacked(along[:, :tile_rows].T, 1)
                corner = stacked(beyond.T[: 2 * HW], 1)
                for at in range(tile_rows, 2 * tile_rows, 2 * HW):
                    turned[view, b, at : at + 2 * HW] = corner
                high, low = split(across[:, tile_cols:].T[: 2 * HW])
                far[b, view] = jnp.concatenate([high, high, low], axis=0)
                inner = stacked(across[:, :tile_cols].T, 1)
                if way == 0:
                    fwd_rows[view, b] = stacked(along[:, : tile_rows + 2 * HW], 0)
                    fwd_cols[view, b] = inner
                else:
                    rows_ref[b, :, view * tile_rows : (view + 1) * tile_rows] = stacked(along[:, :tile_rows], 0)
                    ends = ends + (pltpu.roll(beyond, 2 * HW * view, 1) if view else beyond)
                    cols_ref[view, b] = inner
        ends = jnp.concatenate([ends[:HW], ends[tile_rows - HW :]], axis=0)
        ends_ref[b] = stacked(ends[:, : 2 * HW * views], 0)

    def plane(z, carry):
        b = band_ref[z]
        cells = stacked(cells_ref[z], 1)
        ends = halo(place_ref, even_ref[z], other_ref[z])
        for view in range(views):
            rows = fwd_rows[view, b]
            blurred = quarters(dot(rows[:, :tile_rows], cells)) + halves(dot(rows[:, tile_rows:], ends))
            blurred = quarters(dot(stacked(blurred, 0), fwd_cols[view, b]))
            blurred_ref[view, z] = blurred
        return carry

    lax.fori_loop(0, depth, plane, 0, unroll=2)


def recip_kernel(
    band_ref, place_ref, turned_ref, far_ref, even_ref, other_ref, blurred_ref, out_ref, edge_ref, slab_ref, along_ref
):
    views, depth, tile_rows, tile_cols = blurred_ref.shape
    weights = [turned_ref.at[view] for view in range(views)]
    far_products(place_ref, even_ref.at[0], other_ref.at[0], weights, slab_ref, [along_ref.at[v] for v in range(views)])
    for view in range(views):
        for z in range(depth):
            b = band_ref[z]
            along = jnp.concatenate(far_parts(along_ref, view, b, z), axis=0)
            blurred = blurred_ref[view, z] + dot(along, far_ref[b, view], ((0,), (0,)))
            recip = 1.0 / blurred.astype(BF16).astype(F32)
            out_ref[view, z] = recip
            edge_ref[view, z, :HW] = recip[:HW]
            edge_ref[view, z, HW:] = recip[tile_rows - HW :]


def near_kernel(
    band_ref, place_ref, rows_ref, ends_ref, cols_ref, ratio_ref, even_ref, other_ref, out_ref, inner_ref, outer_ref
):
    views, depth, tile_rows, tile_cols = ratio_ref.shape

    def across(cells, weights):
        blurred = dot(cells, weights)
        return stacked(blurred[:, :tile_cols] + blurred[:, tile_cols:], 1)

    for z in range(depth):
        b = band_ref[z]
        for view in range(views):
            inner_ref[z, view * tile_rows : (view + 1) * tile_rows] = across(ratio_ref[view, z], cols_ref[view, b])
            ends = halo(place_ref, even_ref[view, z], other_ref[view, z])
            outer_ref[z, view * 2 * HW : (view + 1) * 2 * HW] = across(ends, cols_ref[view, b])
    for z in range(depth):
        b = band_ref[z]
        out_ref[z] = quarters(dot(rows_ref[b], inner_ref[z]))
        ends = quarters(dot(ends_ref[b], outer_ref[z]))
        out_ref[z, :HW] += ends[:HW]
        out_ref[z, tile_rows - HW :] += ends[HW:]


def far_kernel(
    band_ref, place_ref, turned_ref, far_ref, near_ref, even_ref, other_ref, estimate_ref, out_hbm,
    slab_ref, along_ref, out_ref, sems,
):
    views, bands = turned_ref.shape[:2]
    depth, tile_rows, tile_cols = near_ref.shape
    step = depth // sems.shape[0]
    for view in range(views):
        far_products(place_ref, even_ref.at[view], other_ref.at[view], [turned_ref.at[view]], slab_ref.at[view], [along_ref.at[view]])
    leave = []
    for z in range(depth):
        b = band_ref[z]
        parts = []
        for view in range(views):
            parts += far_parts(along_ref, view, b, z)
        across = far_ref[b].reshape(views * 6 * HW, tile_cols)
        total = near_ref[z] + dot(jnp.concatenate(parts, axis=0), across, ((0,), (0,)))
        out_ref[z] = estimate_ref[z] * (total * (1.0 / views))
        if z % step == step - 1:
            part = pl.ds(z - step + 1, step)
            leave.append(pltpu.make_async_copy(out_ref.at[part], out_hbm.at[part], sems.at[z // step]))
            leave[-1].start()
    for copy in leave:
        copy.wait()


def swap(first, second, axis, ring=True):
    count = lax.axis_size(axis)
    chain = lambda begin: range(begin, count if ring else count - 1, 2)
    pairs = lambda begin: [p for i in chain(begin) for p in ((i, (i + 1) % count), ((i + 1) % count, i))]
    late = lax.ppermute(second, axis, pairs(1))
    return lax.ppermute(first, axis, pairs(0)), late


def place(count, at):
    return jnp.where(at == count - 1, at + LAST, at).reshape(1)


def body(estimate, measured, kernels, depth_band, group_shift, group_length):
    devices = lax.axis_size("gx") * lax.axis_size("gy")
    gx, gy = lax.axis_index("gx").astype(jnp.int32), lax.axis_index("gy").astype(jnp.int32)
    me = (gx * lax.axis_size("gy") + gy).reshape(1)
    place_x, place_y = (place(lax.axis_size(axis), at) for axis, at in (("gx", gx), ("gy", gy)))
    views, depth, tile_rows, tile_cols = measured.shape
    bands = kernels.shape[1]
    spare = tile_rows + 8
    like = jax.ShapeDtypeStruct
    whole = like(measured.shape, BF16)
    edge_cols = like((views, depth, 2 * HW, tile_rows), BF16)
    edge_rows = like((views, depth, HW, tile_cols), BF16)

    head, tail = estimate[:, :HW], estimate[:, tile_rows - HW :]
    even = gx % 2 == 0
    ex, ox = swap(jnp.where(even, tail, head), jnp.where(even, head, tail), "gx")
    outgoing = call(
        functools.partial(pack_kernel, devices),
        [SMEM, HBM, HBM, HBM],
        like((devices, views, CAP, depth, tile_cols), BF16),
        [
            pltpu.VMEM((views, spare, depth, tile_cols), BF16),
            pltpu.VMEM(measured.shape, BF16),
            pltpu.SMEM(group_shift.shape, jnp.int32),
            pltpu.SMEM(group_length.shape, jnp.int32),
            pltpu.SemaphoreType.DMA((2 * views + 2,)),
        ],
        HBM,
        60,
    )(me, group_shift, group_length, measured)
    outgoing = outgoing.reshape(devices * views * CAP, depth, tile_cols)
    outgoing, ex, ox, cells = lax.optimization_barrier((outgoing, ex, ox, estimate))
    arrived = lax.all_to_all(outgoing, ("gx", "gy"), split_axis=0, concat_axis=0, tiled=True)

    cols = call(cols_kernel, [VMEM], like(edge_cols.shape[1:], BF16))(cells)
    tiles = depth + depth * 2 * HW // tile_rows
    dense = lambda lead, *args: call(
        dense_slab_kernel, [SMEM] * 2 + [VMEM] * 3, (like((lead, tiles, HW, tile_rows), BF16),) * 2
    )(place_x, place_y, *args)
    ey, oy = swap(*dense(1, cols[None], ex, ox), "gy", ring=False)

    norm = kernels / jnp.sum(kernels, axis=3, keepdims=True)
    tap_rows = jnp.stack([norm, norm[..., ::-1]])
    tap_rows = jnp.pad(tap_rows, ((0, 0),) * 4 + ((0, LANES - kernels.shape[3]),))
    turned_like = like((views, bands, 2 * tile_rows, 2 * tile_rows), BF16)
    far_like = like((bands, views, 6 * HW, tile_cols), BF16)
    blurred, fwd_turned, fwd_far, rows_mat, ends_mat, cols_mat, turned_mat, far_mat = call(
        forward_kernel,
        [SMEM] * 2 + [VMEM] * 4,
        (
            like(measured.shape, F32),
            turned_like,
            far_like,
            like((bands, 2 * tile_rows, views * tile_rows), BF16),
            like((bands, 4 * HW, views * 2 * HW), BF16),
            like((views, bands, tile_cols, 2 * tile_cols), BF16),
            turned_like,
            far_like,
        ),
        [
            pltpu.VMEM((views, bands, 2 * tile_rows, tile_rows + 2 * HW), BF16),
            pltpu.VMEM((views, bands, tile_cols, 2 * tile_cols), BF16),
        ],
    )(depth_band, place_x, tap_rows, cells, ex, ox)

    recip, edge_recip = call(
        recip_kernel,
        [SMEM] * 2 + [VMEM] * 5,
        (like(measured.shape, F32), like((views, depth, 2 * HW, tile_cols), F32)),
        [
            pltpu.VMEM((depth * 2 * HW, 2 * tile_rows), BF16),
            pltpu.VMEM((views, bands, 2, depth * 2 * HW, tile_rows), BF16),
        ],
    )(depth_band, place_y, fwd_turned, fwd_far, ey, oy, blurred)

    first, second = call(
        functools.partial(edges_kernel, devices, tile_rows),
        [SMEM] * 4 + [VMEM] * 2,
        (edge_rows, edge_rows),
        [pltpu.VMEM((views, 2, CAP * HW + 8, depth, tile_cols), F32)],
    )(me, place_x, group_shift, group_length, arrived, edge_recip)
    ex, ox = swap(first, second, "gx")
    ratio, cols = call(
        functools.partial(unpack_kernel, devices),
        [SMEM] * 3 + [VMEM] * 2,
        (whole, edge_cols),
        [pltpu.VMEM((views, spare, depth, tile_cols), F32)],
    )(me, group_shift, group_length, arrived, recip)
    ey, oy = swap(*dense(views, cols, ex, ox), "gy")
    near = call(
        near_kernel,
        [SMEM] * 2 + [VMEM] * 6,
        like(estimate.shape, F32),
        [
            pltpu.VMEM((depth, views * tile_rows, 2 * tile_cols), BF16),
            pltpu.VMEM((depth, views * 2 * HW, 2 * tile_cols), BF16),
        ],
    )(depth_band, place_x, rows_mat, ends_mat, cols_mat, ratio, ex, ox)
    return call(
        far_kernel,
        [SMEM] * 2 + [VMEM] * 6,
        like(estimate.shape, F32),
        [
            pltpu.VMEM((views, depth * 2 * HW, 2 * tile_rows), BF16),
            pltpu.VMEM((views, bands, 2, depth * 2 * HW, tile_rows), BF16),
            pltpu.VMEM(estimate.shape, F32),
            pltpu.SemaphoreType.DMA((4,)),
        ],
        HBM,
    )(depth_band, place_y, turned_mat, far_mat, near, ey, oy, estimate)


def solution(mesh):
    return jax.shard_map(
        body,
        mesh=mesh,
        in_specs=(P(None, "gx", "gy"), P(None, None, "gx", "gy"), P(), P(), P(), P()),
        out_specs=P(None, "gx", "gy"),
        check_vma=False,
    )
```

```python
import functools

import jax
import jax.numpy as jnp
from jax import lax
from jax.experimental import pallas as pl
from jax.experimental.pallas import tpu as pltpu
from jax.sharding import PartitionSpec as P

HW = 8
CAP = 3
LANES = 256
LAST = 2**20
F32 = jnp.float32
BF16 = jnp.bfloat16

VMEM = pl.BlockSpec(memory_space=pltpu.VMEM)
SMEM = pl.BlockSpec(memory_space=pltpu.SMEM)
HBM = pl.BlockSpec(memory_space=pltpu.HBM)
NN = ((1,), (0,))
NT = ((1,), (1,))


def call(kernel, ins, out_shape, scratch=(), out_space=VMEM, limit=16):
    return pl.pallas_call(
        kernel,
        in_specs=ins,
        out_specs=jax.tree.map(lambda _: out_space, out_shape),
        out_shape=out_shape,
        scratch_shapes=list(scratch),
        compiler_params=pltpu.CompilerParams(vmem_limit_bytes=limit * 2**20),
    )


def dot(a, b, dims=NN):
    return lax.dot_general(a, b, (dims, ((), ())), preferred_element_type=F32)


def split(x):
    high = x.astype(BF16)
    return high, (x - high.astype(F32)).astype(BF16)


def stacked(x, axis):
    return jnp.concatenate(split(x), axis=axis)


def halves(x):
    n = x.shape[0] // 2
    return x[:n] + x[n:]


def quarters(x):
    n, m = x.shape[0] // 2, x.shape[1] // 2
    return x[:n, :m] + (x[n:, :m] + x[:n, m:])


def is_odd(place_ref):
    return place_ref[0] % 2 == 1


def halo(place_ref, first, second):
    first, second = first.astype(F32), second.astype(F32)
    odd = is_odd(place_ref)
    after = jnp.where(place_ref[0] >= LAST, 0.0, jnp.where(odd, second, first))
    before = jnp.where(place_ref[0] == 0, 0.0, jnp.where(odd, first, second))
    return jnp.concatenate([after, before], axis=0).astype(BF16)


def edge_picker(cols):
    lane = lax.broadcasted_iota(jnp.int32, (2 * HW, cols), 1)
    sub = lax.broadcasted_iota(jnp.int32, (2 * HW, cols), 0)
    return (lane == jnp.where(sub < HW, sub, sub + cols - 2 * HW)).astype(BF16)


def pack_kernel(
    devices, me_ref, shift_hbm, length_hbm, measured_hbm, out_hbm,
    rows_ref, measured_ref, shift_ref, length_ref, sems,
):
    views, depth, tile_rows, tile_cols = measured_ref.shape
    groups = shift_ref.shape[1]
    loads = [pltpu.make_async_copy(measured_hbm.at[v], measured_ref.at[v], sems.at[v]) for v in range(views)]
    tables = [
        pltpu.make_async_copy(shift_hbm, shift_ref, sems.at[views]),
        pltpu.make_async_copy(length_hbm, length_ref, sems.at[views + 1]),
    ]
    for copy in tables + loads:
        copy.start()
    rows_ref[:, tile_rows:] = jnp.zeros((views, rows_ref.shape[1] - tile_rows) + rows_ref.shape[2:], BF16)
    lane = lax.broadcasted_iota(jnp.int32, (tile_cols, tile_cols), 1)
    sub = lax.broadcasted_iota(jnp.int32, (tile_cols, tile_cols), 0)
    turn = (lane + sub == tile_cols - 1).astype(BF16)
    me = me_ref[0]
    for view in range(views):
        loads[view].wait()
        for r0 in range(0, tile_rows, 16):
            x = measured_ref[view, :, r0 : r0 + 16, :]
            if view % 2 == 1:
                x = dot(x.reshape(depth * 16, tile_cols), turn).reshape(depth, 16, tile_cols)
            x = jnp.transpose(x.astype(F32), (1, 0, 2))
            rows_ref[view, r0 : r0 + 16] = x.astype(BF16)
        if view == 0:
            for copy in tables:
                copy.wait()

        def group(g, start, view=view):
            peer = lax.rem(me + shift_ref[view, g], devices)
            blocks = rows_ref.at[view, pl.ds(start, CAP)]
            pltpu.make_async_copy(blocks, out_hbm.at[peer, view], sems.at[views + 2 + view]).start()
            return start + length_ref[view, g]

        lax.fori_loop(0, groups, group, 0, unroll=True)
    for view in range(views):
        sent = out_hbm.at[pl.ds(0, groups), view]
        pltpu.make_async_copy(sent, sent, sems.at[views + 2 + view]).wait()


def cols_kernel(cells_ref, out_ref):
    pick = edge_picker(cells_ref.shape[-1])
    for z in range(cells_ref.shape[0]):
        out_ref[z] = dot(pick, cells_ref[z].astype(BF16), NT).astype(BF16)


def dense_slab_kernel(place_x_ref, place_y_ref, cols_ref, even_ref, other_ref, first_ref, second_ref):
    views, depth, _, tile_rows = cols_ref.shape
    count = tile_rows // (2 * HW)
    pick = edge_picker(even_ref.shape[-1])
    odd = is_odd(place_y_ref)
    for view in range(views):
        for i in range(first_ref.shape[1]):
            if i < depth:
                edge = cols_ref[view, i].astype(F32)
            else:
                planes = range((i - depth) * count, (i - depth + 1) * count)
                lead = () if len(even_ref.shape) == 3 else (view,)
                ends = [halo(place_x_ref, even_ref[*lead, z], other_ref[*lead, z]) for z in planes]
                edge = dot(pick, jnp.concatenate(ends, axis=0), NT)
            first_ref[view, i] = jnp.where(odd, edge[:HW], edge[HW:]).astype(BF16)
            second_ref[view, i] = jnp.where(odd, edge[HW:], edge[:HW]).astype(BF16)


def edges_kernel(
    devices, tile_rows, me_ref, place_ref, shift_ref, length_ref, arrived_ref, recip_ref, first_ref, second_ref, rows_ref
):
    views = recip_ref.shape[0]
    odd = is_odd(place_ref)
    groups = shift_ref.shape[1]
    me = me_ref[0]
    low = tile_rows - CAP * HW
    for view in range(views):
        ending = tile_rows - low
        for g in range(groups - HW, groups):
            ending = ending - length_ref[view, g]
        for side, (first, start) in enumerate(((0, 0), (groups - HW, ending))):
            for g in range(first, first + HW):
                source = lax.rem(me - shift_ref[view, g] + devices, devices)
                base = source * (views * CAP) + view * CAP
                for k in range(CAP):
                    rows_ref[view, side, start + k] = arrived_ref[base + k].astype(F32)
                start = start + length_ref[view, g]
        head = jnp.transpose(rows_ref[view, 0, :HW], (1, 0, 2)) * recip_ref[view, :, :HW]
        tail = rows_ref[view, 1, (CAP - 1) * HW : CAP * HW]
        tail = jnp.transpose(tail, (1, 0, 2)) * recip_ref[view, :, HW:]
        first_ref[view] = jnp.where(odd, head, tail).astype(BF16)
        second_ref[view] = jnp.where(odd, tail, head).astype(BF16)


def unpack_kernel(devices, me_ref, shift_ref, length_ref, arrived_ref, recip_ref, out_ref, cols_ref, rows_ref):
    views, depth, tile_rows, tile_cols = out_ref.shape
    groups = shift_ref.shape[1]
    me = me_ref[0]
    pick = edge_picker(tile_cols)
    for view in range(views):

        def group(g, start, view=view):
            source = lax.rem(me - shift_ref[view, g] + devices, devices)
            base = source * (views * CAP) + view * CAP
            for k in range(CAP):
                rows_ref[view, start + k] = arrived_ref[base + k].astype(F32)
            return start + length_ref[view, g]

        lax.fori_loop(0, groups, group, 0, unroll=True)
        for r0 in range(0, tile_rows, 16):
            x = jnp.transpose(rows_ref[view, r0 : r0 + 16], (1, 0, 2))
            out_ref[view, :, r0 : r0 + 16, :] = (x * recip_ref[view, :, r0 : r0 + 16, :]).astype(BF16)
        for z in range(depth):
            cols_ref[view, z] = dot(pick, out_ref[view, z], NT).astype(BF16)


def band(taps, size):
    wide = jnp.broadcast_to(taps, (size, LANES))
    inner = pltpu.roll(wide, LANES - HW, 1, stride=1, stride_axis=0)
    before = pltpu.roll(wide, size + HW, 1, stride=1, stride_axis=0)
    lane = lax.broadcasted_iota(jnp.int32, (size, LANES), 1)
    return jnp.where(lane < size + HW, inner, jnp.where(lane < size + 2 * HW, before, 0.0))


def far_products(place_ref, even_ref, other_ref, weights, slab_ref, along_ref):
    depth = slab_ref.shape[0] // (2 * HW)
    tile_rows = slab_ref.shape[1] // 2
    count = tile_rows // (2 * HW)
    owner = lax.broadcasted_iota(jnp.int32, (2 * HW, tile_rows), 1) // (2 * HW)
    for z in range(depth):
        at = pl.ds(z * 2 * HW, 2 * HW)
        slab_ref[at, :tile_rows] = halo(place_ref, even_ref[z], other_ref[z])
        corners = halo(place_ref, even_ref[depth + z // count], other_ref[depth + z // count])
        slab_ref[at, tile_rows:] = jnp.where(owner == z % count, corners.astype(F32), 0.0).astype(BF16)
    for turned_ref, out_ref in zip(weights, along_ref):
        for b in range(turned_ref.shape[0]):
            along = dot(slab_ref[...], turned_ref[b])
            high, low = split(along[:, :tile_rows] + along[:, tile_rows:])
            out_ref[b, 0] = high
            out_ref[b, 1] = low


def far_parts(along_ref, view, b, z):
    at = pl.ds(z * 2 * HW, 2 * HW)
    high, low = along_ref[view, b, 0, at, :], along_ref[view, b, 1, at, :]
    return [high, low, high]


def forward_kernel(
    band_ref, place_ref, taps_ref, cells_ref, even_ref, other_ref,
    blurred_ref, fwd_turned_ref, fwd_far_ref, rows_ref, ends_ref, cols_ref, turned_ref, far_ref, fwd_rows, fwd_cols,
):
    views, depth, tile_rows, tile_cols = blurred_ref.shape
    bands = taps_ref.shape[2]
    for b in range(bands):
        ends = jnp.zeros((tile_rows, LANES - tile_rows), F32)
        for view in range(views):
            for way in range(2):
                along = band(taps_ref[way, view, b, 0:1, :], tile_rows)
                across = band(taps_ref[way, view, b, 1:2, :], tile_cols)
                beyond = along[:, tile_rows:]
                turned, far = ((fwd_turned_ref, fwd_far_ref), (turned_ref, far_ref))[way]
                turned[view, b, :tile_rows] = stacked(along[:, :tile_rows].T, 1)
                corner = stacked(beyond.T[: 2 * HW], 1)
                for at in range(tile_rows, 2 * tile_rows, 2 * HW):
                    turned[view, b, at : at + 2 * HW] = corner
                high, low = split(across[:, tile_cols:].T[: 2 * HW])
                far[b, view] = jnp.concatenate([high, high, low], axis=0)
                inner = stacked(across[:, :tile_cols].T, 1)
                if way == 0:
                    fwd_rows[view, b] = stacked(along[:, : tile_rows + 2 * HW], 0)
                    fwd_cols[view, b] = inner
                else:
                    rows_ref[b, :, view * tile_rows : (view + 1) * tile_rows] = stacked(along[:, :tile_rows], 0)
                    ends = ends + (pltpu.roll(beyond, 2 * HW * view, 1) if view else beyond)
                    cols_ref[view, b] = inner
        ends = jnp.concatenate([ends[:HW], ends[tile_rows - HW :]], axis=0)
        ends_ref[b] = stacked(ends[:, : 2 * HW * views], 0)

    def plane(z, carry):
        b = band_ref[z]
        cells = stacked(cells_ref[z], 1)
        ends = halo(place_ref, even_ref[z], other_ref[z])
        for view in range(views):
            rows = fwd_rows[view, b]
            blurred = quarters(dot(rows[:, :tile_rows], cells)) + halves(dot(rows[:, tile_rows:], ends))
            blurred = quarters(dot(stacked(blurred, 0), fwd_cols[view, b]))
            blurred_ref[view, z] = blurred
        return carry

    lax.fori_loop(0, depth, plane, 0, unroll=2)


def recip_kernel(
    band_ref, place_ref, turned_ref, far_ref, even_ref, other_ref, blurred_ref, out_ref, edge_ref, slab_ref, along_ref
):
    views, depth, tile_rows, tile_cols = blurred_ref.shape
    weights = [turned_ref.at[view] for view in range(views)]
    far_products(place_ref, even_ref.at[0], other_ref.at[0], weights, slab_ref, [along_ref.at[v] for v in range(views)])
    for view in range(views):
        for z in range(depth):
            b = band_ref[z]
            along = jnp.concatenate(far_parts(along_ref, view, b, z), axis=0)
            blurred = blurred_ref[view, z] + dot(along, far_ref[b, view], ((0,), (0,)))
            recip = 1.0 / blurred.astype(BF16).astype(F32)
            out_ref[view, z] = recip
            edge_ref[view, z, :HW] = recip[:HW]
            edge_ref[view, z, HW:] = recip[tile_rows - HW :]


def near_kernel(
    band_ref, place_ref, rows_ref, ends_ref, cols_ref, ratio_ref, even_ref, other_ref, out_ref, inner_ref, outer_ref
):
    views, depth, tile_rows, tile_cols = ratio_ref.shape

    def across(cells, weights):
        blurred = dot(cells, weights)
        return stacked(blurred[:, :tile_cols] + blurred[:, tile_cols:], 1)

    for z in range(depth):
        b = band_ref[z]
        for view in range(views):
            inner_ref[z, view * tile_rows : (view + 1) * tile_rows] = across(ratio_ref[view, z], cols_ref[view, b])
            ends = halo(place_ref, even_ref[view, z], other_ref[view, z])
            outer_ref[z, view * 2 * HW : (view + 1) * 2 * HW] = across(ends, cols_ref[view, b])
    for z in range(depth):
        b = band_ref[z]
        out_ref[z] = quarters(dot(rows_ref[b], inner_ref[z]))
        ends = quarters(dot(ends_ref[b], outer_ref[z]))
        out_ref[z, :HW] += ends[:HW]
        out_ref[z, tile_rows - HW :] += ends[HW:]


def half_products(place_ref, turned_ref, far_ref, cells_ref, ring_odd, slab_ref, along_ref, across_ref):
    views, bands = turned_ref.shape[:2]
    tile_rows = along_ref.shape[-1]
    depth = tile_rows // HW
    count = tile_rows // (2 * HW)
    odd = is_odd(place_ref)
    follows = odd if ring_odd else jnp.logical_not(odd)
    end = jnp.logical_or(place_ref[0] == 0, place_ref[0] >= LAST)
    owner = lax.broadcasted_iota(jnp.int32, (HW, tile_rows), 1) // (2 * HW)

    def cells(view, i):
        x = cells_ref[view, i].astype(F32)
        return jnp.where(end, 0.0, x) if ring_odd else x

    for view in range(views):
        for z in range(0, depth, 2):
            at = pl.ds(z * HW, 2 * HW)
            both = (z, z + 1)
            slab_ref[view, at, :tile_rows] = jnp.concatenate([cells(view, i) for i in both], axis=0).astype(BF16)
            corners = [jnp.where(owner == i % count, cells(view, depth + i // count), 0.0) for i in both]
            slab_ref[view, at, tile_rows:] = jnp.concatenate(corners, axis=0).astype(BF16)
    for b in range(bands):
        across = []
        for view in range(views):
            along = dot(slab_ref[view], turned_ref[view, b])
            along_ref[view, b] = along[:, :tile_rows] + along[:, tile_rows:]
            weights = far_ref[b, view].astype(F32)
            high = jnp.where(follows, weights[:HW], weights[HW : 2 * HW])
            low = jnp.where(follows, weights[4 * HW : 5 * HW], weights[5 * HW :])
            across += [high, high, low]
        across_ref[b] = jnp.concatenate(across, axis=0).astype(BF16)


def half_part(along_ref, across_ref, b, z):
    parts = []
    for view in range(along_ref.shape[0]):
        along = along_ref[view, b, z * HW : (z + 1) * HW, :]
        high = along.astype(BF16).astype(F32)
        parts += [high, along - high, high]
    return dot(jnp.concatenate(parts, axis=0).astype(BF16), across_ref[b], ((0,), (0,)))


def even_far_kernel(
    band_ref, place_ref, turned_ref, far_ref, near_ref, cells_ref, out_ref, slab_ref, along_ref, across_ref
):
    half_products(place_ref, turned_ref, far_ref, cells_ref, False, slab_ref, along_ref, across_ref)
    for z in range(near_ref.shape[0]):
        out_ref[z] = near_ref[z] + half_part(along_ref, across_ref, band_ref[z], z)


def odd_far_kernel(
    band_ref, place_ref, turned_ref, far_ref, near_ref, cells_ref, estimate_ref, out_hbm,
    slab_ref, along_ref, across_ref, out_ref, sems,
):
    views = turned_ref.shape[0]
    depth = near_ref.shape[0]
    step = depth // sems.shape[0]
    half_products(place_ref, turned_ref, far_ref, cells_ref, True, slab_ref, along_ref, across_ref)
    leave = []
    for z in range(depth):
        total = near_ref[z] + half_part(along_ref, across_ref, band_ref[z], z)
        out_ref[z] = estimate_ref[z] * (total * (1.0 / views))
        if z % step == step - 1:
            part = pl.ds(z - step + 1, step)
            leave.append(pltpu.make_async_copy(out_ref.at[part], out_hbm.at[part], sems.at[z // step]))
            leave[-1].start()
    for copy in leave:
        copy.wait()


def swap(first, second, axis, ring=True):
    count = lax.axis_size(axis)
    chain = lambda begin: range(begin, count if ring else count - 1, 2)
    pairs = lambda begin: [p for i in chain(begin) for p in ((i, (i + 1) % count), ((i + 1) % count, i))]
    late = lax.ppermute(second, axis, pairs(1))
    return lax.ppermute(first, axis, pairs(0)), late


def place(count, at):
    return jnp.where(at == count - 1, at + LAST, at).reshape(1)


def body(estimate, measured, kernels, depth_band, group_shift, group_length):
    devices = lax.axis_size("gx") * lax.axis_size("gy")
    gx, gy = lax.axis_index("gx").astype(jnp.int32), lax.axis_index("gy").astype(jnp.int32)
    me = (gx * lax.axis_size("gy") + gy).reshape(1)
    place_x, place_y = (place(lax.axis_size(axis), at) for axis, at in (("gx", gx), ("gy", gy)))
    views, depth, tile_rows, tile_cols = measured.shape
    bands = kernels.shape[1]
    spare = tile_rows + 8
    like = jax.ShapeDtypeStruct
    whole = like(measured.shape, BF16)
    edge_cols = like((views, depth, 2 * HW, tile_rows), BF16)
    edge_rows = like((views, depth, HW, tile_cols), BF16)

    head, tail = estimate[:, :HW], estimate[:, tile_rows - HW :]
    even = gx % 2 == 0
    ex, ox = swap(jnp.where(even, tail, head), jnp.where(even, head, tail), "gx")
    outgoing = call(
        functools.partial(pack_kernel, devices),
        [SMEM, HBM, HBM, HBM],
        like((devices, views, CAP, depth, tile_cols), BF16),
        [
            pltpu.VMEM((views, spare, depth, tile_cols), BF16),
            pltpu.VMEM(measured.shape, BF16),
            pltpu.SMEM(group_shift.shape, jnp.int32),
            pltpu.SMEM(group_length.shape, jnp.int32),
            pltpu.SemaphoreType.DMA((2 * views + 2,)),
        ],
        HBM,
        60,
    )(me, group_shift, group_length, measured)
    outgoing = outgoing.reshape(devices * views * CAP, depth, tile_cols)
    outgoing, ex, ox, cells = lax.optimization_barrier((outgoing, ex, ox, estimate))
    arrived = lax.all_to_all(outgoing, ("gx", "gy"), split_axis=0, concat_axis=0, tiled=True)

    cols = call(cols_kernel, [VMEM], like(edge_cols.shape[1:], BF16))(cells)
    tiles = depth + depth * 2 * HW // tile_rows
    dense = lambda lead, *args: call(
        dense_slab_kernel, [SMEM] * 2 + [VMEM] * 3, (like((lead, tiles, HW, tile_rows), BF16),) * 2
    )(place_x, place_y, *args)
    ey, oy = swap(*dense(1, cols[None], ex, ox), "gy", ring=False)

    norm = kernels / jnp.sum(kernels, axis=3, keepdims=True)
    tap_rows = jnp.stack([norm, norm[..., ::-1]])
    tap_rows = jnp.pad(tap_rows, ((0, 0),) * 4 + ((0, LANES - kernels.shape[3]),))
    turned_like = like((views, bands, 2 * tile_rows, 2 * tile_rows), BF16)
    far_like = like((bands, views, 6 * HW, tile_cols), BF16)
    blurred, fwd_turned, fwd_far, rows_mat, ends_mat, cols_mat, turned_mat, far_mat = call(
        forward_kernel,
        [SMEM] * 2 + [VMEM] * 4,
        (
            like(measured.shape, F32),
            turned_like,
            far_like,
            like((bands, 2 * tile_rows, views * tile_rows), BF16),
            like((bands, 4 * HW, views * 2 * HW), BF16),
            like((views, bands, tile_cols, 2 * tile_cols), BF16),
            turned_like,
            far_like,
        ),
        [
            pltpu.VMEM((views, bands, 2 * tile_rows, tile_rows + 2 * HW), BF16),
            pltpu.VMEM((views, bands, tile_cols, 2 * tile_cols), BF16),
        ],
    )(depth_band, place_x, tap_rows, cells, ex, ox)

    recip, edge_recip = call(
        recip_kernel,
        [SMEM] * 2 + [VMEM] * 5,
        (like(measured.shape, F32), like((views, depth, 2 * HW, tile_cols), F32)),
        [
            pltpu.VMEM((depth * 2 * HW, 2 * tile_rows), BF16),
            pltpu.VMEM((views, bands, 2, depth * 2 * HW, tile_rows), BF16),
        ],
    )(depth_band, place_y, fwd_turned, fwd_far, ey, oy, blurred)

    first, second = call(
        functools.partial(edges_kernel, devices, tile_rows),
        [SMEM] * 4 + [VMEM] * 2,
        (edge_rows, edge_rows),
        [pltpu.VMEM((views, 2, CAP * HW + 8, depth, tile_cols), F32)],
    )(me, place_x, group_shift, group_length, arrived, edge_recip)
    ex, ox = swap(first, second, "gx")
    ratio, cols = call(
        functools.partial(unpack_kernel, devices),
        [SMEM] * 3 + [VMEM] * 2,
        (whole, edge_cols),
        [pltpu.VMEM((views, spare, depth, tile_cols), F32)],
    )(me, group_shift, group_length, arrived, recip)
    ey, oy = swap(*dense(views, cols, ex, ox), "gy")
    near = call(
        near_kernel,
        [SMEM] * 2 + [VMEM] * 6,
        like(estimate.shape, F32),
        [
            pltpu.VMEM((depth, views * tile_rows, 2 * tile_cols), BF16),
            pltpu.VMEM((depth, views * 2 * HW, 2 * tile_cols), BF16),
        ],
    )(depth_band, place_x, rows_mat, ends_mat, cols_mat, ratio, ex, ox)
    halves = [
        pltpu.VMEM((views, depth * HW, 2 * tile_rows), BF16),
        pltpu.VMEM((views, bands, depth * HW, tile_rows), F32),
        pltpu.VMEM((bands, views * 3 * HW, tile_cols), BF16),
    ]
    near = call(
        even_far_kernel, [SMEM] * 2 + [VMEM] * 4, like(estimate.shape, F32), halves
    )(depth_band, place_y, turned_mat, far_mat, near, ey)
    return call(
        odd_far_kernel,
        [SMEM] * 2 + [VMEM] * 5,
        like(estimate.shape, F32),
        halves + [pltpu.VMEM(estimate.shape, F32), pltpu.SemaphoreType.DMA((4,))],
        HBM,
    )(depth_band, place_y, turned_mat, far_mat, near, oy, estimate)


def solution(mesh):
    return jax.shard_map(
        body,
        mesh=mesh,
        in_specs=(P(None, "gx", "gy"), P(None, None, "gx", "gy"), P(), P(), P(), P()),
        out_specs=P(None, "gx", "gy"),
        check_vma=False,
    )
```

```python
import functools

import jax
import jax.numpy as jnp
from jax import lax
from jax.experimental import pallas as pl
from jax.experimental.pallas import tpu as pltpu
from jax.sharding import PartitionSpec as P

HW = 8
CAP = 3
LANES = 256
LAST = 2**20
F32 = jnp.float32
BF16 = jnp.bfloat16

VMEM = pl.BlockSpec(memory_space=pltpu.VMEM)
SMEM = pl.BlockSpec(memory_space=pltpu.SMEM)
HBM = pl.BlockSpec(memory_space=pltpu.HBM)
NN = ((1,), (0,))
NT = ((1,), (1,))


def call(kernel, ins, out_shape, scratch=(), out_space=VMEM, limit=16):
    return pl.pallas_call(
        kernel,
        in_specs=ins,
        out_specs=jax.tree.map(lambda _: out_space, out_shape),
        out_shape=out_shape,
        scratch_shapes=list(scratch),
        compiler_params=pltpu.CompilerParams(vmem_limit_bytes=limit * 2**20),
    )


def dot(a, b, dims=NN):
    return lax.dot_general(a, b, (dims, ((), ())), preferred_element_type=F32)


def split(x):
    high = x.astype(BF16)
    return high, (x - high.astype(F32)).astype(BF16)


def stacked(x, axis):
    return jnp.concatenate(split(x), axis=axis)


def halves(x):
    n = x.shape[0] // 2
    return x[:n] + x[n:]


def quarters(x):
    n, m = x.shape[0] // 2, x.shape[1] // 2
    return x[:n, :m] + (x[n:, :m] + x[:n, m:])


def is_odd(place_ref):
    return place_ref[0] % 2 == 1


def halo(place_ref, first, second):
    first, second = first.astype(F32), second.astype(F32)
    odd = is_odd(place_ref)
    after = jnp.where(place_ref[0] >= LAST, 0.0, jnp.where(odd, second, first))
    before = jnp.where(place_ref[0] == 0, 0.0, jnp.where(odd, first, second))
    return jnp.concatenate([after, before], axis=0).astype(BF16)


def edge_picker(cols):
    lane = lax.broadcasted_iota(jnp.int32, (2 * HW, cols), 1)
    sub = lax.broadcasted_iota(jnp.int32, (2 * HW, cols), 0)
    return (lane == jnp.where(sub < HW, sub, sub + cols - 2 * HW)).astype(BF16)


def pack_kernel(
    devices, me_ref, shift_hbm, length_hbm, measured_hbm, out_hbm,
    rows_ref, measured_ref, shift_ref, length_ref, sems,
):
    views, depth, tile_rows, tile_cols = measured_ref.shape
    groups = shift_ref.shape[1]
    loads = [pltpu.make_async_copy(measured_hbm.at[v], measured_ref.at[v], sems.at[v]) for v in range(views)]
    tables = [
        pltpu.make_async_copy(shift_hbm, shift_ref, sems.at[views]),
        pltpu.make_async_copy(length_hbm, length_ref, sems.at[views + 1]),
    ]
    for copy in tables + loads:
        copy.start()
    rows_ref[:, tile_rows:] = jnp.zeros((views, rows_ref.shape[1] - tile_rows) + rows_ref.shape[2:], BF16)
    lane = lax.broadcasted_iota(jnp.int32, (tile_cols, tile_cols), 1)
    sub = lax.broadcasted_iota(jnp.int32, (tile_cols, tile_cols), 0)
    turn = (lane + sub == tile_cols - 1).astype(BF16)
    me = me_ref[0]
    for view in range(views):
        loads[view].wait()
        for r0 in range(0, tile_rows, 16):
            x = measured_ref[view, :, r0 : r0 + 16, :]
            if view % 2 == 1:
                x = dot(x.reshape(depth * 16, tile_cols), turn).reshape(depth, 16, tile_cols)
            x = jnp.transpose(x.astype(F32), (1, 0, 2))
            rows_ref[view, r0 : r0 + 16] = x.astype(BF16)
        if view == 0:
            for copy in tables:
                copy.wait()

        def group(g, start, view=view):
            peer = lax.rem(me + shift_ref[view, g], devices)
            blocks = rows_ref.at[view, pl.ds(start, CAP)]
            pltpu.make_async_copy(blocks, out_hbm.at[peer, view], sems.at[views + 2 + view]).start()
            return start + length_ref[view, g]

        lax.fori_loop(0, groups, group, 0, unroll=True)
    for view in range(views):
        sent = out_hbm.at[pl.ds(0, groups), view]
        pltpu.make_async_copy(sent, sent, sems.at[views + 2 + view]).wait()


def cols_kernel(cells_ref, out_ref):
    pick = edge_picker(cells_ref.shape[-1])
    for z in range(cells_ref.shape[0]):
        out_ref[z] = dot(pick, cells_ref[z].astype(BF16), NT).astype(BF16)


def dense_slab_kernel(place_x_ref, place_y_ref, cols_ref, even_ref, other_ref, first_ref, second_ref):
    views, depth, _, tile_rows = cols_ref.shape
    count = tile_rows // (2 * HW)
    pick = edge_picker(even_ref.shape[-1])
    odd = is_odd(place_y_ref)
    for view in range(views):
        for i in range(first_ref.shape[1]):
            if i < depth:
                edge = cols_ref[view, i].astype(F32)
            else:
                planes = range((i - depth) * count, (i - depth + 1) * count)
                lead = () if len(even_ref.shape) == 3 else (view,)
                ends = [halo(place_x_ref, even_ref[*lead, z], other_ref[*lead, z]) for z in planes]
                edge = dot(pick, jnp.concatenate(ends, axis=0), NT)
            first_ref[view, i] = jnp.where(odd, edge[:HW], edge[HW:]).astype(BF16)
            second_ref[view, i] = jnp.where(odd, edge[HW:], edge[:HW]).astype(BF16)


def edges_kernel(
    devices, tile_rows, me_ref, place_ref, shift_ref, length_ref, arrived_ref, recip_ref, first_ref, second_ref, rows_ref
):
    views = recip_ref.shape[0]
    odd = is_odd(place_ref)
    groups = shift_ref.shape[1]
    me = me_ref[0]
    low = tile_rows - CAP * HW
    for view in range(views):
        ending = tile_rows - low
        for g in range(groups - HW, groups):
            ending = ending - length_ref[view, g]
        for side, (first, start) in enumerate(((0, 0), (groups - HW, ending))):
            for g in range(first, first + HW):
                source = lax.rem(me - shift_ref[view, g] + devices, devices)
                base = source * (views * CAP) + view * CAP
                for k in range(CAP):
                    rows_ref[view, side, start + k] = arrived_ref[base + k].astype(F32)
                start = start + length_ref[view, g]
        head = jnp.transpose(rows_ref[view, 0, :HW], (1, 0, 2)) * recip_ref[view, :, :HW]
        tail = rows_ref[view, 1, (CAP - 1) * HW : CAP * HW]
        tail = jnp.transpose(tail, (1, 0, 2)) * recip_ref[view, :, HW:]
        first_ref[view] = jnp.where(odd, head, tail).astype(BF16)
        second_ref[view] = jnp.where(odd, tail, head).astype(BF16)


def unpack_kernel(devices, me_ref, shift_ref, length_ref, arrived_ref, recip_ref, out_ref, cols_ref, rows_ref):
    views, depth, tile_rows, tile_cols = out_ref.shape
    groups = shift_ref.shape[1]
    me = me_ref[0]
    pick = edge_picker(tile_cols)
    for view in range(views):

        def group(g, start, view=view):
            source = lax.rem(me - shift_ref[view, g] + devices, devices)
            base = source * (views * CAP) + view * CAP
            for k in range(CAP):
                rows_ref[view, start + k] = arrived_ref[base + k].astype(F32)
            return start + length_ref[view, g]

        lax.fori_loop(0, groups, group, 0, unroll=True)
        for r0 in range(0, tile_rows, 16):
            x = jnp.transpose(rows_ref[view, r0 : r0 + 16], (1, 0, 2))
            out_ref[view, :, r0 : r0 + 16, :] = (x * recip_ref[view, :, r0 : r0 + 16, :]).astype(BF16)
        for z in range(depth):
            cols_ref[view, z] = dot(pick, out_ref[view, z], NT).astype(BF16)


def band(taps, size):
    wide = jnp.broadcast_to(taps, (size, LANES))
    inner = pltpu.roll(wide, LANES - HW, 1, stride=1, stride_axis=0)
    before = pltpu.roll(wide, size + HW, 1, stride=1, stride_axis=0)
    lane = lax.broadcasted_iota(jnp.int32, (size, LANES), 1)
    return jnp.where(lane < size + HW, inner, jnp.where(lane < size + 2 * HW, before, 0.0))


def far_products(place_ref, even_ref, other_ref, weights, slab_ref, along_ref):
    depth = slab_ref.shape[0] // (2 * HW)
    tile_rows = slab_ref.shape[1] // 2
    count = tile_rows // (2 * HW)
    owner = lax.broadcasted_iota(jnp.int32, (2 * HW, tile_rows), 1) // (2 * HW)
    for z in range(depth):
        at = pl.ds(z * 2 * HW, 2 * HW)
        slab_ref[at, :tile_rows] = halo(place_ref, even_ref[z], other_ref[z])
        corners = halo(place_ref, even_ref[depth + z // count], other_ref[depth + z // count])
        slab_ref[at, tile_rows:] = jnp.where(owner == z % count, corners.astype(F32), 0.0).astype(BF16)
    for turned_ref, out_ref in zip(weights, along_ref):
        for b in range(turned_ref.shape[0]):
            along = dot(slab_ref[...], turned_ref[b])
            high, low = split(along[:, :tile_rows] + along[:, tile_rows:])
            out_ref[b, 0] = high
            out_ref[b, 1] = low


def far_parts(along_ref, view, b, z):
    at = pl.ds(z * 2 * HW, 2 * HW)
    high, low = along_ref[view, b, 0, at, :], along_ref[view, b, 1, at, :]
    return [high, low, high]


def forward_kernel(
    band_ref, place_ref, taps_ref, cells_ref, even_ref, other_ref,
    blurred_ref, fwd_turned_ref, fwd_far_ref, rows_ref, ends_ref, cols_ref, turned_ref, far_ref, fwd_rows, fwd_cols,
):
    views, depth, tile_rows, tile_cols = blurred_ref.shape
    bands = taps_ref.shape[2]
    for b in range(bands):
        ends = jnp.zeros((tile_rows, LANES - tile_rows), F32)
        for view in range(views):
            for way in range(2):
                along = band(taps_ref[way, view, b, 0:1, :], tile_rows)
                across = band(taps_ref[way, view, b, 1:2, :], tile_cols)
                beyond = along[:, tile_rows:]
                turned, far = ((fwd_turned_ref, fwd_far_ref), (turned_ref, far_ref))[way]
                turned[view, b, :tile_rows] = stacked(along[:, :tile_rows].T, 1)
                corner = stacked(beyond.T[: 2 * HW], 1)
                for at in range(tile_rows, 2 * tile_rows, 2 * HW):
                    turned[view, b, at : at + 2 * HW] = corner
                high, low = split(across[:, tile_cols:].T[: 2 * HW])
                far[b, view] = jnp.concatenate([high, high, low], axis=0)
                inner = stacked(across[:, :tile_cols].T, 1)
                if way == 0:
                    fwd_rows[view, b] = stacked(along[:, : tile_rows + 2 * HW], 0)
                    fwd_cols[view, b] = inner
                else:
                    rows_ref[b, :, view * tile_rows : (view + 1) * tile_rows] = stacked(along[:, :tile_rows], 0)
                    ends = ends + (pltpu.roll(beyond, 2 * HW * view, 1) if view else beyond)
                    cols_ref[view, b] = inner
        ends = jnp.concatenate([ends[:HW], ends[tile_rows - HW :]], axis=0)
        ends_ref[b] = stacked(ends[:, : 2 * HW * views], 0)

    def plane(z, carry):
        b = band_ref[z]
        cells = stacked(cells_ref[z], 1)
        ends = halo(place_ref, even_ref[z], other_ref[z])
        for view in range(views):
            rows = fwd_rows[view, b]
            blurred = quarters(dot(rows[:, :tile_rows], cells)) + halves(dot(rows[:, tile_rows:], ends))
            blurred = quarters(dot(stacked(blurred, 0), fwd_cols[view, b]))
            blurred_ref[view, z] = blurred
        return carry

    lax.fori_loop(0, depth, plane, 0, unroll=2)


def recip_kernel(
    band_ref, place_ref, turned_ref, far_ref, even_ref, other_ref, blurred_ref, out_ref, edge_ref, slab_ref, along_ref
):
    views, depth, tile_rows, tile_cols = blurred_ref.shape
    weights = [turned_ref.at[view] for view in range(views)]
    far_products(place_ref, even_ref.at[0], other_ref.at[0], weights, slab_ref, [along_ref.at[v] for v in range(views)])
    for view in range(views):
        for z in range(depth):
            b = band_ref[z]
            along = jnp.concatenate(far_parts(along_ref, view, b, z), axis=0)
            blurred = blurred_ref[view, z] + dot(along, far_ref[b, view], ((0,), (0,)))
            recip = 1.0 / blurred.astype(BF16).astype(F32)
            out_ref[view, z] = recip
            edge_ref[view, z, :HW] = recip[:HW]
            edge_ref[view, z, HW:] = recip[tile_rows - HW :]


def near_kernel(
    band_ref, place_ref, rows_ref, ends_ref, cols_ref, ratio_ref, even_ref, other_ref, out_ref, inner_ref, outer_ref
):
    views, depth, tile_rows, tile_cols = ratio_ref.shape

    def across(cells, weights):
        blurred = dot(cells, weights)
        return stacked(blurred[:, :tile_cols] + blurred[:, tile_cols:], 1)

    for z in range(depth):
        b = band_ref[z]
        for view in range(views):
            inner_ref[z, view * tile_rows : (view + 1) * tile_rows] = across(ratio_ref[view, z], cols_ref[view, b])
            ends = halo(place_ref, even_ref[view, z], other_ref[view, z])
            outer_ref[z, view * 2 * HW : (view + 1) * 2 * HW] = across(ends, cols_ref[view, b])
    for z in range(depth):
        b = band_ref[z]
        out_ref[z] = quarters(dot(rows_ref[b], inner_ref[z]))
        ends = quarters(dot(ends_ref[b], outer_ref[z]))
        out_ref[z, :HW] += ends[:HW]
        out_ref[z, tile_rows - HW :] += ends[HW:]


def half_products(place_ref, turned_ref, far_ref, cells_ref, ring_odd, slab_ref, along_ref, across_ref):
    views, bands = turned_ref.shape[:2]
    tile_rows = along_ref.shape[-1]
    depth = tile_rows // HW
    count = tile_rows // (2 * HW)
    odd = is_odd(place_ref)
    follows = odd if ring_odd else jnp.logical_not(odd)
    end = jnp.logical_or(place_ref[0] == 0, place_ref[0] >= LAST)
    owner = lax.broadcasted_iota(jnp.int32, (HW, tile_rows), 1) // (2 * HW)

    def cells(view, i):
        x = cells_ref[view, i].astype(F32)
        return jnp.where(end, 0.0, x) if ring_odd else x

    for view in range(views):
        for z in range(0, depth, 2):
            at = pl.ds(z * HW, 2 * HW)
            both = (z, z + 1)
            slab_ref[view, at, :tile_rows] = jnp.concatenate([cells(view, i) for i in both], axis=0).astype(BF16)
            corners = [jnp.where(owner == i % count, cells(view, depth + i // count), 0.0) for i in both]
            slab_ref[view, at, tile_rows:] = jnp.concatenate(corners, axis=0).astype(BF16)
    for b in range(bands):
        across = []
        for view in range(views):
            along = dot(slab_ref[view], turned_ref[view, b])
            along_ref[view, b] = along[:, :tile_rows] + along[:, tile_rows:]
            weights = far_ref[b, view].astype(F32)
            high = jnp.where(follows, weights[:HW], weights[HW : 2 * HW])
            low = jnp.where(follows, weights[4 * HW : 5 * HW], weights[5 * HW :])
            across += [high, high, low]
        across_ref[b] = jnp.concatenate(across, axis=0).astype(BF16)


def half_part(along_ref, across_ref, b, z):
    parts = []
    for view in range(along_ref.shape[0]):
        along = along_ref[view, b, z * HW : (z + 1) * HW, :]
        high = along.astype(BF16).astype(F32)
        parts += [high, along - high, high]
    return dot(jnp.concatenate(parts, axis=0).astype(BF16), across_ref[b], ((0,), (0,)))


def even_far_kernel(
    band_ref, place_ref, turned_ref, far_ref, near_ref, cells_ref, out_ref, slab_ref, along_ref, across_ref
):
    half_products(place_ref, turned_ref, far_ref, cells_ref, False, slab_ref, along_ref, across_ref)
    for z in range(near_ref.shape[0]):
        out_ref[z] = near_ref[z] + half_part(along_ref, across_ref, band_ref[z], z)


def odd_far_kernel(
    band_ref, place_ref, turned_ref, far_ref, near_ref, cells_ref, estimate_ref, out_hbm,
    slab_ref, along_ref, across_ref, out_ref, sems,
):
    views = turned_ref.shape[0]
    depth = near_ref.shape[0]
    step = depth // sems.shape[0]
    half_products(place_ref, turned_ref, far_ref, cells_ref, True, slab_ref, along_ref, across_ref)
    leave = []
    for z in range(depth):
        total = near_ref[z] + half_part(along_ref, across_ref, band_ref[z], z)
        out_ref[z] = estimate_ref[z] * (total * (1.0 / views))
        if z % step == step - 1:
            part = pl.ds(z - step + 1, step)
            leave.append(pltpu.make_async_copy(out_ref.at[part], out_hbm.at[part], sems.at[z // step]))
            leave[-1].start()
    for copy in leave:
        copy.wait()


def swap(first, second, axis, everyone=True):
    count = lax.axis_size(axis)
    ends = lambda begin: [(0, 0), (count - 1, count - 1)] if begin and everyone else []
    pairs = lambda begin: ends(begin) + [p for i in range(begin, count - 1, 2) for p in ((i, i + 1), (i + 1, i))]
    late = lax.ppermute(second, axis, pairs(1))
    return lax.ppermute(first, axis, pairs(0)), late


def place(count, at):
    return jnp.where(at == count - 1, at + LAST, at).reshape(1)


def body(estimate, measured, kernels, depth_band, group_shift, group_length):
    devices = lax.axis_size("gx") * lax.axis_size("gy")
    gx, gy = lax.axis_index("gx").astype(jnp.int32), lax.axis_index("gy").astype(jnp.int32)
    me = (gx * lax.axis_size("gy") + gy).reshape(1)
    place_x, place_y = (place(lax.axis_size(axis), at) for axis, at in (("gx", gx), ("gy", gy)))
    views, depth, tile_rows, tile_cols = measured.shape
    bands = kernels.shape[1]
    spare = tile_rows + 8
    like = jax.ShapeDtypeStruct
    whole = like(measured.shape, BF16)
    edge_cols = like((views, depth, 2 * HW, tile_rows), BF16)
    edge_rows = like((views, depth, HW, tile_cols), BF16)

    head, tail = estimate[:, :HW], estimate[:, tile_rows - HW :]
    even = gx % 2 == 0
    ex, ox = swap(jnp.where(even, tail, head), jnp.where(even, head, tail), "gx")
    outgoing = call(
        functools.partial(pack_kernel, devices),
        [SMEM, HBM, HBM, HBM],
        like((devices, views, CAP, depth, tile_cols), BF16),
        [
            pltpu.VMEM((views, spare, depth, tile_cols), BF16),
            pltpu.VMEM(measured.shape, BF16),
            pltpu.SMEM(group_shift.shape, jnp.int32),
            pltpu.SMEM(group_length.shape, jnp.int32),
            pltpu.SemaphoreType.DMA((2 * views + 2,)),
        ],
        HBM,
        60,
    )(me, group_shift, group_length, measured)
    outgoing = outgoing.reshape(devices * views * CAP, depth, tile_cols)
    outgoing, ex, ox, cells = lax.optimization_barrier((outgoing, ex, ox, estimate))
    arrived = lax.all_to_all(outgoing, ("gx", "gy"), split_axis=0, concat_axis=0, tiled=True)

    cols = call(cols_kernel, [VMEM], like(edge_cols.shape[1:], BF16))(cells)
    tiles = depth + depth * 2 * HW // tile_rows
    dense = lambda lead, *args: call(
        dense_slab_kernel, [SMEM] * 2 + [VMEM] * 3, (like((lead, tiles, HW, tile_rows), BF16),) * 2
    )(place_x, place_y, *args)
    ey, oy = swap(*dense(1, cols[None], ex, ox), "gy", everyone=False)

    norm = kernels / jnp.sum(kernels, axis=3, keepdims=True)
    tap_rows = jnp.stack([norm, norm[..., ::-1]])
    tap_rows = jnp.pad(tap_rows, ((0, 0),) * 4 + ((0, LANES - kernels.shape[3]),))
    turned_like = like((views, bands, 2 * tile_rows, 2 * tile_rows), BF16)
    far_like = like((bands, views, 6 * HW, tile_cols), BF16)
    blurred, fwd_turned, fwd_far, rows_mat, ends_mat, cols_mat, turned_mat, far_mat = call(
        forward_kernel,
        [SMEM] * 2 + [VMEM] * 4,
        (
            like(measured.shape, F32),
            turned_like,
            far_like,
            like((bands, 2 * tile_rows, views * tile_rows), BF16),
            like((bands, 4 * HW, views * 2 * HW), BF16),
            like((views, bands, tile_cols, 2 * tile_cols), BF16),
            turned_like,
            far_like,
        ),
        [
            pltpu.VMEM((views, bands, 2 * tile_rows, tile_rows + 2 * HW), BF16),
            pltpu.VMEM((views, bands, tile_cols, 2 * tile_cols), BF16),
        ],
    )(depth_band, place_x, tap_rows, cells, ex, ox)

    recip, edge_recip = call(
        recip_kernel,
        [SMEM] * 2 + [VMEM] * 5,
        (like(measured.shape, F32), like((views, depth, 2 * HW, tile_cols), F32)),
        [
            pltpu.VMEM((depth * 2 * HW, 2 * tile_rows), BF16),
            pltpu.VMEM((views, bands, 2, depth * 2 * HW, tile_rows), BF16),
        ],
    )(depth_band, place_y, fwd_turned, fwd_far, ey, oy, blurred)

    first, second = call(
        functools.partial(edges_kernel, devices, tile_rows),
        [SMEM] * 4 + [VMEM] * 2,
        (edge_rows, edge_rows),
        [pltpu.VMEM((views, 2, CAP * HW + 8, depth, tile_cols), F32)],
    )(me, place_x, group_shift, group_length, arrived, edge_recip)
    ex, ox = swap(first, second, "gx")
    ratio, cols = call(
        functools.partial(unpack_kernel, devices),
        [SMEM] * 3 + [VMEM] * 2,
        (whole, edge_cols),
        [pltpu.VMEM((views, spare, depth, tile_cols), F32)],
    )(me, group_shift, group_length, arrived, recip)
    ey, oy = swap(*dense(views, cols, ex, ox), "gy")
    near = call(
        near_kernel,
        [SMEM] * 2 + [VMEM] * 6,
        like(estimate.shape, F32),
        [
            pltpu.VMEM((depth, views * tile_rows, 2 * tile_cols), BF16),
            pltpu.VMEM((depth, views * 2 * HW, 2 * tile_cols), BF16),
        ],
    )(depth_band, place_x, rows_mat, ends_mat, cols_mat, ratio, ex, ox)
    halves = [
        pltpu.VMEM((views, depth * HW, 2 * tile_rows), BF16),
        pltpu.VMEM((views, bands, depth * HW, tile_rows), F32),
        pltpu.VMEM((bands, views * 3 * HW, tile_cols), BF16),
    ]
    near = call(
        even_far_kernel, [SMEM] * 2 + [VMEM] * 4, like(estimate.shape, F32), halves
    )(depth_band, place_y, turned_mat, far_mat, near, ey)
    return call(
        odd_far_kernel,
        [SMEM] * 2 + [VMEM] * 5,
        like(estimate.shape, F32),
        halves + [pltpu.VMEM(estimate.shape, F32), pltpu.SemaphoreType.DMA((depth,))],
        HBM,
    )(depth_band, place_y, turned_mat, far_mat, near, oy, estimate)


def solution(mesh):
    return jax.shard_map(
        body,
        mesh=mesh,
        in_specs=(P(None, "gx", "gy"), P(None, None, "gx", "gy"), P(), P(), P(), P()),
        out_specs=P(None, "gx", "gy"),
        check_vma=False,
    )
```

```python
import functools

import jax
import jax.numpy as jnp
from jax import lax
from jax.experimental import pallas as pl
from jax.experimental.pallas import tpu as pltpu
from jax.sharding import PartitionSpec as P

HW = 8
CAP = 3
LANES = 256
LAST = 2**20
F32 = jnp.float32
BF16 = jnp.bfloat16

VMEM = pl.BlockSpec(memory_space=pltpu.VMEM)
SMEM = pl.BlockSpec(memory_space=pltpu.SMEM)
HBM = pl.BlockSpec(memory_space=pltpu.HBM)
NN = ((1,), (0,))
NT = ((1,), (1,))


def call(kernel, ins, out_shape, scratch=(), out_space=VMEM, limit=16):
    return pl.pallas_call(
        kernel,
        in_specs=ins,
        out_specs=jax.tree.map(lambda _: out_space, out_shape),
        out_shape=out_shape,
        scratch_shapes=list(scratch),
        compiler_params=pltpu.CompilerParams(vmem_limit_bytes=limit * 2**20),
    )


def dot(a, b, dims=NN):
    return lax.dot_general(a, b, (dims, ((), ())), preferred_element_type=F32)


def split(x):
    high = x.astype(BF16)
    return high, (x - high.astype(F32)).astype(BF16)


def stacked(x, axis):
    return jnp.concatenate(split(x), axis=axis)


def halves(x):
    n = x.shape[0] // 2
    return x[:n] + x[n:]


def quarters(x):
    n, m = x.shape[0] // 2, x.shape[1] // 2
    return x[:n, :m] + (x[n:, :m] + x[:n, m:])


def is_odd(place_ref):
    return place_ref[0] % 2 == 1


def halo(place_ref, first, second):
    first, second = first.astype(F32), second.astype(F32)
    odd = is_odd(place_ref)
    after = jnp.where(place_ref[0] >= LAST, 0.0, jnp.where(odd, second, first))
    before = jnp.where(place_ref[0] == 0, 0.0, jnp.where(odd, first, second))
    return jnp.concatenate([after, before], axis=0).astype(BF16)


def edge_picker(cols):
    lane = lax.broadcasted_iota(jnp.int32, (2 * HW, cols), 1)
    sub = lax.broadcasted_iota(jnp.int32, (2 * HW, cols), 0)
    return (lane == jnp.where(sub < HW, sub, sub + cols - 2 * HW)).astype(BF16)


def pack_kernel(
    devices, me_ref, shift_hbm, length_hbm, measured_hbm, out_hbm,
    rows_ref, measured_ref, shift_ref, length_ref, sems,
):
    views, depth, tile_rows, tile_cols = measured_ref.shape
    groups = shift_ref.shape[1]
    loads = [pltpu.make_async_copy(measured_hbm.at[v], measured_ref.at[v], sems.at[v]) for v in range(views)]
    tables = [
        pltpu.make_async_copy(shift_hbm, shift_ref, sems.at[views]),
        pltpu.make_async_copy(length_hbm, length_ref, sems.at[views + 1]),
    ]
    for copy in tables + loads:
        copy.start()
    rows_ref[:, tile_rows:] = jnp.zeros((views, rows_ref.shape[1] - tile_rows) + rows_ref.shape[2:], BF16)
    lane = lax.broadcasted_iota(jnp.int32, (tile_cols, tile_cols), 1)
    sub = lax.broadcasted_iota(jnp.int32, (tile_cols, tile_cols), 0)
    turn = (lane + sub == tile_cols - 1).astype(BF16)
    me = me_ref[0]
    for view in range(views):
        loads[view].wait()
        for r0 in range(0, tile_rows, 16):
            x = measured_ref[view, :, r0 : r0 + 16, :]
            if view % 2 == 1:
                x = dot(x.reshape(depth * 16, tile_cols), turn).reshape(depth, 16, tile_cols)
            x = jnp.transpose(x.astype(F32), (1, 0, 2))
            rows_ref[view, r0 : r0 + 16] = x.astype(BF16)
        if view == 0:
            for copy in tables:
                copy.wait()

        def group(g, start, view=view):
            peer = lax.rem(me + shift_ref[view, g], devices)
            blocks = rows_ref.at[view, pl.ds(start, CAP)]
            pltpu.make_async_copy(blocks, out_hbm.at[peer, view], sems.at[views + 2 + view]).start()
            return start + length_ref[view, g]

        lax.fori_loop(0, groups, group, 0, unroll=True)
    for view in range(views):
        sent = out_hbm.at[pl.ds(0, groups), view]
        pltpu.make_async_copy(sent, sent, sems.at[views + 2 + view]).wait()


def cols_kernel(cells_ref, out_ref):
    pick = edge_picker(cells_ref.shape[-1])
    for z in range(cells_ref.shape[0]):
        out_ref[z] = dot(pick, cells_ref[z].astype(BF16), NT).astype(BF16)


def dense_slab_kernel(place_x_ref, place_y_ref, cols_ref, even_ref, other_ref, first_ref, second_ref):
    views, depth, _, tile_rows = cols_ref.shape
    count = tile_rows // (2 * HW)
    pick = edge_picker(even_ref.shape[-1])
    odd = is_odd(place_y_ref)
    for view in range(views):
        for i in range(first_ref.shape[1]):
            if i < depth:
                edge = cols_ref[view, i].astype(F32)
            else:
                planes = range((i - depth) * count, (i - depth + 1) * count)
                lead = () if len(even_ref.shape) == 3 else (view,)
                ends = [halo(place_x_ref, even_ref[*lead, z], other_ref[*lead, z]) for z in planes]
                edge = dot(pick, jnp.concatenate(ends, axis=0), NT)
            first_ref[view, i] = jnp.where(odd, edge[:HW], edge[HW:]).astype(BF16)
            second_ref[view, i] = jnp.where(odd, edge[HW:], edge[:HW]).astype(BF16)


def edges_kernel(
    devices, tile_rows, me_ref, place_ref, shift_ref, length_ref, arrived_ref, recip_ref, first_ref, second_ref, rows_ref
):
    views = recip_ref.shape[0]
    odd = is_odd(place_ref)
    groups = shift_ref.shape[1]
    me = me_ref[0]
    low = tile_rows - CAP * HW
    for view in range(views):
        ending = tile_rows - low
        for g in range(groups - HW, groups):
            ending = ending - length_ref[view, g]
        for side, (first, start) in enumerate(((0, 0), (groups - HW, ending))):
            for g in range(first, first + HW):
                source = lax.rem(me - shift_ref[view, g] + devices, devices)
                base = source * (views * CAP) + view * CAP
                for k in range(CAP):
                    rows_ref[view, side, start + k] = arrived_ref[base + k].astype(F32)
                start = start + length_ref[view, g]
        head = jnp.transpose(rows_ref[view, 0, :HW], (1, 0, 2)) * recip_ref[view, :, :HW]
        tail = rows_ref[view, 1, (CAP - 1) * HW : CAP * HW]
        tail = jnp.transpose(tail, (1, 0, 2)) * recip_ref[view, :, HW:]
        first_ref[view] = jnp.where(odd, head, tail).astype(BF16)
        second_ref[view] = jnp.where(odd, tail, head).astype(BF16)


def unpack_kernel(devices, me_ref, shift_ref, length_ref, arrived_ref, recip_ref, out_ref, cols_ref, rows_ref):
    views, depth, tile_rows, tile_cols = out_ref.shape
    groups = shift_ref.shape[1]
    me = me_ref[0]
    pick = edge_picker(tile_cols)
    for view in range(views):

        def group(g, start, view=view):
            source = lax.rem(me - shift_ref[view, g] + devices, devices)
            base = source * (views * CAP) + view * CAP
            for k in range(CAP):
                rows_ref[view, start + k] = arrived_ref[base + k].astype(F32)
            return start + length_ref[view, g]

        lax.fori_loop(0, groups, group, 0, unroll=True)
        for r0 in range(0, tile_rows, 16):
            x = jnp.transpose(rows_ref[view, r0 : r0 + 16], (1, 0, 2))
            out_ref[view, :, r0 : r0 + 16, :] = (x * recip_ref[view, :, r0 : r0 + 16, :]).astype(BF16)
        for z in range(depth):
            cols_ref[view, z] = dot(pick, out_ref[view, z], NT).astype(BF16)


def band(taps, size):
    wide = jnp.broadcast_to(taps, (size, LANES))
    inner = pltpu.roll(wide, LANES - HW, 1, stride=1, stride_axis=0)
    before = pltpu.roll(wide, size + HW, 1, stride=1, stride_axis=0)
    lane = lax.broadcasted_iota(jnp.int32, (size, LANES), 1)
    return jnp.where(lane < size + HW, inner, jnp.where(lane < size + 2 * HW, before, 0.0))


def far_products(place_ref, even_ref, other_ref, weights, slab_ref, along_ref):
    depth = slab_ref.shape[0] // (2 * HW)
    tile_rows = slab_ref.shape[1] // 2
    count = tile_rows // (2 * HW)
    owner = lax.broadcasted_iota(jnp.int32, (2 * HW, tile_rows), 1) // (2 * HW)
    for z in range(depth):
        at = pl.ds(z * 2 * HW, 2 * HW)
        slab_ref[at, :tile_rows] = halo(place_ref, even_ref[z], other_ref[z])
        corners = halo(place_ref, even_ref[depth + z // count], other_ref[depth + z // count])
        slab_ref[at, tile_rows:] = jnp.where(owner == z % count, corners.astype(F32), 0.0).astype(BF16)
    for turned_ref, out_ref in zip(weights, along_ref):
        for b in range(turned_ref.shape[0]):
            along = dot(slab_ref[...], turned_ref[b])
            high, low = split(along[:, :tile_rows] + along[:, tile_rows:])
            out_ref[b, 0] = high
            out_ref[b, 1] = low


def far_parts(along_ref, view, b, z):
    at = pl.ds(z * 2 * HW, 2 * HW)
    high, low = along_ref[view, b, 0, at, :], along_ref[view, b, 1, at, :]
    return [high, low, high]


def forward_kernel(
    band_ref, place_ref, taps_ref, cells_ref, even_ref, other_ref,
    blurred_ref, fwd_turned_ref, fwd_far_ref, rows_ref, ends_ref, cols_ref, turned_ref, far_ref, fwd_rows, fwd_cols,
):
    views, depth, tile_rows, tile_cols = blurred_ref.shape
    bands = taps_ref.shape[2]
    for b in range(bands):
        ends = jnp.zeros((tile_rows, LANES - tile_rows), F32)
        for view in range(views):
            for way in range(2):
                along = band(taps_ref[way, view, b, 0:1, :], tile_rows)
                across = band(taps_ref[way, view, b, 1:2, :], tile_cols)
                beyond = along[:, tile_rows:]
                turned, far = ((fwd_turned_ref, fwd_far_ref), (turned_ref, far_ref))[way]
                turned[view, b, :tile_rows] = stacked(along[:, :tile_rows].T, 1)
                corner = stacked(beyond.T[: 2 * HW], 1)
                for at in range(tile_rows, 2 * tile_rows, 2 * HW):
                    turned[view, b, at : at + 2 * HW] = corner
                high, low = split(across[:, tile_cols:].T[: 2 * HW])
                far[b, view] = jnp.concatenate([high, high, low], axis=0)
                inner = stacked(across[:, :tile_cols].T, 1)
                if way == 0:
                    fwd_rows[view, b] = stacked(along[:, : tile_rows + 2 * HW], 0)
                    fwd_cols[view, b] = inner
                else:
                    rows_ref[b, :, view * tile_rows : (view + 1) * tile_rows] = stacked(along[:, :tile_rows], 0)
                    ends = ends + (pltpu.roll(beyond, 2 * HW * view, 1) if view else beyond)
                    cols_ref[view, b] = inner
        ends = jnp.concatenate([ends[:HW], ends[tile_rows - HW :]], axis=0)
        ends_ref[b] = stacked(ends[:, : 2 * HW * views], 0)

    def plane(z, carry):
        b = band_ref[z]
        cells = stacked(cells_ref[z], 1)
        ends = halo(place_ref, even_ref[z], other_ref[z])
        for view in range(views):
            rows = fwd_rows[view, b]
            blurred = quarters(dot(rows[:, :tile_rows], cells)) + halves(dot(rows[:, tile_rows:], ends))
            blurred = quarters(dot(stacked(blurred, 0), fwd_cols[view, b]))
            blurred_ref[view, z] = blurred
        return carry

    lax.fori_loop(0, depth, plane, 0, unroll=2)


def recip_kernel(
    band_ref, place_ref, turned_ref, far_ref, even_ref, other_ref, blurred_ref, out_ref, edge_ref, slab_ref, along_ref
):
    views, depth, tile_rows, tile_cols = blurred_ref.shape
    weights = [turned_ref.at[view] for view in range(views)]
    far_products(place_ref, even_ref.at[0], other_ref.at[0], weights, slab_ref, [along_ref.at[v] for v in range(views)])
    for view in range(views):
        for z in range(depth):
            b = band_ref[z]
            along = jnp.concatenate(far_parts(along_ref, view, b, z), axis=0)
            blurred = blurred_ref[view, z] + dot(along, far_ref[b, view], ((0,), (0,)))
            recip = 1.0 / blurred.astype(BF16).astype(F32)
            out_ref[view, z] = recip
            edge_ref[view, z, :HW] = recip[:HW]
            edge_ref[view, z, HW:] = recip[tile_rows - HW :]


def near_kernel(
    band_ref, place_ref, rows_ref, ends_ref, cols_ref, ratio_ref, even_ref, other_ref, out_ref, inner_ref, outer_ref
):
    views, depth, tile_rows, tile_cols = ratio_ref.shape

    def across(cells, weights):
        blurred = dot(cells, weights)
        return stacked(blurred[:, :tile_cols] + blurred[:, tile_cols:], 1)

    for z in range(depth):
        b = band_ref[z]
        for view in range(views):
            inner_ref[z, view * tile_rows : (view + 1) * tile_rows] = across(ratio_ref[view, z], cols_ref[view, b])
            ends = halo(place_ref, even_ref[view, z], other_ref[view, z])
            outer_ref[z, view * 2 * HW : (view + 1) * 2 * HW] = across(ends, cols_ref[view, b])
    for z in range(depth):
        b = band_ref[z]
        out_ref[z] = quarters(dot(rows_ref[b], inner_ref[z]))
        ends = quarters(dot(ends_ref[b], outer_ref[z]))
        out_ref[z, :HW] += ends[:HW]
        out_ref[z, tile_rows - HW :] += ends[HW:]


def far_kernel(
    band_ref, place_ref, turned_ref, far_ref, near_ref, even_ref, other_ref, estimate_ref, out_hbm,
    slab_ref, along_ref, out_ref, sems,
):
    views, bands = turned_ref.shape[:2]
    depth, tile_rows, tile_cols = near_ref.shape
    step = depth // sems.shape[0]
    for view in range(views):
        far_products(place_ref, even_ref.at[view], other_ref.at[view], [turned_ref.at[view]], slab_ref.at[view], [along_ref.at[view]])
    leave = []
    for z in range(depth):
        b = band_ref[z]
        parts = []
        for view in range(views):
            parts += far_parts(along_ref, view, b, z)
        across = far_ref[b].reshape(views * 6 * HW, tile_cols)
        total = near_ref[z] + dot(jnp.concatenate(parts, axis=0), across, ((0,), (0,)))
        out_ref[z] = estimate_ref[z] * (total * (1.0 / views))
        if z % step == step - 1:
            part = pl.ds(z - step + 1, step)
            leave.append(pltpu.make_async_copy(out_ref.at[part], out_hbm.at[part], sems.at[z // step]))
            leave[-1].start()
    for copy in leave:
        copy.wait()


def swap(first, second, axis, everyone=True):
    both = ("gx", "gy")
    rows, cols = (lax.axis_size(name) for name in both)
    count = lax.axis_size(axis)
    at = lambda p, q: p * cols + q
    partner = lambda i, begin: begin + ((i - begin) ^ 1)
    pairs = []
    for begin in range(2):
        found = []
        for p in range(rows):
            for q in range(cols):
                i = partner(p if axis == "gx" else q, begin)
                if 0 <= i < count:
                    found.append((at(p, q), at(i, q) if axis == "gx" else at(p, i)))
                elif everyone:
                    found.append((at(p, q), at(rows - 1 - p, q) if axis == "gx" else at(p ^ 1, q)))
        pairs.append(found)
    late = lax.ppermute(second, both, pairs[1])
    return lax.ppermute(first, both, pairs[0]), late


def place(count, at):
    return jnp.where(at == count - 1, at + LAST, at).reshape(1)


def body(estimate, measured, kernels, depth_band, group_shift, group_length):
    devices = lax.axis_size("gx") * lax.axis_size("gy")
    gx, gy = lax.axis_index("gx").astype(jnp.int32), lax.axis_index("gy").astype(jnp.int32)
    me = (gx * lax.axis_size("gy") + gy).reshape(1)
    place_x, place_y = (place(lax.axis_size(axis), at) for axis, at in (("gx", gx), ("gy", gy)))
    views, depth, tile_rows, tile_cols = measured.shape
    bands = kernels.shape[1]
    spare = tile_rows + 8
    like = jax.ShapeDtypeStruct
    whole = like(measured.shape, BF16)
    edge_cols = like((views, depth, 2 * HW, tile_rows), BF16)
    edge_rows = like((views, depth, HW, tile_cols), BF16)

    head, tail = estimate[:, :HW], estimate[:, tile_rows - HW :]
    even = gx % 2 == 0
    ex, ox = swap(jnp.where(even, tail, head), jnp.where(even, head, tail), "gx")
    outgoing = call(
        functools.partial(pack_kernel, devices),
        [SMEM, HBM, HBM, HBM],
        like((devices, views, CAP, depth, tile_cols), BF16),
        [
            pltpu.VMEM((views, spare, depth, tile_cols), BF16),
            pltpu.VMEM(measured.shape, BF16),
            pltpu.SMEM(group_shift.shape, jnp.int32),
            pltpu.SMEM(group_length.shape, jnp.int32),
            pltpu.SemaphoreType.DMA((2 * views + 2,)),
        ],
        HBM,
        60,
    )(me, group_shift, group_length, measured)
    outgoing = outgoing.reshape(devices * views * CAP, depth, tile_cols)
    outgoing, ex, ox, cells = lax.optimization_barrier((outgoing, ex, ox, estimate))
    arrived = lax.all_to_all(outgoing, ("gx", "gy"), split_axis=0, concat_axis=0, tiled=True)

    cols = call(cols_kernel, [VMEM], like(edge_cols.shape[1:], BF16))(cells)
    tiles = depth + depth * 2 * HW // tile_rows
    dense = lambda lead, *args: call(
        dense_slab_kernel, [SMEM] * 2 + [VMEM] * 3, (like((lead, tiles, HW, tile_rows), BF16),) * 2
    )(place_x, place_y, *args)
    ey, oy = swap(*dense(1, cols[None], ex, ox), "gy", everyone=False)

    norm = kernels / jnp.sum(kernels, axis=3, keepdims=True)
    tap_rows = jnp.stack([norm, norm[..., ::-1]])
    tap_rows = jnp.pad(tap_rows, ((0, 0),) * 4 + ((0, LANES - kernels.shape[3]),))
    turned_like = like((views, bands, 2 * tile_rows, 2 * tile_rows), BF16)
    far_like = like((bands, views, 6 * HW, tile_cols), BF16)
    blurred, fwd_turned, fwd_far, rows_mat, ends_mat, cols_mat, turned_mat, far_mat = call(
        forward_kernel,
        [SMEM] * 2 + [VMEM] * 4,
        (
            like(measured.shape, F32),
            turned_like,
            far_like,
            like((bands, 2 * tile_rows, views * tile_rows), BF16),
            like((bands, 4 * HW, views * 2 * HW), BF16),
            like((views, bands, tile_cols, 2 * tile_cols), BF16),
            turned_like,
            far_like,
        ),
        [
            pltpu.VMEM((views, bands, 2 * tile_rows, tile_rows + 2 * HW), BF16),
            pltpu.VMEM((views, bands, tile_cols, 2 * tile_cols), BF16),
        ],
    )(depth_band, place_x, tap_rows, cells, ex, ox)

    recip, edge_recip = call(
        recip_kernel,
        [SMEM] * 2 + [VMEM] * 5,
        (like(measured.shape, F32), like((views, depth, 2 * HW, tile_cols), F32)),
        [
            pltpu.VMEM((depth * 2 * HW, 2 * tile_rows), BF16),
            pltpu.VMEM((views, bands, 2, depth * 2 * HW, tile_rows), BF16),
        ],
    )(depth_band, place_y, fwd_turned, fwd_far, ey, oy, blurred)

    first, second = call(
        functools.partial(edges_kernel, devices, tile_rows),
        [SMEM] * 4 + [VMEM] * 2,
        (edge_rows, edge_rows),
        [pltpu.VMEM((views, 2, CAP * HW + 8, depth, tile_cols), F32)],
    )(me, place_x, group_shift, group_length, arrived, edge_recip)
    ex, ox = swap(first, second, "gx")
    ratio, cols = call(
        functools.partial(unpack_kernel, devices),
        [SMEM] * 3 + [VMEM] * 2,
        (whole, edge_cols),
        [pltpu.VMEM((views, spare, depth, tile_cols), F32)],
    )(me, group_shift, group_length, arrived, recip)
    ey, oy = swap(*dense(views, cols, ex, ox), "gy")
    near = call(
        near_kernel,
        [SMEM] * 2 + [VMEM] * 6,
        like(estimate.shape, F32),
        [
            pltpu.VMEM((depth, views * tile_rows, 2 * tile_cols), BF16),
            pltpu.VMEM((depth, views * 2 * HW, 2 * tile_cols), BF16),
        ],
    )(depth_band, place_x, rows_mat, ends_mat, cols_mat, ratio, ex, ox)
    return call(
        far_kernel,
        [SMEM] * 2 + [VMEM] * 6,
        like(estimate.shape, F32),
        [
            pltpu.VMEM((views, depth * 2 * HW, 2 * tile_rows), BF16),
            pltpu.VMEM((views, bands, 2, depth * 2 * HW, tile_rows), BF16),
            pltpu.VMEM(estimate.shape, F32),
            pltpu.SemaphoreType.DMA((4,)),
        ],
        HBM,
    )(depth_band, place_y, turned_mat, far_mat, near, ey, oy, estimate)


def solution(mesh):
    return jax.shard_map(
        body,
        mesh=mesh,
        in_specs=(P(None, "gx", "gy"), P(None, None, "gx", "gy"), P(), P(), P(), P()),
        out_specs=P(None, "gx", "gy"),
        check_vma=False,
    )
```

```python
import functools

import jax
import jax.numpy as jnp
from jax import lax
from jax.experimental import pallas as pl
from jax.experimental.pallas import tpu as pltpu
from jax.sharding import PartitionSpec as P

HW = 8
CAP = 3
LANES = 256
LAST = 2**20
F32 = jnp.float32
BF16 = jnp.bfloat16

VMEM = pl.BlockSpec(memory_space=pltpu.VMEM)
SMEM = pl.BlockSpec(memory_space=pltpu.SMEM)
HBM = pl.BlockSpec(memory_space=pltpu.HBM)
NN = ((1,), (0,))
NT = ((1,), (1,))


def call(kernel, ins, out_shape, scratch=(), out_space=VMEM, limit=16):
    return pl.pallas_call(
        kernel,
        in_specs=ins,
        out_specs=jax.tree.map(lambda _: out_space, out_shape),
        out_shape=out_shape,
        scratch_shapes=list(scratch),
        compiler_params=pltpu.CompilerParams(vmem_limit_bytes=limit * 2**20),
    )


def dot(a, b, dims=NN):
    return lax.dot_general(a, b, (dims, ((), ())), preferred_element_type=F32)


def split(x):
    high = x.astype(BF16)
    return high, (x - high.astype(F32)).astype(BF16)


def stacked(x, axis):
    return jnp.concatenate(split(x), axis=axis)


def halves(x):
    n = x.shape[0] // 2
    return x[:n] + x[n:]


def quarters(x):
    n, m = x.shape[0] // 2, x.shape[1] // 2
    return x[:n, :m] + (x[n:, :m] + x[:n, m:])


def is_odd(place_ref):
    return place_ref[0] % 2 == 1


def halo(place_ref, first, second):
    first, second = first.astype(F32), second.astype(F32)
    odd = is_odd(place_ref)
    after = jnp.where(place_ref[0] >= LAST, 0.0, jnp.where(odd, second, first))
    before = jnp.where(place_ref[0] == 0, 0.0, jnp.where(odd, first, second))
    return jnp.concatenate([after, before], axis=0).astype(BF16)


def edge_picker(cols):
    lane = lax.broadcasted_iota(jnp.int32, (2 * HW, cols), 1)
    sub = lax.broadcasted_iota(jnp.int32, (2 * HW, cols), 0)
    return (lane == jnp.where(sub < HW, sub, sub + cols - 2 * HW)).astype(BF16)


def pack_kernel(
    devices, me_ref, shift_hbm, length_hbm, measured_hbm, out_hbm,
    rows_ref, measured_ref, shift_ref, length_ref, sems,
):
    views, depth, tile_rows, tile_cols = measured_ref.shape
    groups = shift_ref.shape[1]
    loads = [pltpu.make_async_copy(measured_hbm.at[v], measured_ref.at[v], sems.at[v]) for v in range(views)]
    tables = [
        pltpu.make_async_copy(shift_hbm, shift_ref, sems.at[views]),
        pltpu.make_async_copy(length_hbm, length_ref, sems.at[views + 1]),
    ]
    for copy in tables + loads:
        copy.start()
    rows_ref[:, tile_rows:] = jnp.zeros((views, rows_ref.shape[1] - tile_rows) + rows_ref.shape[2:], BF16)
    lane = lax.broadcasted_iota(jnp.int32, (tile_cols, tile_cols), 1)
    sub = lax.broadcasted_iota(jnp.int32, (tile_cols, tile_cols), 0)
    turn = (lane + sub == tile_cols - 1).astype(BF16)
    me = me_ref[0]
    for view in range(views):
        loads[view].wait()
        for r0 in range(0, tile_rows, 16):
            x = measured_ref[view, :, r0 : r0 + 16, :]
            if view % 2 == 1:
                x = dot(x.reshape(depth * 16, tile_cols), turn).reshape(depth, 16, tile_cols)
            x = jnp.transpose(x.astype(F32), (1, 0, 2))
            rows_ref[view, r0 : r0 + 16] = x.astype(BF16)
        if view == 0:
            for copy in tables:
                copy.wait()

        def group(g, start, view=view):
            peer = lax.rem(me + shift_ref[view, g], devices)
            blocks = rows_ref.at[view, pl.ds(start, CAP)]
            pltpu.make_async_copy(blocks, out_hbm.at[peer, view], sems.at[views + 2 + view]).start()
            return start + length_ref[view, g]

        lax.fori_loop(0, groups, group, 0, unroll=True)
    for view in range(views):
        sent = out_hbm.at[pl.ds(0, groups), view]
        pltpu.make_async_copy(sent, sent, sems.at[views + 2 + view]).wait()


def cols_kernel(cells_ref, out_ref):
    pick = edge_picker(cells_ref.shape[-1])
    for z in range(cells_ref.shape[0]):
        out_ref[z] = dot(pick, cells_ref[z].astype(BF16), NT).astype(BF16)


def dense_slab_kernel(place_x_ref, place_y_ref, cols_ref, even_ref, other_ref, first_ref, second_ref):
    views, depth, _, tile_rows = cols_ref.shape
    count = tile_rows // (2 * HW)
    pick = edge_picker(even_ref.shape[-1])
    odd = is_odd(place_y_ref)
    for view in range(views):
        for i in range(first_ref.shape[1]):
            if i < depth:
                edge = cols_ref[view, i].astype(F32)
            else:
                planes = range((i - depth) * count, (i - depth + 1) * count)
                lead = () if len(even_ref.shape) == 3 else (view,)
                ends = [halo(place_x_ref, even_ref[*lead, z], other_ref[*lead, z]) for z in planes]
                edge = dot(pick, jnp.concatenate(ends, axis=0), NT)
            first_ref[view, i] = jnp.where(odd, edge[:HW], edge[HW:]).astype(BF16)
            second_ref[view, i] = jnp.where(odd, edge[HW:], edge[:HW]).astype(BF16)


def edges_kernel(
    devices, tile_rows, me_ref, place_ref, shift_ref, length_ref, arrived_ref, recip_ref, first_ref, second_ref, rows_ref
):
    views = recip_ref.shape[0]
    odd = is_odd(place_ref)
    groups = shift_ref.shape[1]
    me = me_ref[0]
    low = tile_rows - CAP * HW
    for view in range(views):
        ending = tile_rows - low
        for g in range(groups - HW, groups):
            ending = ending - length_ref[view, g]
        for side, (first, start) in enumerate(((0, 0), (groups - HW, ending))):
            for g in range(first, first + HW):
                source = lax.rem(me - shift_ref[view, g] + devices, devices)
                base = source * (views * CAP) + view * CAP
                for k in range(CAP):
                    rows_ref[view, side, start + k] = arrived_ref[base + k].astype(F32)
                start = start + length_ref[view, g]
        head = jnp.transpose(rows_ref[view, 0, :HW], (1, 0, 2)) * recip_ref[view, :, :HW]
        tail = rows_ref[view, 1, (CAP - 1) * HW : CAP * HW]
        tail = jnp.transpose(tail, (1, 0, 2)) * recip_ref[view, :, HW:]
        first_ref[view] = jnp.where(odd, head, tail).astype(BF16)
        second_ref[view] = jnp.where(odd, tail, head).astype(BF16)


def unpack_kernel(devices, me_ref, shift_ref, length_ref, arrived_ref, forward_ref, out_ref, cols_ref, rows_ref):
    views, depth, tile_rows, tile_cols = out_ref.shape
    groups = shift_ref.shape[1]
    me = me_ref[0]
    pick = edge_picker(tile_cols)
    for view in range(views):

        def group(g, start, view=view):
            source = lax.rem(me - shift_ref[view, g] + devices, devices)
            base = source * (views * CAP) + view * CAP
            for k in range(CAP):
                rows_ref[view, start + k] = arrived_ref[base + k].astype(F32)
            return start + length_ref[view, g]

        lax.fori_loop(0, groups, group, 0, unroll=True)
        for r0 in range(0, tile_rows, 16):
            x = jnp.transpose(rows_ref[view, r0 : r0 + 16], (1, 0, 2))
            forward = forward_ref[view, :, r0 : r0 + 16, :].astype(F32)
            out_ref[view, :, r0 : r0 + 16, :] = (x / forward).astype(BF16)
        for z in range(depth):
            cols_ref[view, z] = dot(pick, out_ref[view, z], NT).astype(BF16)


def band(taps, size):
    wide = jnp.broadcast_to(taps, (size, LANES))
    inner = pltpu.roll(wide, LANES - HW, 1, stride=1, stride_axis=0)
    before = pltpu.roll(wide, size + HW, 1, stride=1, stride_axis=0)
    lane = lax.broadcasted_iota(jnp.int32, (size, LANES), 1)
    return jnp.where(lane < size + HW, inner, jnp.where(lane < size + 2 * HW, before, 0.0))


def far_products(place_ref, even_ref, other_ref, weights, slab_ref, along_ref):
    depth = slab_ref.shape[0] // (2 * HW)
    tile_rows = slab_ref.shape[1] // 2
    count = tile_rows // (2 * HW)
    owner = lax.broadcasted_iota(jnp.int32, (2 * HW, tile_rows), 1) // (2 * HW)
    for z in range(depth):
        at = pl.ds(z * 2 * HW, 2 * HW)
        slab_ref[at, :tile_rows] = halo(place_ref, even_ref[z], other_ref[z])
        corners = halo(place_ref, even_ref[depth + z // count], other_ref[depth + z // count])
        slab_ref[at, tile_rows:] = jnp.where(owner == z % count, corners.astype(F32), 0.0).astype(BF16)
    for turned_ref, out_ref in zip(weights, along_ref):
        for b in range(turned_ref.shape[0]):
            along = dot(slab_ref[...], turned_ref[b])
            high, low = split(along[:, :tile_rows] + along[:, tile_rows:])
            out_ref[b, 0] = high
            out_ref[b, 1] = low


def far_parts(along_ref, view, b, z):
    at = pl.ds(z * 2 * HW, 2 * HW)
    high, low = along_ref[view, b, 0, at, :], along_ref[view, b, 1, at, :]
    return [high, low, high]


def forward_kernel(
    band_ref, place_ref, taps_ref, cells_ref, even_ref, other_ref,
    blurred_ref, fwd_turned_ref, fwd_far_ref, rows_ref, ends_ref, cols_ref, turned_ref, far_ref, fwd_rows, fwd_cols,
):
    views, depth, tile_rows, tile_cols = blurred_ref.shape
    bands = taps_ref.shape[2]
    for b in range(bands):
        ends = jnp.zeros((tile_rows, LANES - tile_rows), F32)
        for view in range(views):
            for way in range(2):
                along = band(taps_ref[way, view, b, 0:1, :], tile_rows)
                across = band(taps_ref[way, view, b, 1:2, :], tile_cols)
                beyond = along[:, tile_rows:]
                turned, far = ((fwd_turned_ref, fwd_far_ref), (turned_ref, far_ref))[way]
                turned[view, b, :tile_rows] = stacked(along[:, :tile_rows].T, 1)
                corner = stacked(beyond.T[: 2 * HW], 1)
                for at in range(tile_rows, 2 * tile_rows, 2 * HW):
                    turned[view, b, at : at + 2 * HW] = corner
                high, low = split(across[:, tile_cols:].T[: 2 * HW])
                far[b, view] = jnp.concatenate([high, high, low], axis=0)
                inner = stacked(across[:, :tile_cols].T, 1)
                if way == 0:
                    fwd_rows[view, b] = stacked(along[:, : tile_rows + 2 * HW], 0)
                    fwd_cols[view, b] = inner
                else:
                    rows_ref[b, :, view * tile_rows : (view + 1) * tile_rows] = stacked(along[:, :tile_rows], 0)
                    ends = ends + (pltpu.roll(beyond, 2 * HW * view, 1) if view else beyond)
                    cols_ref[view, b] = inner
        ends = jnp.concatenate([ends[:HW], ends[tile_rows - HW :]], axis=0)
        ends_ref[b] = stacked(ends[:, : 2 * HW * views], 0)

    def plane(z, carry):
        b = band_ref[z]
        cells = stacked(cells_ref[z], 1)
        ends = halo(place_ref, even_ref[z], other_ref[z])
        for view in range(views):
            rows = fwd_rows[view, b]
            blurred = quarters(dot(rows[:, :tile_rows], cells)) + halves(dot(rows[:, tile_rows:], ends))
            blurred = quarters(dot(stacked(blurred, 0), fwd_cols[view, b]))
            blurred_ref[view, z] = blurred
        return carry

    lax.fori_loop(0, depth, plane, 0, unroll=2)


def late_kernel(
    band_ref, place_ref, turned_ref, far_ref, even_ref, other_ref, blurred_ref, out_ref, edge_ref, slab_ref, along_ref
):
    views, depth, tile_rows, tile_cols = blurred_ref.shape
    weights = [turned_ref.at[view] for view in range(views)]
    far_products(place_ref, even_ref.at[0], other_ref.at[0], weights, slab_ref, [along_ref.at[v] for v in range(views)])
    for view in range(views):
        for z in range(depth):
            b = band_ref[z]
            along = jnp.concatenate(far_parts(along_ref, view, b, z), axis=0)
            blurred = blurred_ref[view, z] + dot(along, far_ref[b, view], ((0,), (0,)))
            blurred = blurred.astype(BF16)
            out_ref[view, z] = blurred
            recip = 1.0 / blurred.astype(F32)
            edge_ref[view, z, :HW] = recip[:HW]
            edge_ref[view, z, HW:] = recip[tile_rows - HW :]


def near_kernel(
    band_ref, place_ref, rows_ref, ends_ref, cols_ref, ratio_ref, even_ref, other_ref, out_ref, inner_ref, outer_ref
):
    views, depth, tile_rows, tile_cols = ratio_ref.shape

    def across(cells, weights):
        blurred = dot(cells, weights)
        return stacked(blurred[:, :tile_cols] + blurred[:, tile_cols:], 1)

    for z in range(depth):
        b = band_ref[z]
        for view in range(views):
            inner_ref[z, view * tile_rows : (view + 1) * tile_rows] = across(ratio_ref[view, z], cols_ref[view, b])
            ends = halo(place_ref, even_ref[view, z], other_ref[view, z])
            outer_ref[z, view * 2 * HW : (view + 1) * 2 * HW] = across(ends, cols_ref[view, b])
    for z in range(depth):
        b = band_ref[z]
        out_ref[z] = quarters(dot(rows_ref[b], inner_ref[z]))
        ends = quarters(dot(ends_ref[b], outer_ref[z]))
        out_ref[z, :HW] += ends[:HW]
        out_ref[z, tile_rows - HW :] += ends[HW:]


def far_kernel(
    band_ref, place_ref, turned_ref, far_ref, near_ref, even_ref, other_ref, estimate_ref, out_hbm,
    slab_ref, along_ref, out_ref, sems,
):
    views, bands = turned_ref.shape[:2]
    depth, tile_rows, tile_cols = near_ref.shape
    step = depth // sems.shape[0]
    for view in range(views):
        far_products(place_ref, even_ref.at[view], other_ref.at[view], [turned_ref.at[view]], slab_ref.at[view], [along_ref.at[view]])
    leave = []
    for z in range(depth):
        b = band_ref[z]
        parts = []
        for view in range(views):
            parts += far_parts(along_ref, view, b, z)
        across = far_ref[b].reshape(views * 6 * HW, tile_cols)
        total = near_ref[z] + dot(jnp.concatenate(parts, axis=0), across, ((0,), (0,)))
        out_ref[z] = estimate_ref[z] * (total * (1.0 / views))
        if z % step == step - 1:
            part = pl.ds(z - step + 1, step)
            leave.append(pltpu.make_async_copy(out_ref.at[part], out_hbm.at[part], sems.at[z // step]))
            leave[-1].start()
    for copy in leave:
        copy.wait()


def swap(first, second, axis, everyone=True):
    both = ("gx", "gy")
    rows, cols = (lax.axis_size(name) for name in both)
    count = lax.axis_size(axis)
    at = lambda p, q: p * cols + q
    partner = lambda i, begin: begin + ((i - begin) ^ 1)
    pairs = []
    for begin in range(2):
        found = []
        for p in range(rows):
            for q in range(cols):
                i = partner(p if axis == "gx" else q, begin)
                if 0 <= i < count:
                    found.append((at(p, q), at(i, q) if axis == "gx" else at(p, i)))
                elif everyone:
                    found.append((at(p, q), at(p, q ^ 1) if axis == "gx" else at(p ^ 1, q)))
        pairs.append(found)
    late = lax.ppermute(second, both, pairs[1])
    return lax.ppermute(first, both, pairs[0]), late


def place(count, at):
    return jnp.where(at == count - 1, at + LAST, at).reshape(1)


def body(estimate, measured, kernels, depth_band, group_shift, group_length):
    devices = lax.axis_size("gx") * lax.axis_size("gy")
    gx, gy = lax.axis_index("gx").astype(jnp.int32), lax.axis_index("gy").astype(jnp.int32)
    me = (gx * lax.axis_size("gy") + gy).reshape(1)
    place_x, place_y = (place(lax.axis_size(axis), at) for axis, at in (("gx", gx), ("gy", gy)))
    views, depth, tile_rows, tile_cols = measured.shape
    bands = kernels.shape[1]
    spare = tile_rows + 8
    like = jax.ShapeDtypeStruct
    whole = like(measured.shape, BF16)
    edge_cols = like((views, depth, 2 * HW, tile_rows), BF16)
    edge_rows = like((views, depth, HW, tile_cols), BF16)

    head, tail = estimate[:, :HW], estimate[:, tile_rows - HW :]
    even = gx % 2 == 0
    ex, ox = swap(jnp.where(even, tail, head), jnp.where(even, head, tail), "gx")
    outgoing = call(
        functools.partial(pack_kernel, devices),
        [SMEM, HBM, HBM, HBM],
        like((devices, views, CAP, depth, tile_cols), BF16),
        [
            pltpu.VMEM((views, spare, depth, tile_cols), BF16),
            pltpu.VMEM(measured.shape, BF16),
            pltpu.SMEM(group_shift.shape, jnp.int32),
            pltpu.SMEM(group_length.shape, jnp.int32),
            pltpu.SemaphoreType.DMA((2 * views + 2,)),
        ],
        HBM,
        60,
    )(me, group_shift, group_length, measured)
    outgoing = outgoing.reshape(devices * views * CAP, depth, tile_cols)
    outgoing, ex, ox, cells = lax.optimization_barrier((outgoing, ex, ox, estimate))
    arrived = lax.all_to_all(outgoing, ("gx", "gy"), split_axis=0, concat_axis=0, tiled=True)

    cols = call(cols_kernel, [VMEM], like(edge_cols.shape[1:], BF16))(cells)
    tiles = depth + depth * 2 * HW // tile_rows
    dense = lambda lead, *args: call(
        dense_slab_kernel, [SMEM] * 2 + [VMEM] * 3, (like((lead, tiles, HW, tile_rows), BF16),) * 2
    )(place_x, place_y, *args)
    ey, oy = swap(*dense(1, cols[None], ex, ox), "gy", everyone=False)

    norm = kernels / jnp.sum(kernels, axis=3, keepdims=True)
    tap_rows = jnp.stack([norm, norm[..., ::-1]])
    tap_rows = jnp.pad(tap_rows, ((0, 0),) * 4 + ((0, LANES - kernels.shape[3]),))
    turned_like = like((views, bands, 2 * tile_rows, 2 * tile_rows), BF16)
    far_like = like((bands, views, 6 * HW, tile_cols), BF16)
    blurred, fwd_turned, fwd_far, rows_mat, ends_mat, cols_mat, turned_mat, far_mat = call(
        forward_kernel,
        [SMEM] * 2 + [VMEM] * 4,
        (
            like(measured.shape, F32),
            turned_like,
            far_like,
            like((bands, 2 * tile_rows, views * tile_rows), BF16),
            like((bands, 4 * HW, views * 2 * HW), BF16),
            like((views, bands, tile_cols, 2 * tile_cols), BF16),
            turned_like,
            far_like,
        ),
        [
            pltpu.VMEM((views, bands, 2 * tile_rows, tile_rows + 2 * HW), BF16),
            pltpu.VMEM((views, bands, tile_cols, 2 * tile_cols), BF16),
        ],
    )(depth_band, place_x, tap_rows, cells, ex, ox)

    forward, edge_recip = call(
        late_kernel,
        [SMEM] * 2 + [VMEM] * 5,
        (whole, like((views, depth, 2 * HW, tile_cols), F32)),
        [
            pltpu.VMEM((depth * 2 * HW, 2 * tile_rows), BF16),
            pltpu.VMEM((views, bands, 2, depth * 2 * HW, tile_rows), BF16),
        ],
    )(depth_band, place_y, fwd_turned, fwd_far, ey, oy, blurred)

    first, second = call(
        functools.partial(edges_kernel, devices, tile_rows),
        [SMEM] * 4 + [VMEM] * 2,
        (edge_rows, edge_rows),
        [pltpu.VMEM((views, 2, CAP * HW + 8, depth, tile_cols), F32)],
    )(me, place_x, group_shift, group_length, arrived, edge_recip)
    ex, ox = swap(first, second, "gx")
    ratio, cols = call(
        functools.partial(unpack_kernel, devices),
        [SMEM] * 3 + [VMEM] * 2,
        (whole, edge_cols),
        [pltpu.VMEM((views, spare, depth, tile_cols), F32)],
    )(me, group_shift, group_length, arrived, forward)
    ey, oy = swap(*dense(views, cols, ex, ox), "gy")
    near = call(
        near_kernel,
        [SMEM] * 2 + [VMEM] * 6,
        like(estimate.shape, F32),
        [
            pltpu.VMEM((depth, views * tile_rows, 2 * tile_cols), BF16),
            pltpu.VMEM((depth, views * 2 * HW, 2 * tile_cols), BF16),
        ],
    )(depth_band, place_x, rows_mat, ends_mat, cols_mat, ratio, ex, ox)
    return call(
        far_kernel,
        [SMEM] * 2 + [VMEM] * 6,
        like(estimate.shape, F32),
        [
            pltpu.VMEM((views, depth * 2 * HW, 2 * tile_rows), BF16),
            pltpu.VMEM((views, bands, 2, depth * 2 * HW, tile_rows), BF16),
            pltpu.VMEM(estimate.shape, F32),
            pltpu.SemaphoreType.DMA((4,)),
        ],
        HBM,
    )(depth_band, place_y, turned_mat, far_mat, near, ey, oy, estimate)


def solution(mesh):
    return jax.shard_map(
        body,
        mesh=mesh,
        in_specs=(P(None, "gx", "gy"), P(None, None, "gx", "gy"), P(), P(), P(), P()),
        out_specs=P(None, "gx", "gy"),
        check_vma=False,
    )
```

```python
import functools

import jax
import jax.numpy as jnp
from jax import lax
from jax.experimental import pallas as pl
from jax.experimental.pallas import tpu as pltpu
from jax.sharding import PartitionSpec as P

HW = 8
CAP = 3
LANES = 256
LAST = 2**20
F32 = jnp.float32
BF16 = jnp.bfloat16

VMEM = pl.BlockSpec(memory_space=pltpu.VMEM)
SMEM = pl.BlockSpec(memory_space=pltpu.SMEM)
HBM = pl.BlockSpec(memory_space=pltpu.HBM)
NN = ((1,), (0,))
NT = ((1,), (1,))


def call(kernel, ins, out_shape, scratch=(), out_space=VMEM, limit=16):
    return pl.pallas_call(
        kernel,
        in_specs=ins,
        out_specs=jax.tree.map(lambda _: out_space, out_shape),
        out_shape=out_shape,
        scratch_shapes=list(scratch),
        compiler_params=pltpu.CompilerParams(vmem_limit_bytes=limit * 2**20),
    )


def dot(a, b, dims=NN):
    return lax.dot_general(a, b, (dims, ((), ())), preferred_element_type=F32)


def split(x):
    high = x.astype(BF16)
    return high, (x - high.astype(F32)).astype(BF16)


def stacked(x, axis):
    return jnp.concatenate(split(x), axis=axis)


def halves(x):
    n = x.shape[0] // 2
    return x[:n] + x[n:]


def quarters(x):
    n, m = x.shape[0] // 2, x.shape[1] // 2
    return x[:n, :m] + (x[n:, :m] + x[:n, m:])


def is_odd(place_ref):
    return place_ref[0] % 2 == 1


def halo(place_ref, first, second):
    first, second = first.astype(F32), second.astype(F32)
    odd = is_odd(place_ref)
    after = jnp.where(place_ref[0] >= LAST, 0.0, jnp.where(odd, second, first))
    before = jnp.where(place_ref[0] == 0, 0.0, jnp.where(odd, first, second))
    return jnp.concatenate([after, before], axis=0).astype(BF16)


def edge_picker(cols):
    lane = lax.broadcasted_iota(jnp.int32, (2 * HW, cols), 1)
    sub = lax.broadcasted_iota(jnp.int32, (2 * HW, cols), 0)
    return (lane == jnp.where(sub < HW, sub, sub + cols - 2 * HW)).astype(BF16)


def pack_kernel(
    devices, me_ref, shift_hbm, length_hbm, measured_hbm, out_hbm,
    rows_ref, measured_ref, shift_ref, length_ref, sems,
):
    views, depth, tile_rows, tile_cols = measured_ref.shape
    groups = shift_ref.shape[1]
    loads = [pltpu.make_async_copy(measured_hbm.at[v], measured_ref.at[v], sems.at[v]) for v in range(views)]
    tables = [
        pltpu.make_async_copy(shift_hbm, shift_ref, sems.at[views]),
        pltpu.make_async_copy(length_hbm, length_ref, sems.at[views + 1]),
    ]
    for copy in tables + loads:
        copy.start()
    rows_ref[:, tile_rows:] = jnp.zeros((views, rows_ref.shape[1] - tile_rows) + rows_ref.shape[2:], BF16)
    lane = lax.broadcasted_iota(jnp.int32, (tile_cols, tile_cols), 1)
    sub = lax.broadcasted_iota(jnp.int32, (tile_cols, tile_cols), 0)
    turn = (lane + sub == tile_cols - 1).astype(BF16)
    me = me_ref[0]
    for view in range(views):
        loads[view].wait()
        for r0 in range(0, tile_rows, 16):
            x = measured_ref[view, :, r0 : r0 + 16, :]
            if view % 2 == 1:
                x = dot(x.reshape(depth * 16, tile_cols), turn).reshape(depth, 16, tile_cols)
            x = jnp.transpose(x.astype(F32), (1, 0, 2))
            rows_ref[view, r0 : r0 + 16] = x.astype(BF16)
        if view == 0:
            for copy in tables:
                copy.wait()

        def group(g, start, view=view):
            peer = lax.rem(me + shift_ref[view, g], devices)
            blocks = rows_ref.at[view, pl.ds(start, CAP)]
            pltpu.make_async_copy(blocks, out_hbm.at[peer, view], sems.at[views + 2 + view]).start()
            return start + length_ref[view, g]

        lax.fori_loop(0, groups, group, 0, unroll=True)
    for view in range(views):
        sent = out_hbm.at[pl.ds(0, groups), view]
        pltpu.make_async_copy(sent, sent, sems.at[views + 2 + view]).wait()


def cols_kernel(cells_ref, out_ref):
    pick = edge_picker(cells_ref.shape[-1])
    for z in range(cells_ref.shape[0]):
        out_ref[z] = dot(pick, cells_ref[z].astype(BF16), NT).astype(BF16)


def dense_slab_kernel(place_x_ref, place_y_ref, cols_ref, even_ref, other_ref, first_ref, second_ref):
    views, depth, _, tile_rows = cols_ref.shape
    count = tile_rows // (2 * HW)
    pick = edge_picker(even_ref.shape[-1])
    odd = is_odd(place_y_ref)
    for view in range(views):
        for i in range(first_ref.shape[1]):
            if i < depth:
                edge = cols_ref[view, i].astype(F32)
            else:
                planes = range((i - depth) * count, (i - depth + 1) * count)
                lead = () if len(even_ref.shape) == 3 else (view,)
                ends = [halo(place_x_ref, even_ref[*lead, z], other_ref[*lead, z]) for z in planes]
                edge = dot(pick, jnp.concatenate(ends, axis=0), NT)
            first_ref[view, i] = jnp.where(odd, edge[:HW], edge[HW:]).astype(BF16)
            second_ref[view, i] = jnp.where(odd, edge[HW:], edge[:HW]).astype(BF16)


def edges_kernel(
    devices, tile_rows, me_ref, place_ref, shift_ref, length_ref, arrived_ref, edge_ref, first_ref, second_ref, rows_ref
):
    views = edge_ref.shape[0]
    odd = is_odd(place_ref)
    groups = shift_ref.shape[1]
    me = me_ref[0]
    low = tile_rows - CAP * HW
    for view in range(views):
        ending = tile_rows - low
        for g in range(groups - HW, groups):
            ending = ending - length_ref[view, g]
        for side, (first, start) in enumerate(((0, 0), (groups - HW, ending))):
            for g in range(first, first + HW):
                source = lax.rem(me - shift_ref[view, g] + devices, devices)
                base = source * (views * CAP) + view * CAP
                for k in range(CAP):
                    rows_ref[view, side, start + k] = arrived_ref[base + k].astype(F32)
                start = start + length_ref[view, g]
        edge = edge_ref[view, :, 4 * HW :].astype(F32)
        head = jnp.transpose(rows_ref[view, 0, :HW], (1, 0, 2)) / edge[:, :HW]
        tail = rows_ref[view, 1, (CAP - 1) * HW : CAP * HW]
        tail = jnp.transpose(tail, (1, 0, 2)) / edge[:, HW:]
        first_ref[view] = jnp.where(odd, head, tail).astype(BF16)
        second_ref[view] = jnp.where(odd, tail, head).astype(BF16)


def unpack_kernel(
    devices, me_ref, band_ref, shift_ref, length_ref, arrived_ref, blurred_ref, far_ref, parts_ref,
    out_ref, cols_ref, rows_ref, forward_ref,
):
    views, depth, tile_rows, tile_cols = out_ref.shape
    groups = shift_ref.shape[1]
    me = me_ref[0]
    pick = edge_picker(tile_cols)
    for view in range(views):

        def group(g, start, view=view):
            source = lax.rem(me - shift_ref[view, g] + devices, devices)
            base = source * (views * CAP) + view * CAP
            for k in range(CAP):
                rows_ref[view, start + k] = arrived_ref[base + k].astype(F32)
            return start + length_ref[view, g]

        lax.fori_loop(0, groups, group, 0, unroll=True)
        for z in range(depth):
            parts = parts_ref[view, z, : 4 * HW]
            parts = jnp.concatenate([parts, parts[: 2 * HW]], axis=0)
            across = dot(parts, far_ref[band_ref[z], view], ((0,), (0,)))
            forward_ref[view, z] = (blurred_ref[view, z] + across).astype(BF16)
        for r0 in range(0, tile_rows, 16):
            x = jnp.transpose(rows_ref[view, r0 : r0 + 16], (1, 0, 2))
            forward = forward_ref[view, :, r0 : r0 + 16, :].astype(F32)
            out_ref[view, :, r0 : r0 + 16, :] = (x / forward).astype(BF16)
        for z in range(depth):
            cols_ref[view, z] = dot(pick, out_ref[view, z], NT).astype(BF16)


def band(taps, size):
    wide = jnp.broadcast_to(taps, (size, LANES))
    inner = pltpu.roll(wide, LANES - HW, 1, stride=1, stride_axis=0)
    before = pltpu.roll(wide, size + HW, 1, stride=1, stride_axis=0)
    lane = lax.broadcasted_iota(jnp.int32, (size, LANES), 1)
    return jnp.where(lane < size + HW, inner, jnp.where(lane < size + 2 * HW, before, 0.0))


def far_products(place_ref, even_ref, other_ref, weights, slab_ref, along_ref):
    depth = slab_ref.shape[0] // (2 * HW)
    tile_rows = slab_ref.shape[1] // 2
    count = tile_rows // (2 * HW)
    owner = lax.broadcasted_iota(jnp.int32, (2 * HW, tile_rows), 1) // (2 * HW)
    for z in range(depth):
        at = pl.ds(z * 2 * HW, 2 * HW)
        slab_ref[at, :tile_rows] = halo(place_ref, even_ref[z], other_ref[z])
        corners = halo(place_ref, even_ref[depth + z // count], other_ref[depth + z // count])
        slab_ref[at, tile_rows:] = jnp.where(owner == z % count, corners.astype(F32), 0.0).astype(BF16)
    for turned_ref, out_ref in zip(weights, along_ref):
        for b in range(turned_ref.shape[0]):
            along = dot(slab_ref[...], turned_ref[b])
            high, low = split(along[:, :tile_rows] + along[:, tile_rows:])
            out_ref[b, 0] = high
            out_ref[b, 1] = low


def far_parts(along_ref, view, b, z):
    at = pl.ds(z * 2 * HW, 2 * HW)
    high, low = along_ref[view, b, 0, at, :], along_ref[view, b, 1, at, :]
    return [high, low, high]


def forward_kernel(
    band_ref, place_ref, taps_ref, cells_ref, even_ref, other_ref,
    blurred_ref, edge_ref, fwd_turned_ref, fwd_far_ref, later_far_ref, rows_ref, ends_ref, cols_ref, turned_ref, far_ref, fwd_rows, fwd_cols,
):
    views, depth, tile_rows, tile_cols = blurred_ref.shape
    bands = taps_ref.shape[2]
    for b in range(bands):
        ends = jnp.zeros((tile_rows, LANES - tile_rows), F32)
        for view in range(views):
            for way in range(2):
                along = band(taps_ref[way, view, b, 0:1, :], tile_rows)
                across = band(taps_ref[way, view, b, 1:2, :], tile_cols)
                beyond = along[:, tile_rows:]
                turned, far = ((fwd_turned_ref, fwd_far_ref), (turned_ref, far_ref))[way]
                turned[view, b, :tile_rows] = stacked(along[:, :tile_rows].T, 1)
                corner = stacked(beyond.T[: 2 * HW], 1)
                for at in range(tile_rows, 2 * tile_rows, 2 * HW):
                    turned[view, b, at : at + 2 * HW] = corner
                high, low = split(across[:, tile_cols:].T[: 2 * HW])
                far[b, view] = jnp.concatenate([high, high, low], axis=0)
                inner = stacked(across[:, :tile_cols].T, 1)
                if way == 0:
                    fwd_rows[view, b] = stacked(along[:, : tile_rows + 2 * HW], 0)
                    fwd_cols[view, b] = inner
                else:
                    rows_ref[b, :, view * tile_rows : (view + 1) * tile_rows] = stacked(along[:, :tile_rows], 0)
                    ends = ends + (pltpu.roll(beyond, 2 * HW * view, 1) if view else beyond)
                    cols_ref[view, b] = inner
        ends = jnp.concatenate([ends[:HW], ends[tile_rows - HW :]], axis=0)
        ends_ref[b] = stacked(ends[:, : 2 * HW * views], 0)
        later_far_ref[b] = fwd_far_ref[b]

    def plane(z, carry):
        b = band_ref[z]
        cells = stacked(cells_ref[z], 1)
        ends = halo(place_ref, even_ref[z], other_ref[z])
        for view in range(views):
            rows = fwd_rows[view, b]
            blurred = quarters(dot(rows[:, :tile_rows], cells)) + halves(dot(rows[:, tile_rows:], ends))
            blurred = quarters(dot(stacked(blurred, 0), fwd_cols[view, b]))
            blurred_ref[view, z] = blurred
            edge_ref[view, z, :HW] = blurred[:HW]
            edge_ref[view, z, HW:] = blurred[tile_rows - HW :]
        return carry

    lax.fori_loop(0, depth, plane, 0, unroll=2)


def late_kernel(
    band_ref, place_ref, turned_ref, far_ref, even_ref, other_ref, blurred_ref, out_ref, slab_ref, along_ref
):
    views, depth = blurred_ref.shape[:2]
    tile_rows = along_ref.shape[-1]
    weights = [turned_ref.at[view] for view in range(views)]
    far_products(place_ref, even_ref.at[0], other_ref.at[0], weights, slab_ref, [along_ref.at[v] for v in range(views)])
    for view in range(views):
        for z in range(depth):
            b = band_ref[z]
            parts = far_parts(along_ref, view, b, z)
            out_ref[view, z, : 4 * HW] = jnp.concatenate(parts[:2], axis=0)
            across = dot(jnp.concatenate(parts, axis=0), far_ref[b, view], ((0,), (0,)))
            ends = jnp.concatenate([across[:HW], across[tile_rows - HW :]], axis=0)
            out_ref[view, z, 4 * HW :] = (blurred_ref[view, z] + ends).astype(BF16)


def near_kernel(
    band_ref, place_ref, rows_ref, ends_ref, cols_ref, ratio_ref, even_ref, other_ref, out_ref, inner_ref, outer_ref
):
    views, depth, tile_rows, tile_cols = ratio_ref.shape

    def across(cells, weights):
        blurred = dot(cells, weights)
        return stacked(blurred[:, :tile_cols] + blurred[:, tile_cols:], 1)

    for z in range(depth):
        b = band_ref[z]
        for view in range(views):
            inner_ref[z, view * tile_rows : (view + 1) * tile_rows] = across(ratio_ref[view, z], cols_ref[view, b])
            ends = halo(place_ref, even_ref[view, z], other_ref[view, z])
            outer_ref[z, view * 2 * HW : (view + 1) * 2 * HW] = across(ends, cols_ref[view, b])
    for z in range(depth):
        b = band_ref[z]
        out_ref[z] = quarters(dot(rows_ref[b], inner_ref[z]))
        ends = quarters(dot(ends_ref[b], outer_ref[z]))
        out_ref[z, :HW] += ends[:HW]
        out_ref[z, tile_rows - HW :] += ends[HW:]


def far_kernel(
    band_ref, place_ref, turned_ref, far_ref, near_ref, even_ref, other_ref, estimate_ref, out_hbm,
    slab_ref, along_ref, out_ref, sems,
):
    views, bands = turned_ref.shape[:2]
    depth, tile_rows, tile_cols = near_ref.shape
    step = depth // sems.shape[0]
    for view in range(views):
        far_products(place_ref, even_ref.at[view], other_ref.at[view], [turned_ref.at[view]], slab_ref.at[view], [along_ref.at[view]])
    leave = []
    for z in range(depth):
        b = band_ref[z]
        parts = []
        for view in range(views):
            parts += far_parts(along_ref, view, b, z)
        across = far_ref[b].reshape(views * 6 * HW, tile_cols)
        total = near_ref[z] + dot(jnp.concatenate(parts, axis=0), across, ((0,), (0,)))
        out_ref[z] = estimate_ref[z] * (total * (1.0 / views))
        if z % step == step - 1:
            part = pl.ds(z - step + 1, step)
            leave.append(pltpu.make_async_copy(out_ref.at[part], out_hbm.at[part], sems.at[z // step]))
            leave[-1].start()
    for copy in leave:
        copy.wait()


def swap(first, second, axis, everyone=True):
    both = ("gx", "gy")
    rows, cols = (lax.axis_size(name) for name in both)
    count = lax.axis_size(axis)
    at = lambda p, q: p * cols + q
    partner = lambda i, begin: begin + ((i - begin) ^ 1)
    pairs = []
    for begin in range(2):
        found = []
        for p in range(rows):
            for q in range(cols):
                i = partner(p if axis == "gx" else q, begin)
                if 0 <= i < count:
                    found.append((at(p, q), at(i, q) if axis == "gx" else at(p, i)))
                elif everyone:
                    found.append((at(p, q), at(p, q ^ 1) if axis == "gx" else at(p ^ 1, q)))
        pairs.append(found)
    late = lax.ppermute(second, both, pairs[1])
    return lax.ppermute(first, both, pairs[0]), late


def place(count, at):
    return jnp.where(at == count - 1, at + LAST, at).reshape(1)


def body(estimate, measured, kernels, depth_band, group_shift, group_length):
    devices = lax.axis_size("gx") * lax.axis_size("gy")
    gx, gy = lax.axis_index("gx").astype(jnp.int32), lax.axis_index("gy").astype(jnp.int32)
    me = (gx * lax.axis_size("gy") + gy).reshape(1)
    place_x, place_y = (place(lax.axis_size(axis), at) for axis, at in (("gx", gx), ("gy", gy)))
    views, depth, tile_rows, tile_cols = measured.shape
    bands = kernels.shape[1]
    spare = tile_rows + 8
    like = jax.ShapeDtypeStruct
    whole = like(measured.shape, BF16)
    edge_cols = like((views, depth, 2 * HW, tile_rows), BF16)
    edge_rows = like((views, depth, HW, tile_cols), BF16)

    head, tail = estimate[:, :HW], estimate[:, tile_rows - HW :]
    even = gx % 2 == 0
    ex, ox = swap(jnp.where(even, tail, head), jnp.where(even, head, tail), "gx")
    outgoing = call(
        functools.partial(pack_kernel, devices),
        [SMEM, HBM, HBM, HBM],
        like((devices, views, CAP, depth, tile_cols), BF16),
        [
            pltpu.VMEM((views, spare, depth, tile_cols), BF16),
            pltpu.VMEM(measured.shape, BF16),
            pltpu.SMEM(group_shift.shape, jnp.int32),
            pltpu.SMEM(group_length.shape, jnp.int32),
            pltpu.SemaphoreType.DMA((2 * views + 2,)),
        ],
        HBM,
        60,
    )(me, group_shift, group_length, measured)
    outgoing = outgoing.reshape(devices * views * CAP, depth, tile_cols)
    outgoing, ex, ox, cells = lax.optimization_barrier((outgoing, ex, ox, estimate))
    arrived = lax.all_to_all(outgoing, ("gx", "gy"), split_axis=0, concat_axis=0, tiled=True)

    cols = call(cols_kernel, [VMEM], like(edge_cols.shape[1:], BF16))(cells)
    tiles = depth + depth * 2 * HW // tile_rows
    dense = lambda lead, *args: call(
        dense_slab_kernel, [SMEM] * 2 + [VMEM] * 3, (like((lead, tiles, HW, tile_rows), BF16),) * 2
    )(place_x, place_y, *args)
    ey, oy = swap(*dense(1, cols[None], ex, ox), "gy", everyone=False)

    norm = kernels / jnp.sum(kernels, axis=3, keepdims=True)
    tap_rows = jnp.stack([norm, norm[..., ::-1]])
    tap_rows = jnp.pad(tap_rows, ((0, 0),) * 4 + ((0, LANES - kernels.shape[3]),))
    turned_like = like((views, bands, 2 * tile_rows, 2 * tile_rows), BF16)
    far_like = like((bands, views, 6 * HW, tile_cols), BF16)
    blurred, edge, fwd_turned, fwd_far, later_far, rows_mat, ends_mat, cols_mat, turned_mat, far_mat = call(
        forward_kernel,
        [SMEM] * 2 + [VMEM] * 4,
        (
            like(measured.shape, F32),
            like((views, depth, 2 * HW, tile_cols), F32),
            turned_like,
            far_like,
            far_like,
            like((bands, 2 * tile_rows, views * tile_rows), BF16),
            like((bands, 4 * HW, views * 2 * HW), BF16),
            like((views, bands, tile_cols, 2 * tile_cols), BF16),
            turned_like,
            far_like,
        ),
        [
            pltpu.VMEM((views, bands, 2 * tile_rows, tile_rows + 2 * HW), BF16),
            pltpu.VMEM((views, bands, tile_cols, 2 * tile_cols), BF16),
        ],
    )(depth_band, place_x, tap_rows, cells, ex, ox)

    parts = call(
        late_kernel,
        [SMEM] * 2 + [VMEM] * 5,
        like((views, depth, 6 * HW, tile_rows), BF16),
        [
            pltpu.VMEM((depth * 2 * HW, 2 * tile_rows), BF16),
            pltpu.VMEM((views, bands, 2, depth * 2 * HW, tile_rows), BF16),
        ],
    )(depth_band, place_y, fwd_turned, fwd_far, ey, oy, edge)

    first, second = call(
        functools.partial(edges_kernel, devices, tile_rows),
        [SMEM] * 4 + [VMEM] * 2,
        (edge_rows, edge_rows),
        [pltpu.VMEM((views, 2, CAP * HW + 8, depth, tile_cols), F32)],
    )(me, place_x, group_shift, group_length, arrived, parts)
    ex, ox = swap(first, second, "gx")
    ratio, cols = call(
        functools.partial(unpack_kernel, devices),
        [SMEM] * 4 + [VMEM] * 4,
        (whole, edge_cols),
        [pltpu.VMEM((views, spare, depth, tile_cols), F32), pltpu.VMEM(measured.shape, BF16)],
    )(me, depth_band, group_shift, group_length, arrived, blurred, later_far, parts)
    ey, oy = swap(*dense(views, cols, ex, ox), "gy")
    near = call(
        near_kernel,
        [SMEM] * 2 + [VMEM] * 6,
        like(estimate.shape, F32),
        [
            pltpu.VMEM((depth, views * tile_rows, 2 * tile_cols), BF16),
            pltpu.VMEM((depth, views * 2 * HW, 2 * tile_cols), BF16),
        ],
    )(depth_band, place_x, rows_mat, ends_mat, cols_mat, ratio, ex, ox)
    return call(
        far_kernel,
        [SMEM] * 2 + [VMEM] * 6,
        like(estimate.shape, F32),
        [
            pltpu.VMEM((views, depth * 2 * HW, 2 * tile_rows), BF16),
            pltpu.VMEM((views, bands, 2, depth * 2 * HW, tile_rows), BF16),
            pltpu.VMEM(estimate.shape, F32),
            pltpu.SemaphoreType.DMA((4,)),
        ],
        HBM,
    )(depth_band, place_y, turned_mat, far_mat, near, ey, oy, estimate)


def solution(mesh):
    return jax.shard_map(
        body,
        mesh=mesh,
        in_specs=(P(None, "gx", "gy"), P(None, None, "gx", "gy"), P(), P(), P(), P()),
        out_specs=P(None, "gx", "gy"),
        check_vma=False,
    )
```

```python
import functools

import jax
import jax.numpy as jnp
from jax import lax
from jax.experimental import pallas as pl
from jax.experimental.pallas import tpu as pltpu
from jax.sharding import PartitionSpec as P

HW = 8
CAP = 3
LANES = 256
LAST = 2**20
F32 = jnp.float32
BF16 = jnp.bfloat16

VMEM = pl.BlockSpec(memory_space=pltpu.VMEM)
SMEM = pl.BlockSpec(memory_space=pltpu.SMEM)
HBM = pl.BlockSpec(memory_space=pltpu.HBM)
NN = ((1,), (0,))
NT = ((1,), (1,))


def call(kernel, ins, out_shape, scratch=(), out_space=VMEM, limit=16):
    return pl.pallas_call(
        kernel,
        in_specs=ins,
        out_specs=jax.tree.map(lambda _: out_space, out_shape),
        out_shape=out_shape,
        scratch_shapes=list(scratch),
        compiler_params=pltpu.CompilerParams(vmem_limit_bytes=limit * 2**20),
    )


def dot(a, b, dims=NN):
    return lax.dot_general(a, b, (dims, ((), ())), preferred_element_type=F32)


def split(x):
    high = x.astype(BF16)
    return high, (x - high.astype(F32)).astype(BF16)


def stacked(x, axis):
    return jnp.concatenate(split(x), axis=axis)


def halves(x):
    n = x.shape[0] // 2
    return x[:n] + x[n:]


def quarters(x):
    n, m = x.shape[0] // 2, x.shape[1] // 2
    return x[:n, :m] + (x[n:, :m] + x[:n, m:])


def is_odd(place_ref):
    return place_ref[0] % 2 == 1


def halo(place_ref, first, second):
    first, second = first.astype(F32), second.astype(F32)
    odd = is_odd(place_ref)
    after = jnp.where(place_ref[0] >= LAST, 0.0, jnp.where(odd, second, first))
    before = jnp.where(place_ref[0] == 0, 0.0, jnp.where(odd, first, second))
    return jnp.concatenate([after, before], axis=0).astype(BF16)


def edge_picker(cols):
    lane = lax.broadcasted_iota(jnp.int32, (2 * HW, cols), 1)
    sub = lax.broadcasted_iota(jnp.int32, (2 * HW, cols), 0)
    return (lane == jnp.where(sub < HW, sub, sub + cols - 2 * HW)).astype(BF16)


def pack_kernel(
    devices, me_ref, shift_hbm, length_hbm, measured_hbm, out_hbm,
    rows_ref, measured_ref, shift_ref, length_ref, sems,
):
    views, depth, tile_rows, tile_cols = measured_ref.shape
    groups = shift_ref.shape[1]
    loads = [pltpu.make_async_copy(measured_hbm.at[v], measured_ref.at[v], sems.at[v]) for v in range(views)]
    tables = [
        pltpu.make_async_copy(shift_hbm, shift_ref, sems.at[views]),
        pltpu.make_async_copy(length_hbm, length_ref, sems.at[views + 1]),
    ]
    for copy in tables + loads:
        copy.start()
    rows_ref[:, tile_rows:] = jnp.zeros((views, rows_ref.shape[1] - tile_rows) + rows_ref.shape[2:], BF16)
    lane = lax.broadcasted_iota(jnp.int32, (tile_cols, tile_cols), 1)
    sub = lax.broadcasted_iota(jnp.int32, (tile_cols, tile_cols), 0)
    turn = (lane + sub == tile_cols - 1).astype(BF16)
    me = me_ref[0]
    for view in range(views):
        loads[view].wait()
        for r0 in range(0, tile_rows, 16):
            x = measured_ref[view, :, r0 : r0 + 16, :]
            if view % 2 == 1:
                x = dot(x.reshape(depth * 16, tile_cols), turn).reshape(depth, 16, tile_cols)
            x = jnp.transpose(x.astype(F32), (1, 0, 2))
            rows_ref[view, r0 : r0 + 16] = x.astype(BF16)
        if view == 0:
            for copy in tables:
                copy.wait()

        def group(g, start, view=view):
            peer = lax.rem(me + shift_ref[view, g], devices)
            blocks = rows_ref.at[view, pl.ds(start, CAP)]
            pltpu.make_async_copy(blocks, out_hbm.at[peer, view], sems.at[views + 2 + view]).start()
            return start + length_ref[view, g]

        lax.fori_loop(0, groups, group, 0, unroll=True)
    for view in range(views):
        sent = out_hbm.at[pl.ds(0, groups), view]
        pltpu.make_async_copy(sent, sent, sems.at[views + 2 + view]).wait()


def cols_kernel(cells_ref, out_ref):
    pick = edge_picker(cells_ref.shape[-1])
    for z in range(cells_ref.shape[0]):
        out_ref[z] = dot(pick, cells_ref[z].astype(BF16), NT).astype(BF16)


def dense_slab_kernel(place_x_ref, place_y_ref, cols_ref, even_ref, other_ref, first_ref, second_ref):
    views, depth, _, tile_rows = cols_ref.shape
    count = tile_rows // (2 * HW)
    pick = edge_picker(even_ref.shape[-1])
    odd = is_odd(place_y_ref)
    for view in range(views):
        for i in range(first_ref.shape[1]):
            if i < depth:
                edge = cols_ref[view, i].astype(F32)
            else:
                planes = range((i - depth) * count, (i - depth + 1) * count)
                lead = () if len(even_ref.shape) == 3 else (view,)
                ends = [halo(place_x_ref, even_ref[*lead, z], other_ref[*lead, z]) for z in planes]
                edge = dot(pick, jnp.concatenate(ends, axis=0), NT)
            first_ref[view, i] = jnp.where(odd, edge[:HW], edge[HW:]).astype(BF16)
            second_ref[view, i] = jnp.where(odd, edge[HW:], edge[:HW]).astype(BF16)


def edges_kernel(
    devices, tile_rows, me_ref, place_ref, shift_ref, length_ref, arrived_ref, edge_ref, first_ref, second_ref, rows_ref
):
    views = edge_ref.shape[0]
    odd = is_odd(place_ref)
    groups = shift_ref.shape[1]
    me = me_ref[0]
    low = tile_rows - CAP * HW
    for view in range(views):
        ending = tile_rows - low
        for g in range(groups - HW, groups):
            ending = ending - length_ref[view, g]
        for side, (first, start) in enumerate(((0, 0), (groups - HW, ending))):
            for g in range(first, first + HW):
                source = lax.rem(me - shift_ref[view, g] + devices, devices)
                base = source * (views * CAP) + view * CAP
                for k in range(CAP):
                    rows_ref[view, side, start + k] = arrived_ref[base + k].astype(F32)
                start = start + length_ref[view, g]
        edge = edge_ref[view, :, 4 * HW :].astype(F32)
        head = jnp.transpose(rows_ref[view, 0, :HW], (1, 0, 2)) / edge[:, :HW]
        tail = rows_ref[view, 1, (CAP - 1) * HW : CAP * HW]
        tail = jnp.transpose(tail, (1, 0, 2)) / edge[:, HW:]
        first_ref[view] = jnp.where(odd, head, tail).astype(BF16)
        second_ref[view] = jnp.where(odd, tail, head).astype(BF16)


def unpack_kernel(
    devices, me_ref, band_ref, shift_ref, length_ref, arrived_ref, blurred_ref, far_ref, parts_ref,
    out_ref, cols_ref, rows_ref, forward_ref,
):
    views, depth, tile_rows, tile_cols = out_ref.shape
    groups = shift_ref.shape[1]
    me = me_ref[0]
    pick = edge_picker(tile_cols)
    for view in range(views):

        def group(g, start, view=view):
            source = lax.rem(me - shift_ref[view, g] + devices, devices)
            base = source * (views * CAP) + view * CAP
            for k in range(CAP):
                rows_ref[view, start + k] = arrived_ref[base + k].astype(F32)
            return start + length_ref[view, g]

        lax.fori_loop(0, groups, group, 0, unroll=True)
        for z in range(depth):
            parts = parts_ref[view, z, : 4 * HW]
            parts = jnp.concatenate([parts, parts[: 2 * HW]], axis=0)
            across = dot(parts, far_ref[band_ref[z], view], ((0,), (0,)))
            forward_ref[view, z] = (blurred_ref[view, z] + across).astype(BF16)
        for r0 in range(0, tile_rows, 16):
            x = jnp.transpose(rows_ref[view, r0 : r0 + 16], (1, 0, 2))
            forward = forward_ref[view, :, r0 : r0 + 16, :].astype(F32)
            out_ref[view, :, r0 : r0 + 16, :] = (x / forward).astype(BF16)
        for z in range(depth):
            cols_ref[view, z] = dot(pick, out_ref[view, z], NT).astype(BF16)


def band(taps, size):
    wide = jnp.broadcast_to(taps, (size, LANES))
    inner = pltpu.roll(wide, LANES - HW, 1, stride=1, stride_axis=0)
    before = pltpu.roll(wide, size + HW, 1, stride=1, stride_axis=0)
    lane = lax.broadcasted_iota(jnp.int32, (size, LANES), 1)
    return jnp.where(lane < size + HW, inner, jnp.where(lane < size + 2 * HW, before, 0.0))


def far_products(place_ref, even_ref, other_ref, weights, slab_ref, along_ref):
    depth = slab_ref.shape[0] // (2 * HW)
    tile_rows = slab_ref.shape[1] // 2
    count = tile_rows // (2 * HW)
    owner = lax.broadcasted_iota(jnp.int32, (2 * HW, tile_rows), 1) // (2 * HW)
    for z in range(depth):
        at = pl.ds(z * 2 * HW, 2 * HW)
        slab_ref[at, :tile_rows] = halo(place_ref, even_ref[z], other_ref[z])
        corners = halo(place_ref, even_ref[depth + z // count], other_ref[depth + z // count])
        slab_ref[at, tile_rows:] = jnp.where(owner == z % count, corners.astype(F32), 0.0).astype(BF16)
    for turned_ref, out_ref in zip(weights, along_ref):
        for b in range(turned_ref.shape[0]):
            along = dot(slab_ref[...], turned_ref[b])
            high, low = split(along[:, :tile_rows] + along[:, tile_rows:])
            out_ref[b, 0] = high
            out_ref[b, 1] = low


def far_parts(along_ref, view, b, z):
    at = pl.ds(z * 2 * HW, 2 * HW)
    high, low = along_ref[view, b, 0, at, :], along_ref[view, b, 1, at, :]
    return [high, low, high]


def forward_kernel(
    band_ref, place_ref, taps_ref, cells_ref, even_ref, other_ref,
    blurred_ref, edge_ref, fwd_turned_ref, fwd_far_ref, later_far_ref, rows_ref, ends_ref, cols_ref, turned_ref, far_ref, fwd_rows, fwd_cols,
):
    views, depth, tile_rows, tile_cols = blurred_ref.shape
    bands = taps_ref.shape[2]
    for b in range(bands):
        ends = jnp.zeros((tile_rows, LANES - tile_rows), F32)
        for view in range(views):
            for way in range(2):
                along = band(taps_ref[way, view, b, 0:1, :], tile_rows)
                across = band(taps_ref[way, view, b, 1:2, :], tile_cols)
                beyond = along[:, tile_rows:]
                turned, far = ((fwd_turned_ref, fwd_far_ref), (turned_ref, far_ref))[way]
                turned[view, b, :tile_rows] = stacked(along[:, :tile_rows].T, 1)
                corner = stacked(beyond.T[: 2 * HW], 1)
                for at in range(tile_rows, 2 * tile_rows, 2 * HW):
                    turned[view, b, at : at + 2 * HW] = corner
                high, low = split(across[:, tile_cols:].T[: 2 * HW])
                far[b, view] = jnp.concatenate([high, high, low], axis=0)
                inner = stacked(across[:, :tile_cols].T, 1)
                if way == 0:
                    fwd_rows[view, b] = stacked(along[:, : tile_rows + 2 * HW], 0)
                    fwd_cols[view, b] = inner
                else:
                    rows_ref[b, :, view * tile_rows : (view + 1) * tile_rows] = stacked(along[:, :tile_rows], 0)
                    ends = ends + (pltpu.roll(beyond, 2 * HW * view, 1) if view else beyond)
                    cols_ref[view, b] = inner
        ends = jnp.concatenate([ends[:HW], ends[tile_rows - HW :]], axis=0)
        ends_ref[b] = stacked(ends[:, : 2 * HW * views], 0)
        later_far_ref[b] = fwd_far_ref[b]

    def plane(z, carry):
        b = band_ref[z]
        cells = stacked(cells_ref[z], 1)
        ends = halo(place_ref, even_ref[z], other_ref[z])
        for view in range(views):
            rows = fwd_rows[view, b]
            blurred = quarters(dot(rows[:, :tile_rows], cells)) + halves(dot(rows[:, tile_rows:], ends))
            blurred = quarters(dot(stacked(blurred, 0), fwd_cols[view, b]))
            blurred_ref[view, z] = blurred
            edge_ref[view, z, :HW] = blurred[:HW]
            edge_ref[view, z, HW:] = blurred[tile_rows - HW :]
        return carry

    lax.fori_loop(0, depth, plane, 0, unroll=2)


def late_kernel(
    band_ref, place_ref, turned_ref, far_ref, even_ref, other_ref, blurred_ref, out_ref, slab_ref, along_ref
):
    views, depth = blurred_ref.shape[:2]
    tile_rows = along_ref.shape[-1]
    weights = [turned_ref.at[view] for view in range(views)]
    far_products(place_ref, even_ref.at[0], other_ref.at[0], weights, slab_ref, [along_ref.at[v] for v in range(views)])
    for view in range(views):
        for z in range(depth):
            b = band_ref[z]
            parts = far_parts(along_ref, view, b, z)
            out_ref[view, z, : 4 * HW] = jnp.concatenate(parts[:2], axis=0)
            across = dot(jnp.concatenate(parts, axis=0), far_ref[b, view], ((0,), (0,)))
            ends = jnp.concatenate([across[:HW], across[tile_rows - HW :]], axis=0)
            out_ref[view, z, 4 * HW :] = (blurred_ref[view, z] + ends).astype(BF16)


def near_kernel(
    band_ref, place_ref, rows_ref, ends_ref, cols_ref, ratio_ref, even_ref, other_ref, out_ref, inner_ref, outer_ref
):
    views, depth, tile_rows, tile_cols = ratio_ref.shape

    def across(cells, weights):
        blurred = dot(cells, weights)
        return stacked(blurred[:, :tile_cols] + blurred[:, tile_cols:], 1)

    for z in range(depth):
        b = band_ref[z]
        for view in range(views):
            inner_ref[z, view * tile_rows : (view + 1) * tile_rows] = across(ratio_ref[view, z], cols_ref[view, b])
            ends = halo(place_ref, even_ref[view, z], other_ref[view, z])
            outer_ref[z, view * 2 * HW : (view + 1) * 2 * HW] = across(ends, cols_ref[view, b])
    for z in range(depth):
        b = band_ref[z]
        out_ref[z] = quarters(dot(rows_ref[b], inner_ref[z]))
        ends = quarters(dot(ends_ref[b], outer_ref[z]))
        out_ref[z, :HW] += ends[:HW]
        out_ref[z, tile_rows - HW :] += ends[HW:]


def far_kernel(
    band_ref, place_ref, turned_ref, far_ref, near_ref, even_ref, other_ref, estimate_ref, out_hbm,
    slab_ref, along_ref, out_ref, sems,
):
    views, bands = turned_ref.shape[:2]
    depth, tile_rows, tile_cols = near_ref.shape
    step = depth // sems.shape[0]
    for view in range(views):
        far_products(place_ref, even_ref.at[view], other_ref.at[view], [turned_ref.at[view]], slab_ref.at[view], [along_ref.at[view]])
    leave = []
    for z in range(depth):
        b = band_ref[z]
        parts = []
        for view in range(views):
            parts += far_parts(along_ref, view, b, z)
        across = far_ref[b].reshape(views * 6 * HW, tile_cols)
        total = near_ref[z] + dot(jnp.concatenate(parts, axis=0), across, ((0,), (0,)))
        out_ref[z] = estimate_ref[z] * (total * (1.0 / views))
        if z % step == step - 1:
            part = pl.ds(z - step + 1, step)
            leave.append(pltpu.make_async_copy(out_ref.at[part], out_hbm.at[part], sems.at[z // step]))
            leave[-1].start()
    for copy in leave:
        copy.wait()


def swap(first, second, axis):
    both = ("gx", "gy")
    rows, cols = (lax.axis_size(name) for name in both)
    count = lax.axis_size(axis)
    at = lambda p, q: p * cols + q
    partner = lambda i, begin: begin + ((i - begin) ^ 1)
    pairs = []
    for begin in range(2):
        found = []
        for p in range(rows):
            for q in range(cols):
                i = partner(p if axis == "gx" else q, begin)
                if 0 <= i < count:
                    found.append((at(p, q), at(i, q) if axis == "gx" else at(p, i)))
                else:
                    found.append((at(p, q), at(p, q ^ 1) if axis == "gx" else at(p ^ 1, q)))
        pairs.append(found)
    late = lax.ppermute(second, both, pairs[1])
    return lax.ppermute(first, both, pairs[0]), late


def place(count, at):
    return jnp.where(at == count - 1, at + LAST, at).reshape(1)


def body(estimate, measured, kernels, depth_band, group_shift, group_length):
    devices = lax.axis_size("gx") * lax.axis_size("gy")
    gx, gy = lax.axis_index("gx").astype(jnp.int32), lax.axis_index("gy").astype(jnp.int32)
    me = (gx * lax.axis_size("gy") + gy).reshape(1)
    place_x, place_y = (place(lax.axis_size(axis), at) for axis, at in (("gx", gx), ("gy", gy)))
    views, depth, tile_rows, tile_cols = measured.shape
    bands = kernels.shape[1]
    spare = tile_rows + 8
    like = jax.ShapeDtypeStruct
    whole = like(measured.shape, BF16)
    edge_cols = like((views, depth, 2 * HW, tile_rows), BF16)
    edge_rows = like((views, depth, HW, tile_cols), BF16)

    head, tail = estimate[:, :HW], estimate[:, tile_rows - HW :]
    even = gx % 2 == 0
    ex, ox = swap(jnp.where(even, tail, head), jnp.where(even, head, tail), "gx")
    outgoing = call(
        functools.partial(pack_kernel, devices),
        [SMEM, HBM, HBM, HBM],
        like((devices, views, CAP, depth, tile_cols), BF16),
        [
            pltpu.VMEM((views, spare, depth, tile_cols), BF16),
            pltpu.VMEM(measured.shape, BF16),
            pltpu.SMEM(group_shift.shape, jnp.int32),
            pltpu.SMEM(group_length.shape, jnp.int32),
            pltpu.SemaphoreType.DMA((2 * views + 2,)),
        ],
        HBM,
        60,
    )(me, group_shift, group_length, measured)
    outgoing = outgoing.reshape(devices * views * CAP, depth, tile_cols)
    outgoing, ex, ox, cells = lax.optimization_barrier((outgoing, ex, ox, estimate))
    arrived = lax.all_to_all(outgoing, ("gx", "gy"), split_axis=0, concat_axis=0, tiled=True)

    cols = call(cols_kernel, [VMEM], like(edge_cols.shape[1:], BF16))(cells)
    tiles = depth + depth * 2 * HW // tile_rows
    dense = lambda lead, *args: call(
        dense_slab_kernel, [SMEM] * 2 + [VMEM] * 3, (like((lead, tiles, HW, tile_rows), BF16),) * 2
    )(place_x, place_y, *args)
    ey, oy = swap(*dense(1, cols[None], ex, ox), "gy")

    norm = kernels / jnp.sum(kernels, axis=3, keepdims=True)
    tap_rows = jnp.stack([norm, norm[..., ::-1]])
    tap_rows = jnp.pad(tap_rows, ((0, 0),) * 4 + ((0, LANES - kernels.shape[3]),))
    turned_like = like((views, bands, 2 * tile_rows, 2 * tile_rows), BF16)
    far_like = like((bands, views, 6 * HW, tile_cols), BF16)
    blurred, edge, fwd_turned, fwd_far, later_far, rows_mat, ends_mat, cols_mat, turned_mat, far_mat = call(
        forward_kernel,
        [SMEM] * 2 + [VMEM] * 4,
        (
            like(measured.shape, F32),
            like((views, depth, 2 * HW, tile_cols), F32),
            turned_like,
            far_like,
            far_like,
            like((bands, 2 * tile_rows, views * tile_rows), BF16),
            like((bands, 4 * HW, views * 2 * HW), BF16),
            like((views, bands, tile_cols, 2 * tile_cols), BF16),
            turned_like,
            far_like,
        ),
        [
            pltpu.VMEM((views, bands, 2 * tile_rows, tile_rows + 2 * HW), BF16),
            pltpu.VMEM((views, bands, tile_cols, 2 * tile_cols), BF16),
        ],
    )(depth_band, place_x, tap_rows, cells, ex, ox)

    parts = call(
        late_kernel,
        [SMEM] * 2 + [VMEM] * 5,
        like((views, depth, 6 * HW, tile_rows), BF16),
        [
            pltpu.VMEM((depth * 2 * HW, 2 * tile_rows), BF16),
            pltpu.VMEM((views, bands, 2, depth * 2 * HW, tile_rows), BF16),
        ],
    )(depth_band, place_y, fwd_turned, fwd_far, ey, oy, edge)

    first, second = call(
        functools.partial(edges_kernel, devices, tile_rows),
        [SMEM] * 4 + [VMEM] * 2,
        (edge_rows, edge_rows),
        [pltpu.VMEM((views, 2, CAP * HW + 8, depth, tile_cols), F32)],
    )(me, place_x, group_shift, group_length, arrived, parts)
    ex, ox = swap(first, second, "gx")
    ratio, cols = call(
        functools.partial(unpack_kernel, devices),
        [SMEM] * 4 + [VMEM] * 4,
        (whole, edge_cols),
        [pltpu.VMEM((views, spare, depth, tile_cols), F32), pltpu.VMEM(measured.shape, BF16)],
    )(me, depth_band, group_shift, group_length, arrived, blurred, later_far, parts)
    ey, oy = swap(*dense(views, cols, ex, ox), "gy")
    near = call(
        near_kernel,
        [SMEM] * 2 + [VMEM] * 6,
        like(estimate.shape, F32),
        [
            pltpu.VMEM((depth, views * tile_rows, 2 * tile_cols), BF16),
            pltpu.VMEM((depth, views * 2 * HW, 2 * tile_cols), BF16),
        ],
    )(depth_band, place_x, rows_mat, ends_mat, cols_mat, ratio, ex, ox)
    return call(
        far_kernel,
        [SMEM] * 2 + [VMEM] * 6,
        like(estimate.shape, F32),
        [
            pltpu.VMEM((views, depth * 2 * HW, 2 * tile_rows), BF16),
            pltpu.VMEM((views, bands, 2, depth * 2 * HW, tile_rows), BF16),
            pltpu.VMEM(estimate.shape, F32),
            pltpu.SemaphoreType.DMA((4,)),
        ],
        HBM,
    )(depth_band, place_y, turned_mat, far_mat, near, ey, oy, estimate)


def solution(mesh):
    return jax.shard_map(
        body,
        mesh=mesh,
        in_specs=(P(None, "gx", "gy"), P(None, None, "gx", "gy"), P(), P(), P(), P()),
        out_specs=P(None, "gx", "gy"),
        check_vma=False,
    )
```

```python
import functools

import jax
import jax.numpy as jnp
from jax import lax
from jax.experimental import pallas as pl
from jax.experimental.pallas import tpu as pltpu
from jax.sharding import PartitionSpec as P

HW = 8
CAP = 3
LANES = 256
LAST = 2**20
F32 = jnp.float32
BF16 = jnp.bfloat16

VMEM = pl.BlockSpec(memory_space=pltpu.VMEM)
SMEM = pl.BlockSpec(memory_space=pltpu.SMEM)
HBM = pl.BlockSpec(memory_space=pltpu.HBM)
NN = ((1,), (0,))
NT = ((1,), (1,))


def call(kernel, ins, out_shape, scratch=(), out_space=VMEM, limit=16):
    return pl.pallas_call(
        kernel,
        in_specs=ins,
        out_specs=jax.tree.map(lambda _: out_space, out_shape),
        out_shape=out_shape,
        scratch_shapes=list(scratch),
        compiler_params=pltpu.CompilerParams(vmem_limit_bytes=limit * 2**20),
    )


def dot(a, b, dims=NN):
    return lax.dot_general(a, b, (dims, ((), ())), preferred_element_type=F32)


def split(x):
    high = x.astype(BF16)
    return high, (x - high.astype(F32)).astype(BF16)


def stacked(x, axis):
    return jnp.concatenate(split(x), axis=axis)


def halves(x):
    n = x.shape[0] // 2
    return x[:n] + x[n:]


def quarters(x):
    n, m = x.shape[0] // 2, x.shape[1] // 2
    return x[:n, :m] + (x[n:, :m] + x[:n, m:])


def is_odd(place_ref):
    return place_ref[0] % 2 == 1


def halo(place_ref, first, second):
    first, second = first.astype(F32), second.astype(F32)
    odd = is_odd(place_ref)
    after = jnp.where(place_ref[0] >= LAST, 0.0, jnp.where(odd, second, first))
    before = jnp.where(place_ref[0] == 0, 0.0, jnp.where(odd, first, second))
    return jnp.concatenate([after, before], axis=0).astype(BF16)


def edge_picker(cols):
    lane = lax.broadcasted_iota(jnp.int32, (2 * HW, cols), 1)
    sub = lax.broadcasted_iota(jnp.int32, (2 * HW, cols), 0)
    return (lane == jnp.where(sub < HW, sub, sub + cols - 2 * HW)).astype(BF16)


def pack_kernel(
    devices, me_ref, shift_hbm, length_hbm, measured_hbm, out_hbm,
    rows_ref, measured_ref, shift_ref, length_ref, sems,
):
    views, depth, tile_rows, tile_cols = measured_ref.shape
    groups = shift_ref.shape[1]
    loads = [pltpu.make_async_copy(measured_hbm.at[v], measured_ref.at[v], sems.at[v]) for v in range(views)]
    tables = [
        pltpu.make_async_copy(shift_hbm, shift_ref, sems.at[views]),
        pltpu.make_async_copy(length_hbm, length_ref, sems.at[views + 1]),
    ]
    for copy in tables + loads:
        copy.start()
    rows_ref[:, tile_rows:] = jnp.zeros((views, rows_ref.shape[1] - tile_rows) + rows_ref.shape[2:], BF16)
    lane = lax.broadcasted_iota(jnp.int32, (tile_cols, tile_cols), 1)
    sub = lax.broadcasted_iota(jnp.int32, (tile_cols, tile_cols), 0)
    turn = (lane + sub == tile_cols - 1).astype(BF16)
    me = me_ref[0]

    def leave(view, begin, end, start):
        for g in range(begin, end):
            peer = lax.rem(me + shift_ref[view, g], devices)
            blocks = rows_ref.at[view, pl.ds(start, CAP)]
            pltpu.make_async_copy(blocks, out_hbm.at[peer, view], sems.at[views + 2 + view]).start()
            start = start + length_ref[view, g]
        return start

    share = groups * 16 // tile_rows
    for view in range(views):
        loads[view].wait()
        start = 0
        for r0 in range(0, tile_rows, 16):
            x = measured_ref[view, :, r0 : r0 + 16, :]
            if view % 2 == 1:
                x = dot(x.reshape(depth * 16, tile_cols), turn).reshape(depth, 16, tile_cols)
            x = jnp.transpose(x.astype(F32), (1, 0, 2))
            rows_ref[view, r0 : r0 + 16] = x.astype(BF16)
            if view > 0:
                at = r0 // 16 * share
                start = leave(view - 1, at, at + share, start)
        if view == 0:
            for copy in tables:
                copy.wait()
    leave(views - 1, 0, groups, 0)
    for view in range(views):
        sent = out_hbm.at[pl.ds(0, groups), view]
        pltpu.make_async_copy(sent, sent, sems.at[views + 2 + view]).wait()


def cols_kernel(cells_ref, out_ref):
    pick = edge_picker(cells_ref.shape[-1])
    for z in range(cells_ref.shape[0]):
        out_ref[z] = dot(pick, cells_ref[z].astype(BF16), NT).astype(BF16)


def dense_slab_kernel(place_x_ref, place_y_ref, cols_ref, even_ref, other_ref, first_ref, second_ref):
    views, depth, _, tile_rows = cols_ref.shape
    count = tile_rows // (2 * HW)
    pick = edge_picker(even_ref.shape[-1])
    odd = is_odd(place_y_ref)
    for view in range(views):
        for i in range(first_ref.shape[1]):
            if i < depth:
                edge = cols_ref[view, i].astype(F32)
            else:
                planes = range((i - depth) * count, (i - depth + 1) * count)
                lead = () if len(even_ref.shape) == 3 else (view,)
                ends = [halo(place_x_ref, even_ref[*lead, z], other_ref[*lead, z]) for z in planes]
                edge = dot(pick, jnp.concatenate(ends, axis=0), NT)
            first_ref[view, i] = jnp.where(odd, edge[:HW], edge[HW:]).astype(BF16)
            second_ref[view, i] = jnp.where(odd, edge[HW:], edge[:HW]).astype(BF16)


def edges_kernel(
    devices, tile_rows, me_ref, place_ref, shift_ref, length_ref, arrived_ref, edge_ref, first_ref, second_ref, rows_ref
):
    views = edge_ref.shape[0]
    odd = is_odd(place_ref)
    groups = shift_ref.shape[1]
    me = me_ref[0]
    low = tile_rows - CAP * HW
    for view in range(views):
        ending = tile_rows - low
        for g in range(groups - HW, groups):
            ending = ending - length_ref[view, g]
        for side, (first, start) in enumerate(((0, 0), (groups - HW, ending))):
            for g in range(first, first + HW):
                source = lax.rem(me - shift_ref[view, g] + devices, devices)
                base = source * (views * CAP) + view * CAP
                for k in range(CAP):
                    rows_ref[view, side, start + k] = arrived_ref[base + k].astype(F32)
                start = start + length_ref[view, g]
        edge = edge_ref[view, :, 4 * HW :].astype(F32)
        head = jnp.transpose(rows_ref[view, 0, :HW], (1, 0, 2)) / edge[:, :HW]
        tail = rows_ref[view, 1, (CAP - 1) * HW : CAP * HW]
        tail = jnp.transpose(tail, (1, 0, 2)) / edge[:, HW:]
        first_ref[view] = jnp.where(odd, head, tail).astype(BF16)
        second_ref[view] = jnp.where(odd, tail, head).astype(BF16)


def unpack_kernel(
    devices, me_ref, band_ref, shift_ref, length_ref, arrived_ref, blurred_ref, far_ref, parts_ref,
    out_ref, cols_ref, rows_ref, forward_ref,
):
    views, depth, tile_rows, tile_cols = out_ref.shape
    groups = shift_ref.shape[1]
    me = me_ref[0]
    pick = edge_picker(tile_cols)
    for view in range(views):

        def group(g, start, view=view):
            source = lax.rem(me - shift_ref[view, g] + devices, devices)
            base = source * (views * CAP) + view * CAP
            for k in range(CAP):
                rows_ref[view, start + k] = arrived_ref[base + k].astype(F32)
            return start + length_ref[view, g]

        lax.fori_loop(0, groups, group, 0, unroll=True)
        for z in range(depth):
            parts = parts_ref[view, z, : 4 * HW]
            parts = jnp.concatenate([parts, parts[: 2 * HW]], axis=0)
            across = dot(parts, far_ref[band_ref[z], view], ((0,), (0,)))
            forward_ref[view, z] = (blurred_ref[view, z] + across).astype(BF16)
        for r0 in range(0, tile_rows, 16):
            x = jnp.transpose(rows_ref[view, r0 : r0 + 16], (1, 0, 2))
            forward = forward_ref[view, :, r0 : r0 + 16, :].astype(F32)
            out_ref[view, :, r0 : r0 + 16, :] = (x / forward).astype(BF16)
        for z in range(depth):
            cols_ref[view, z] = dot(pick, out_ref[view, z], NT).astype(BF16)


def band(taps, size):
    wide = jnp.broadcast_to(taps, (size, LANES))
    inner = pltpu.roll(wide, LANES - HW, 1, stride=1, stride_axis=0)
    before = pltpu.roll(wide, size + HW, 1, stride=1, stride_axis=0)
    lane = lax.broadcasted_iota(jnp.int32, (size, LANES), 1)
    return jnp.where(lane < size + HW, inner, jnp.where(lane < size + 2 * HW, before, 0.0))


def far_products(place_ref, even_ref, other_ref, weights, slab_ref, along_ref):
    depth = slab_ref.shape[0] // (2 * HW)
    tile_rows = slab_ref.shape[1] // 2
    count = tile_rows // (2 * HW)
    owner = lax.broadcasted_iota(jnp.int32, (2 * HW, tile_rows), 1) // (2 * HW)
    for z in range(depth):
        at = pl.ds(z * 2 * HW, 2 * HW)
        slab_ref[at, :tile_rows] = halo(place_ref, even_ref[z], other_ref[z])
        corners = halo(place_ref, even_ref[depth + z // count], other_ref[depth + z // count])
        slab_ref[at, tile_rows:] = jnp.where(owner == z % count, corners.astype(F32), 0.0).astype(BF16)
    for turned_ref, out_ref in zip(weights, along_ref):
        for b in range(turned_ref.shape[0]):
            along = dot(slab_ref[...], turned_ref[b])
            high, low = split(along[:, :tile_rows] + along[:, tile_rows:])
            out_ref[b, 0] = high
            out_ref[b, 1] = low


def far_parts(along_ref, view, b, z):
    at = pl.ds(z * 2 * HW, 2 * HW)
    high, low = along_ref[view, b, 0, at, :], along_ref[view, b, 1, at, :]
    return [high, low, high]


def forward_kernel(
    band_ref, place_ref, taps_ref, cells_ref, even_ref, other_ref,
    blurred_ref, edge_ref, fwd_turned_ref, fwd_far_ref, later_far_ref, rows_ref, ends_ref, cols_ref, turned_ref, far_ref, fwd_rows, fwd_cols,
):
    views, depth, tile_rows, tile_cols = blurred_ref.shape
    bands = taps_ref.shape[2]
    for b in range(bands):
        ends = jnp.zeros((tile_rows, LANES - tile_rows), F32)
        for view in range(views):
            for way in range(2):
                along = band(taps_ref[way, view, b, 0:1, :], tile_rows)
                across = band(taps_ref[way, view, b, 1:2, :], tile_cols)
                beyond = along[:, tile_rows:]
                turned, far = ((fwd_turned_ref, fwd_far_ref), (turned_ref, far_ref))[way]
                turned[view, b, :tile_rows] = stacked(along[:, :tile_rows].T, 1)
                corner = stacked(beyond.T[: 2 * HW], 1)
                for at in range(tile_rows, 2 * tile_rows, 2 * HW):
                    turned[view, b, at : at + 2 * HW] = corner
                high, low = split(across[:, tile_cols:].T[: 2 * HW])
                far[b, view] = jnp.concatenate([high, high, low], axis=0)
                inner = stacked(across[:, :tile_cols].T, 1)
                if way == 0:
                    fwd_rows[view, b] = stacked(along[:, : tile_rows + 2 * HW], 0)
                    fwd_cols[view, b] = inner
                else:
                    rows_ref[b, :, view * tile_rows : (view + 1) * tile_rows] = stacked(along[:, :tile_rows], 0)
                    ends = ends + (pltpu.roll(beyond, 2 * HW * view, 1) if view else beyond)
                    cols_ref[view, b] = inner
        ends = jnp.concatenate([ends[:HW], ends[tile_rows - HW :]], axis=0)
        ends_ref[b] = stacked(ends[:, : 2 * HW * views], 0)
        later_far_ref[b] = fwd_far_ref[b]

    def plane(z, carry):
        b = band_ref[z]
        cells = stacked(cells_ref[z], 1)
        ends = halo(place_ref, even_ref[z], other_ref[z])
        for view in range(views):
            rows = fwd_rows[view, b]
            blurred = quarters(dot(rows[:, :tile_rows], cells)) + halves(dot(rows[:, tile_rows:], ends))
            blurred = quarters(dot(stacked(blurred, 0), fwd_cols[view, b]))
            blurred_ref[view, z] = blurred
            edge_ref[view, z, :HW] = blurred[:HW]
            edge_ref[view, z, HW:] = blurred[tile_rows - HW :]
        return carry

    lax.fori_loop(0, depth, plane, 0, unroll=2)


def late_kernel(
    band_ref, place_ref, turned_ref, far_ref, even_ref, other_ref, blurred_ref, out_ref, slab_ref, along_ref
):
    views, depth = blurred_ref.shape[:2]
    tile_rows = along_ref.shape[-1]
    weights = [turned_ref.at[view] for view in range(views)]
    far_products(place_ref, even_ref.at[0], other_ref.at[0], weights, slab_ref, [along_ref.at[v] for v in range(views)])
    for view in range(views):
        for z in range(depth):
            b = band_ref[z]
            parts = far_parts(along_ref, view, b, z)
            out_ref[view, z, : 4 * HW] = jnp.concatenate(parts[:2], axis=0)
            across = dot(jnp.concatenate(parts, axis=0), far_ref[b, view], ((0,), (0,)))
            ends = jnp.concatenate([across[:HW], across[tile_rows - HW :]], axis=0)
            out_ref[view, z, 4 * HW :] = (blurred_ref[view, z] + ends).astype(BF16)


def near_kernel(
    band_ref, place_ref, rows_ref, ends_ref, cols_ref, ratio_ref, even_ref, other_ref, out_ref, inner_ref, outer_ref
):
    views, depth, tile_rows, tile_cols = ratio_ref.shape

    def across(cells, weights):
        blurred = dot(cells, weights)
        return stacked(blurred[:, :tile_cols] + blurred[:, tile_cols:], 1)

    for z in range(depth):
        b = band_ref[z]
        for view in range(views):
            inner_ref[z, view * tile_rows : (view + 1) * tile_rows] = across(ratio_ref[view, z], cols_ref[view, b])
            ends = halo(place_ref, even_ref[view, z], other_ref[view, z])
            outer_ref[z, view * 2 * HW : (view + 1) * 2 * HW] = across(ends, cols_ref[view, b])
    for z in range(depth):
        b = band_ref[z]
        out_ref[z] = quarters(dot(rows_ref[b], inner_ref[z]))
        ends = quarters(dot(ends_ref[b], outer_ref[z]))
        out_ref[z, :HW] += ends[:HW]
        out_ref[z, tile_rows - HW :] += ends[HW:]


def far_kernel(
    band_ref, place_ref, turned_ref, far_ref, near_ref, even_ref, other_ref, estimate_ref, out_hbm,
    slab_ref, along_ref, out_ref, sems,
):
    views, bands = turned_ref.shape[:2]
    depth, tile_rows, tile_cols = near_ref.shape
    step = depth // sems.shape[0]
    for view in range(views):
        far_products(place_ref, even_ref.at[view], other_ref.at[view], [turned_ref.at[view]], slab_ref.at[view], [along_ref.at[view]])
    leave = []
    for z in range(depth):
        b = band_ref[z]
        parts = []
        for view in range(views):
            parts += far_parts(along_ref, view, b, z)
        across = far_ref[b].reshape(views * 6 * HW, tile_cols)
        total = near_ref[z] + dot(jnp.concatenate(parts, axis=0), across, ((0,), (0,)))
        out_ref[z] = estimate_ref[z] * (total * (1.0 / views))
        if z % step == step - 1:
            part = pl.ds(z - step + 1, step)
            leave.append(pltpu.make_async_copy(out_ref.at[part], out_hbm.at[part], sems.at[z // step]))
            leave[-1].start()
    for copy in leave:
        copy.wait()


def swap(first, second, axis, everyone=True):
    both = ("gx", "gy")
    rows, cols = (lax.axis_size(name) for name in both)
    count = lax.axis_size(axis)
    at = lambda p, q: p * cols + q
    partner = lambda i, begin: begin + ((i - begin) ^ 1)
    pairs = []
    for begin in range(2):
        found = []
        for p in range(rows):
            for q in range(cols):
                i = partner(p if axis == "gx" else q, begin)
                if 0 <= i < count:
                    found.append((at(p, q), at(i, q) if axis == "gx" else at(p, i)))
                elif everyone:
                    found.append((at(p, q), at(p, q ^ 1) if axis == "gx" else at(p ^ 1, q)))
        pairs.append(found)
    late = lax.ppermute(second, both, pairs[1])
    return lax.ppermute(first, both, pairs[0]), late


def place(count, at):
    return jnp.where(at == count - 1, at + LAST, at).reshape(1)


def body(estimate, measured, kernels, depth_band, group_shift, group_length):
    devices = lax.axis_size("gx") * lax.axis_size("gy")
    gx, gy = lax.axis_index("gx").astype(jnp.int32), lax.axis_index("gy").astype(jnp.int32)
    me = (gx * lax.axis_size("gy") + gy).reshape(1)
    place_x, place_y = (place(lax.axis_size(axis), at) for axis, at in (("gx", gx), ("gy", gy)))
    views, depth, tile_rows, tile_cols = measured.shape
    bands = kernels.shape[1]
    spare = tile_rows + 8
    like = jax.ShapeDtypeStruct
    whole = like(measured.shape, BF16)
    edge_cols = like((views, depth, 2 * HW, tile_rows), BF16)
    edge_rows = like((views, depth, HW, tile_cols), BF16)

    head, tail = estimate[:, :HW], estimate[:, tile_rows - HW :]
    even = gx % 2 == 0
    ex, ox = swap(jnp.where(even, tail, head), jnp.where(even, head, tail), "gx")
    outgoing = call(
        functools.partial(pack_kernel, devices),
        [SMEM, HBM, HBM, HBM],
        like((devices, views, CAP, depth, tile_cols), BF16),
        [
            pltpu.VMEM((views, spare, depth, tile_cols), BF16),
            pltpu.VMEM(measured.shape, BF16),
            pltpu.SMEM(group_shift.shape, jnp.int32),
            pltpu.SMEM(group_length.shape, jnp.int32),
            pltpu.SemaphoreType.DMA((2 * views + 2,)),
        ],
        HBM,
        60,
    )(me, group_shift, group_length, measured)
    outgoing = outgoing.reshape(devices * views * CAP, depth, tile_cols)
    outgoing, ex, ox, cells = lax.optimization_barrier((outgoing, ex, ox, estimate))
    arrived = lax.all_to_all(outgoing, ("gx", "gy"), split_axis=0, concat_axis=0, tiled=True)

    cols = call(cols_kernel, [VMEM], like(edge_cols.shape[1:], BF16))(cells)
    tiles = depth + depth * 2 * HW // tile_rows
    dense = lambda lead, *args: call(
        dense_slab_kernel, [SMEM] * 2 + [VMEM] * 3, (like((lead, tiles, HW, tile_rows), BF16),) * 2
    )(place_x, place_y, *args)
    ey, oy = swap(*dense(1, cols[None], ex, ox), "gy", everyone=False)

    norm = kernels / jnp.sum(kernels, axis=3, keepdims=True)
    tap_rows = jnp.stack([norm, norm[..., ::-1]])
    tap_rows = jnp.pad(tap_rows, ((0, 0),) * 4 + ((0, LANES - kernels.shape[3]),))
    turned_like = like((views, bands, 2 * tile_rows, 2 * tile_rows), BF16)
    far_like = like((bands, views, 6 * HW, tile_cols), BF16)
    blurred, edge, fwd_turned, fwd_far, later_far, rows_mat, ends_mat, cols_mat, turned_mat, far_mat = call(
        forward_kernel,
        [SMEM] * 2 + [VMEM] * 4,
        (
            like(measured.shape, F32),
            like((views, depth, 2 * HW, tile_cols), F32),
            turned_like,
            far_like,
            far_like,
            like((bands, 2 * tile_rows, views * tile_rows), BF16),
            like((bands, 4 * HW, views * 2 * HW), BF16),
            like((views, bands, tile_cols, 2 * tile_cols), BF16),
            turned_like,
            far_like,
        ),
        [
            pltpu.VMEM((views, bands, 2 * tile_rows, tile_rows + 2 * HW), BF16),
            pltpu.VMEM((views, bands, tile_cols, 2 * tile_cols), BF16),
        ],
    )(depth_band, place_x, tap_rows, cells, ex, ox)

    parts = call(
        late_kernel,
        [SMEM] * 2 + [VMEM] * 5,
        like((views, depth, 6 * HW, tile_rows), BF16),
        [
            pltpu.VMEM((depth * 2 * HW, 2 * tile_rows), BF16),
            pltpu.VMEM((views, bands, 2, depth * 2 * HW, tile_rows), BF16),
        ],
    )(depth_band, place_y, fwd_turned, fwd_far, ey, oy, edge)

    first, second = call(
        functools.partial(edges_kernel, devices, tile_rows),
        [SMEM] * 4 + [VMEM] * 2,
        (edge_rows, edge_rows),
        [pltpu.VMEM((views, 2, CAP * HW + 8, depth, tile_cols), F32)],
    )(me, place_x, group_shift, group_length, arrived, parts)
    ex, ox = swap(first, second, "gx")
    ratio, cols = call(
        functools.partial(unpack_kernel, devices),
        [SMEM] * 4 + [VMEM] * 4,
        (whole, edge_cols),
        [pltpu.VMEM((views, spare, depth, tile_cols), F32), pltpu.VMEM(measured.shape, BF16)],
    )(me, depth_band, group_shift, group_length, arrived, blurred, later_far, parts)
    ey, oy = swap(*dense(views, cols, ex, ox), "gy")
    near = call(
        near_kernel,
        [SMEM] * 2 + [VMEM] * 6,
        like(estimate.shape, F32),
        [
            pltpu.VMEM((depth, views * tile_rows, 2 * tile_cols), BF16),
            pltpu.VMEM((depth, views * 2 * HW, 2 * tile_cols), BF16),
        ],
    )(depth_band, place_x, rows_mat, ends_mat, cols_mat, ratio, ex, ox)
    return call(
        far_kernel,
        [SMEM] * 2 + [VMEM] * 6,
        like(estimate.shape, F32),
        [
            pltpu.VMEM((views, depth * 2 * HW, 2 * tile_rows), BF16),
            pltpu.VMEM((views, bands, 2, depth * 2 * HW, tile_rows), BF16),
            pltpu.VMEM(estimate.shape, F32),
            pltpu.SemaphoreType.DMA((4,)),
        ],
        HBM,
    )(depth_band, place_y, turned_mat, far_mat, near, ey, oy, estimate)


def solution(mesh):
    return jax.shard_map(
        body,
        mesh=mesh,
        in_specs=(P(None, "gx", "gy"), P(None, None, "gx", "gy"), P(), P(), P(), P()),
        out_specs=P(None, "gx", "gy"),
        check_vma=False,
    )
```

```python
import functools

import jax
import jax.numpy as jnp
from jax import lax
from jax.experimental import pallas as pl
from jax.experimental.pallas import tpu as pltpu
from jax.sharding import PartitionSpec as P

HW = 8
CAP = 3
LANES = 256
LAST = 2**20
F32 = jnp.float32
BF16 = jnp.bfloat16

VMEM = pl.BlockSpec(memory_space=pltpu.VMEM)
SMEM = pl.BlockSpec(memory_space=pltpu.SMEM)
HBM = pl.BlockSpec(memory_space=pltpu.HBM)
NN = ((1,), (0,))
NT = ((1,), (1,))


def call(kernel, ins, out_shape, scratch=(), out_space=VMEM, limit=16):
    return pl.pallas_call(
        kernel,
        in_specs=ins,
        out_specs=jax.tree.map(lambda _: out_space, out_shape),
        out_shape=out_shape,
        scratch_shapes=list(scratch),
        compiler_params=pltpu.CompilerParams(vmem_limit_bytes=limit * 2**20),
    )


def dot(a, b, dims=NN):
    return lax.dot_general(a, b, (dims, ((), ())), preferred_element_type=F32)


def split(x):
    high = x.astype(BF16)
    return high, (x - high.astype(F32)).astype(BF16)


def stacked(x, axis):
    return jnp.concatenate(split(x), axis=axis)


def halves(x):
    n = x.shape[0] // 2
    return x[:n] + x[n:]


def quarters(x):
    n, m = x.shape[0] // 2, x.shape[1] // 2
    return x[:n, :m] + (x[n:, :m] + x[:n, m:])


def is_odd(place_ref):
    return place_ref[0] % 2 == 1


def halo(place_ref, first, second):
    first, second = first.astype(F32), second.astype(F32)
    odd = is_odd(place_ref)
    after = jnp.where(place_ref[0] >= LAST, 0.0, jnp.where(odd, second, first))
    before = jnp.where(place_ref[0] == 0, 0.0, jnp.where(odd, first, second))
    return jnp.concatenate([after, before], axis=0).astype(BF16)


def edge_picker(cols):
    lane = lax.broadcasted_iota(jnp.int32, (2 * HW, cols), 1)
    sub = lax.broadcasted_iota(jnp.int32, (2 * HW, cols), 0)
    return (lane == jnp.where(sub < HW, sub, sub + cols - 2 * HW)).astype(BF16)


def pack_kernel(
    devices, me_ref, shift_hbm, length_hbm, measured_hbm, out_hbm,
    rows_ref, measured_ref, shift_ref, length_ref, sems,
):
    views, depth, tile_rows, tile_cols = measured_ref.shape
    groups = shift_ref.shape[1]
    loads = [pltpu.make_async_copy(measured_hbm.at[v], measured_ref.at[v], sems.at[v]) for v in range(views)]
    tables = [
        pltpu.make_async_copy(shift_hbm, shift_ref, sems.at[views]),
        pltpu.make_async_copy(length_hbm, length_ref, sems.at[views + 1]),
    ]
    for copy in tables + loads:
        copy.start()
    rows_ref[:, tile_rows:] = jnp.zeros((views, rows_ref.shape[1] - tile_rows) + rows_ref.shape[2:], BF16)
    lane = lax.broadcasted_iota(jnp.int32, (tile_cols, tile_cols), 1)
    sub = lax.broadcasted_iota(jnp.int32, (tile_cols, tile_cols), 0)
    turn = (lane + sub == tile_cols - 1).astype(BF16)
    me = me_ref[0]
    for view in range(views):
        loads[view].wait()
        for r0 in range(0, tile_rows, 16):
            x = measured_ref[view, :, r0 : r0 + 16, :]
            if view % 2 == 1:
                x = dot(x.reshape(depth * 16, tile_cols), turn).reshape(depth, 16, tile_cols)
            x = jnp.transpose(x.astype(F32), (1, 0, 2))
            rows_ref[view, r0 : r0 + 16] = x.astype(BF16)
        if view == 0:
            for copy in tables:
                copy.wait()

        def group(g, start, view=view):
            peer = lax.rem(me + shift_ref[view, g], devices)
            blocks = rows_ref.at[view, pl.ds(start, CAP)]
            pltpu.make_async_copy(blocks, out_hbm.at[peer, view], sems.at[views + 2 + view]).start()
            return start + length_ref[view, g]

        lax.fori_loop(0, groups, group, 0, unroll=True)
    for view in range(views):
        sent = out_hbm.at[pl.ds(0, groups), view]
        pltpu.make_async_copy(sent, sent, sems.at[views + 2 + view]).wait()


def cols_kernel(cells_ref, out_ref):
    pick = edge_picker(cells_ref.shape[-1])
    for z in range(cells_ref.shape[0]):
        out_ref[z] = dot(pick, cells_ref[z].astype(BF16), NT).astype(BF16)


def dense_slab_kernel(place_x_ref, place_y_ref, cols_ref, even_ref, other_ref, first_ref, second_ref):
    views, depth, _, tile_rows = cols_ref.shape
    count = tile_rows // (2 * HW)
    pick = edge_picker(even_ref.shape[-1])
    odd = is_odd(place_y_ref)
    for view in range(views):
        for i in range(first_ref.shape[1]):
            if i < depth:
                edge = cols_ref[view, i].astype(F32)
            else:
                planes = range((i - depth) * count, (i - depth + 1) * count)
                lead = () if len(even_ref.shape) == 3 else (view,)
                ends = [halo(place_x_ref, even_ref[*lead, z], other_ref[*lead, z]) for z in planes]
                edge = dot(pick, jnp.concatenate(ends, axis=0), NT)
            first_ref[view, i] = jnp.where(odd, edge[:HW], edge[HW:]).astype(BF16)
            second_ref[view, i] = jnp.where(odd, edge[HW:], edge[:HW]).astype(BF16)


def half_slab_kernel(late, place_x_ref, place_y_ref, cols_ref, even_ref, other_ref, *refs):
    out_ref = refs[-1]
    views, depth, _, tile_rows = cols_ref.shape
    count = tile_rows // (2 * HW)
    pick = edge_picker(even_ref.shape[-1])
    head = is_odd(place_y_ref) != late
    for view in range(views):
        for i in range(out_ref.shape[1]):
            if i < depth:
                edge = cols_ref[view, i].astype(F32)
            else:
                planes = range((i - depth) * count, (i - depth + 1) * count)
                ends = [halo(place_x_ref, even_ref[view, z], other_ref[view, z]) for z in planes]
                edge = dot(pick, jnp.concatenate(ends, axis=0), NT)
            out_ref[view, i] = jnp.where(head, edge[:HW], edge[HW:]).astype(BF16)


def edges_kernel(
    devices, tile_rows, me_ref, place_ref, shift_ref, length_ref, arrived_ref, edge_ref, first_ref, second_ref, rows_ref
):
    views = edge_ref.shape[0]
    odd = is_odd(place_ref)
    groups = shift_ref.shape[1]
    me = me_ref[0]
    low = tile_rows - CAP * HW
    for view in range(views):
        ending = tile_rows - low
        for g in range(groups - HW, groups):
            ending = ending - length_ref[view, g]
        for side, (first, start) in enumerate(((0, 0), (groups - HW, ending))):
            for g in range(first, first + HW):
                source = lax.rem(me - shift_ref[view, g] + devices, devices)
                base = source * (views * CAP) + view * CAP
                for k in range(CAP):
                    rows_ref[view, side, start + k] = arrived_ref[base + k].astype(F32)
                start = start + length_ref[view, g]
        edge = edge_ref[view, :, 4 * HW :].astype(F32)
        head = jnp.transpose(rows_ref[view, 0, :HW], (1, 0, 2)) / edge[:, :HW]
        tail = rows_ref[view, 1, (CAP - 1) * HW : CAP * HW]
        tail = jnp.transpose(tail, (1, 0, 2)) / edge[:, HW:]
        first_ref[view] = jnp.where(odd, head, tail).astype(BF16)
        second_ref[view] = jnp.where(odd, tail, head).astype(BF16)


def unpack_kernel(
    devices, me_ref, band_ref, shift_ref, length_ref, arrived_ref, blurred_ref, far_ref, parts_ref,
    out_ref, cols_ref, rows_ref, forward_ref,
):
    views, depth, tile_rows, tile_cols = out_ref.shape
    groups = shift_ref.shape[1]
    me = me_ref[0]
    pick = edge_picker(tile_cols)
    for view in range(views):

        def group(g, start, view=view):
            source = lax.rem(me - shift_ref[view, g] + devices, devices)
            base = source * (views * CAP) + view * CAP
            for k in range(CAP):
                rows_ref[view, start + k] = arrived_ref[base + k].astype(F32)
            return start + length_ref[view, g]

        lax.fori_loop(0, groups, group, 0, unroll=True)
        for z in range(depth):
            parts = parts_ref[view, z, : 4 * HW]
            parts = jnp.concatenate([parts, parts[: 2 * HW]], axis=0)
            across = dot(parts, far_ref[band_ref[z], view], ((0,), (0,)))
            forward_ref[view, z] = (blurred_ref[view, z] + across).astype(BF16)
        for r0 in range(0, tile_rows, 16):
            x = jnp.transpose(rows_ref[view, r0 : r0 + 16], (1, 0, 2))
            forward = forward_ref[view, :, r0 : r0 + 16, :].astype(F32)
            out_ref[view, :, r0 : r0 + 16, :] = (x / forward).astype(BF16)
        for z in range(depth):
            cols_ref[view, z] = dot(pick, out_ref[view, z], NT).astype(BF16)


def band(taps, size):
    wide = jnp.broadcast_to(taps, (size, LANES))
    inner = pltpu.roll(wide, LANES - HW, 1, stride=1, stride_axis=0)
    before = pltpu.roll(wide, size + HW, 1, stride=1, stride_axis=0)
    lane = lax.broadcasted_iota(jnp.int32, (size, LANES), 1)
    return jnp.where(lane < size + HW, inner, jnp.where(lane < size + 2 * HW, before, 0.0))


def far_products(place_ref, even_ref, other_ref, weights, slab_ref, along_ref):
    depth = slab_ref.shape[0] // (2 * HW)
    tile_rows = slab_ref.shape[1] // 2
    count = tile_rows // (2 * HW)
    owner = lax.broadcasted_iota(jnp.int32, (2 * HW, tile_rows), 1) // (2 * HW)
    for z in range(depth):
        at = pl.ds(z * 2 * HW, 2 * HW)
        slab_ref[at, :tile_rows] = halo(place_ref, even_ref[z], other_ref[z])
        corners = halo(place_ref, even_ref[depth + z // count], other_ref[depth + z // count])
        slab_ref[at, tile_rows:] = jnp.where(owner == z % count, corners.astype(F32), 0.0).astype(BF16)
    for turned_ref, out_ref in zip(weights, along_ref):
        for b in range(turned_ref.shape[0]):
            along = dot(slab_ref[...], turned_ref[b])
            high, low = split(along[:, :tile_rows] + along[:, tile_rows:])
            out_ref[b, 0] = high
            out_ref[b, 1] = low


def far_parts(along_ref, view, b, z):
    at = pl.ds(z * 2 * HW, 2 * HW)
    high, low = along_ref[view, b, 0, at, :], along_ref[view, b, 1, at, :]
    return [high, low, high]


def forward_kernel(
    band_ref, place_ref, taps_ref, cells_ref, even_ref, other_ref,
    blurred_ref, edge_ref, fwd_turned_ref, fwd_far_ref, later_far_ref, rows_ref, ends_ref, cols_ref, turned_ref, far_ref, fwd_rows, fwd_cols,
):
    views, depth, tile_rows, tile_cols = blurred_ref.shape
    bands = taps_ref.shape[2]
    for b in range(bands):
        ends = jnp.zeros((tile_rows, LANES - tile_rows), F32)
        for view in range(views):
            for way in range(2):
                along = band(taps_ref[way, view, b, 0:1, :], tile_rows)
                across = band(taps_ref[way, view, b, 1:2, :], tile_cols)
                beyond = along[:, tile_rows:]
                turned, far = ((fwd_turned_ref, fwd_far_ref), (turned_ref, far_ref))[way]
                turned[view, b, :tile_rows] = stacked(along[:, :tile_rows].T, 1)
                corner = stacked(beyond.T[: 2 * HW], 1)
                for at in range(tile_rows, 2 * tile_rows, 2 * HW):
                    turned[view, b, at : at + 2 * HW] = corner
                high, low = split(across[:, tile_cols:].T[: 2 * HW])
                far[b, view] = jnp.concatenate([high, high, low], axis=0)
                inner = stacked(across[:, :tile_cols].T, 1)
                if way == 0:
                    fwd_rows[view, b] = stacked(along[:, : tile_rows + 2 * HW], 0)
                    fwd_cols[view, b] = inner
                else:
                    rows_ref[b, :, view * tile_rows : (view + 1) * tile_rows] = stacked(along[:, :tile_rows], 0)
                    ends = ends + (pltpu.roll(beyond, 2 * HW * view, 1) if view else beyond)
                    cols_ref[view, b] = inner
        ends = jnp.concatenate([ends[:HW], ends[tile_rows - HW :]], axis=0)
        ends_ref[b] = stacked(ends[:, : 2 * HW * views], 0)
        later_far_ref[b] = fwd_far_ref[b]

    def plane(z, carry):
        b = band_ref[z]
        cells = stacked(cells_ref[z], 1)
        ends = halo(place_ref, even_ref[z], other_ref[z])
        for view in range(views):
            rows = fwd_rows[view, b]
            blurred = quarters(dot(rows[:, :tile_rows], cells)) + halves(dot(rows[:, tile_rows:], ends))
            blurred = quarters(dot(stacked(blurred, 0), fwd_cols[view, b]))
            blurred_ref[view, z] = blurred
            edge_ref[view, z, :HW] = blurred[:HW]
            edge_ref[view, z, HW:] = blurred[tile_rows - HW :]
        return carry

    lax.fori_loop(0, depth, plane, 0, unroll=2)


def late_kernel(
    band_ref, place_ref, turned_ref, far_ref, even_ref, other_ref, blurred_ref, out_ref, slab_ref, along_ref
):
    views, depth = blurred_ref.shape[:2]
    tile_rows = along_ref.shape[-1]
    weights = [turned_ref.at[view] for view in range(views)]
    far_products(place_ref, even_ref.at[0], other_ref.at[0], weights, slab_ref, [along_ref.at[v] for v in range(views)])
    for view in range(views):
        for z in range(depth):
            b = band_ref[z]
            parts = far_parts(along_ref, view, b, z)
            out_ref[view, z, : 4 * HW] = jnp.concatenate(parts[:2], axis=0)
            across = dot(jnp.concatenate(parts, axis=0), far_ref[b, view], ((0,), (0,)))
            ends = jnp.concatenate([across[:HW], across[tile_rows - HW :]], axis=0)
            out_ref[view, z, 4 * HW :] = (blurred_ref[view, z] + ends).astype(BF16)


def near_kernel(
    band_ref, place_ref, rows_ref, ends_ref, cols_ref, ratio_ref, even_ref, other_ref, out_ref, inner_ref, outer_ref
):
    views, depth, tile_rows, tile_cols = ratio_ref.shape

    def across(cells, weights):
        blurred = dot(cells, weights)
        return stacked(blurred[:, :tile_cols] + blurred[:, tile_cols:], 1)

    for z in range(depth):
        b = band_ref[z]
        for view in range(views):
            inner_ref[z, view * tile_rows : (view + 1) * tile_rows] = across(ratio_ref[view, z], cols_ref[view, b])
            ends = halo(place_ref, even_ref[view, z], other_ref[view, z])
            outer_ref[z, view * 2 * HW : (view + 1) * 2 * HW] = across(ends, cols_ref[view, b])
    for z in range(depth):
        b = band_ref[z]
        out_ref[z] = quarters(dot(rows_ref[b], inner_ref[z]))
        ends = quarters(dot(ends_ref[b], outer_ref[z]))
        out_ref[z, :HW] += ends[:HW]
        out_ref[z, tile_rows - HW :] += ends[HW:]


def far_kernel(
    band_ref, place_ref, turned_ref, far_ref, near_ref, even_ref, other_ref, estimate_ref, out_hbm,
    slab_ref, along_ref, out_ref, sems,
):
    views, bands = turned_ref.shape[:2]
    depth, tile_rows, tile_cols = near_ref.shape
    step = depth // sems.shape[0]
    for view in range(views):
        far_products(place_ref, even_ref.at[view], other_ref.at[view], [turned_ref.at[view]], slab_ref.at[view], [along_ref.at[view]])
    leave = []
    for z in range(depth):
        b = band_ref[z]
        parts = []
        for view in range(views):
            parts += far_parts(along_ref, view, b, z)
        across = far_ref[b].reshape(views * 6 * HW, tile_cols)
        total = near_ref[z] + dot(jnp.concatenate(parts, axis=0), across, ((0,), (0,)))
        out_ref[z] = estimate_ref[z] * (total * (1.0 / views))
        if z % step == step - 1:
            part = pl.ds(z - step + 1, step)
            leave.append(pltpu.make_async_copy(out_ref.at[part], out_hbm.at[part], sems.at[z // step]))
            leave[-1].start()
    for copy in leave:
        copy.wait()


def swap(first, second, axis, everyone=True):
    both = ("gx", "gy")
    rows, cols = (lax.axis_size(name) for name in both)
    count = lax.axis_size(axis)
    at = lambda p, q: p * cols + q
    partner = lambda i, begin: begin + ((i - begin) ^ 1)
    pairs = []
    for begin in range(2):
        found = []
        for p in range(rows):
            for q in range(cols):
                i = partner(p if axis == "gx" else q, begin)
                if 0 <= i < count:
                    found.append((at(p, q), at(i, q) if axis == "gx" else at(p, i)))
                elif everyone:
                    found.append((at(p, q), at(p, q ^ 1) if axis == "gx" else at(p ^ 1, q)))
        pairs.append(found)
    late = lax.ppermute(second, both, pairs[1])
    return lax.ppermute(first, both, pairs[0]), late


def place(count, at):
    return jnp.where(at == count - 1, at + LAST, at).reshape(1)


def body(estimate, measured, kernels, depth_band, group_shift, group_length):
    devices = lax.axis_size("gx") * lax.axis_size("gy")
    gx, gy = lax.axis_index("gx").astype(jnp.int32), lax.axis_index("gy").astype(jnp.int32)
    me = (gx * lax.axis_size("gy") + gy).reshape(1)
    place_x, place_y = (place(lax.axis_size(axis), at) for axis, at in (("gx", gx), ("gy", gy)))
    views, depth, tile_rows, tile_cols = measured.shape
    bands = kernels.shape[1]
    spare = tile_rows + 8
    like = jax.ShapeDtypeStruct
    whole = like(measured.shape, BF16)
    edge_cols = like((views, depth, 2 * HW, tile_rows), BF16)
    edge_rows = like((views, depth, HW, tile_cols), BF16)

    head, tail = estimate[:, :HW], estimate[:, tile_rows - HW :]
    even = gx % 2 == 0
    ex, ox = swap(jnp.where(even, tail, head), jnp.where(even, head, tail), "gx")
    outgoing = call(
        functools.partial(pack_kernel, devices),
        [SMEM, HBM, HBM, HBM],
        like((devices, views, CAP, depth, tile_cols), BF16),
        [
            pltpu.VMEM((views, spare, depth, tile_cols), BF16),
            pltpu.VMEM(measured.shape, BF16),
            pltpu.SMEM(group_shift.shape, jnp.int32),
            pltpu.SMEM(group_length.shape, jnp.int32),
            pltpu.SemaphoreType.DMA((2 * views + 2,)),
        ],
        HBM,
        60,
    )(me, group_shift, group_length, measured)
    outgoing = outgoing.reshape(devices * views * CAP, depth, tile_cols)
    outgoing, ex, ox, cells = lax.optimization_barrier((outgoing, ex, ox, estimate))
    arrived = lax.all_to_all(outgoing, ("gx", "gy"), split_axis=0, concat_axis=0, tiled=True)

    cols = call(cols_kernel, [VMEM], like(edge_cols.shape[1:], BF16))(cells)
    tiles = depth + depth * 2 * HW // tile_rows
    dense = lambda lead, *args: call(
        dense_slab_kernel, [SMEM] * 2 + [VMEM] * 3, (like((lead, tiles, HW, tile_rows), BF16),) * 2
    )(place_x, place_y, *args)
    ey, oy = swap(*dense(1, cols[None], ex, ox), "gy", everyone=False)

    norm = kernels / jnp.sum(kernels, axis=3, keepdims=True)
    tap_rows = jnp.stack([norm, norm[..., ::-1]])
    tap_rows = jnp.pad(tap_rows, ((0, 0),) * 4 + ((0, LANES - kernels.shape[3]),))
    turned_like = like((views, bands, 2 * tile_rows, 2 * tile_rows), BF16)
    far_like = like((bands, views, 6 * HW, tile_cols), BF16)
    blurred, edge, fwd_turned, fwd_far, later_far, rows_mat, ends_mat, cols_mat, turned_mat, far_mat = call(
        forward_kernel,
        [SMEM] * 2 + [VMEM] * 4,
        (
            like(measured.shape, F32),
            like((views, depth, 2 * HW, tile_cols), F32),
            turned_like,
            far_like,
            far_like,
            like((bands, 2 * tile_rows, views * tile_rows), BF16),
            like((bands, 4 * HW, views * 2 * HW), BF16),
            like((views, bands, tile_cols, 2 * tile_cols), BF16),
            turned_like,
            far_like,
        ),
        [
            pltpu.VMEM((views, bands, 2 * tile_rows, tile_rows + 2 * HW), BF16),
            pltpu.VMEM((views, bands, tile_cols, 2 * tile_cols), BF16),
        ],
    )(depth_band, place_x, tap_rows, cells, ex, ox)

    parts = call(
        late_kernel,
        [SMEM] * 2 + [VMEM] * 5,
        like((views, depth, 6 * HW, tile_rows), BF16),
        [
            pltpu.VMEM((depth * 2 * HW, 2 * tile_rows), BF16),
            pltpu.VMEM((views, bands, 2, depth * 2 * HW, tile_rows), BF16),
        ],
    )(depth_band, place_y, fwd_turned, fwd_far, ey, oy, edge)

    first, second = call(
        functools.partial(edges_kernel, devices, tile_rows),
        [SMEM] * 4 + [VMEM] * 2,
        (edge_rows, edge_rows),
        [pltpu.VMEM((views, 2, CAP * HW + 8, depth, tile_cols), F32)],
    )(me, place_x, group_shift, group_length, arrived, parts)
    ex, ox = swap(first, second, "gx")
    ratio, cols = call(
        functools.partial(unpack_kernel, devices),
        [SMEM] * 4 + [VMEM] * 4,
        (whole, edge_cols),
        [pltpu.VMEM((views, spare, depth, tile_cols), F32), pltpu.VMEM(measured.shape, BF16)],
    )(me, depth_band, group_shift, group_length, arrived, blurred, later_far, parts)
    slab = lambda late, *args: call(
        functools.partial(half_slab_kernel, late), [SMEM] * 2 + [VMEM] * (len(args)), like((views, tiles, HW, tile_rows), BF16)
    )(place_x, place_y, *args)
    second = slab(True, cols, ex, ox)
    ey, oy = swap(slab(False, cols, ex, ox, second), second, "gy")
    near = call(
        near_kernel,
        [SMEM] * 2 + [VMEM] * 6,
        like(estimate.shape, F32),
        [
            pltpu.VMEM((depth, views * tile_rows, 2 * tile_cols), BF16),
            pltpu.VMEM((depth, views * 2 * HW, 2 * tile_cols), BF16),
        ],
    )(depth_band, place_x, rows_mat, ends_mat, cols_mat, ratio, ex, ox)
    return call(
        far_kernel,
        [SMEM] * 2 + [VMEM] * 6,
        like(estimate.shape, F32),
        [
            pltpu.VMEM((views, depth * 2 * HW, 2 * tile_rows), BF16),
            pltpu.VMEM((views, bands, 2, depth * 2 * HW, tile_rows), BF16),
            pltpu.VMEM(estimate.shape, F32),
            pltpu.SemaphoreType.DMA((4,)),
        ],
        HBM,
    )(depth_band, place_y, turned_mat, far_mat, near, ey, oy, estimate)


def solution(mesh):
    return jax.shard_map(
        body,
        mesh=mesh,
        in_specs=(P(None, "gx", "gy"), P(None, None, "gx", "gy"), P(), P(), P(), P()),
        out_specs=P(None, "gx", "gy"),
        check_vma=False,
    )
```
